32 devices in a mesh: head: 2 (over y), blk: 16 (over z, x, core).
Axes of the slice: x: 2, y: 2, z: 4, core: 2. Of those that a mesh axis runs over, the one named last changes fastest.
Arguments:
- tokens: bfloat16 [4096, 1024], P(('blk', 'head')), may hold values from -6 to 6
- segments: int32 [4096], replicated, may hold values from 0 to 23, never falling along the last dimension, each value on 1 to 2560 neighbouring positions
- cotangent: bfloat16 [4096, 1024], P(('blk', 'head')), may hold values from -6 to 6
- w_query: bfloat16 [1024, 1024], P(('head', 'blk')), may hold values from -0.1875 to 0.1875
- w_key: bfloat16 [1024, 1024], P(('head', 'blk')), may hold values from -0.1875 to 0.1875
- w_value: bfloat16 [1024, 1024], P(('head', 'blk')), may hold values from -0.1875 to 0.1875
- b_query: bfloat16 [1024], P(('head', 'blk')), may hold values from -3 to 3
- b_value: bfloat16 [1024], P(('head', 'blk')), may hold values from -3 to 3
- w_output: bfloat16 [1024, 1024], P(('head', 'blk')), may hold values from -1.5 to 1.5
- b_output: bfloat16 [1024], P(('head', 'blk')), may hold values from -3 to 3
- gain_attn: bfloat16 [1024], P(('head', 'blk')), may hold values from 0.5 to 1.5
- shift_attn: bfloat16 [1024], P(('head', 'blk')), may hold values from -2 to 2
- w_inner: bfloat16 [1024, 4096], P(('head', 'blk')), may hold values from -0.1875 to 0.1875
- b_inner: bfloat16 [4096], P(('head', 'blk')), may hold values from -3 to 3
- w_outer: bfloat16 [4096, 1024], P(('head', 'blk')), may hold values from -0.09375 to 0.09375
- b_outer: bfloat16 [1024], P(('head', 'blk')), may hold values from -3 to 3
- gain_ffn: bfloat16 [1024], P(('head', 'blk')), may hold values from 0.5 to 1.5
- shift_ffn: bfloat16 [1024], P(('head', 'blk')), may hold values from -2 to 2
Outputs:
- out_rows: bfloat16 [4096, 1024], P(('blk', 'head'))
- grad_tokens: float32 [4096, 1024], P(('blk', 'head'))
- grad_wq: float32 [1024, 1024], P(('head', 'blk'))
- grad_wk: float32 [1024, 1024], P(('head', 'blk'))
- grad_wv: float32 [1024, 1024], P(('head', 'blk'))
- grad_bq: float32 [1024], P(('head', 'blk'))
- grad_bv: float32 [1024], P(('head', 'blk'))
- grad_wo: float32 [1024, 1024], P(('head', 'blk'))
- grad_bo: float32 [1024], P(('head', 'blk'))
- grad_g1: float32 [1024], P(('head', 'blk'))
- grad_n1: float32 [1024], P(('head', 'blk'))
- grad_w1: float32 [1024, 4096], P(('head', 'blk'))
- grad_b1: float32 [4096], P(('head', 'blk'))
- grad_w2: float32 [4096, 1024], P(('head', 'blk'))
- grad_b2: float32 [1024], P(('head', 'blk'))
- grad_g2: float32 [1024], P(('head', 'blk'))
- grad_n2: float32 [1024], P(('head', 'blk'))
The draws below stay inside these ranges and needn't reach their ends.
Inputs may be any that keep to these rules, and one draw needn't show every extreme that they name: `segments`: segment numbers never fall along the stream; each document holds 1 to 2560 tokens, and one holds exactly 2560.
All inputs are finite; a program needn't handle non-finite values.
Results may differ from the reference program's by a relative error of at most 0.019.
Values may be sent and summed in bfloat16 or wider, within the bound.
No kernel may reach another device: no remote copies, remote signals or barrier semaphores. Data moves between devices by JAX's collectives and lax.ppermute only.
A program may use at most 192 MiB of HBM per device.

```python
import math
import jax
import jax.numpy as jnp
import numpy as np
from jax import lax

D = 1024
H = 16
HD = 64
FF = 4096
DOCS = 24
SEQ = 4096
MOST = 2560


def levels(key, extent, pieces, low, high):
    loudness = 1.0
    for axis_at, blocks in pieces:
        steps = jax.random.uniform(jax.random.fold_in(jax.random.fold_in(key, 6), axis_at), (blocks,), jnp.float32, low / len(pieces), high / len(pieces))
        loudness = loudness * jnp.repeat(jnp.exp(steps), extent[axis_at] // blocks).reshape((-1,) + (1,) * (len(extent) - 1 - axis_at))
    return loudness


def length_profile(number_of, total, limit, slope):
    weights = [(1 << 20) // math.isqrt(standing ** slope) + 1 for standing in range(2, number_of + 1)]
    spare, holding = total - limit - (number_of - 1), [1] * (number_of - 1)
    while spare > 0:
        free = [i for i in range(number_of - 1) if holding[i] < limit]
        whole, budget = sum([weights[i] for i in free]), spare
        for i in free:
            extra = min(limit - holding[i], max(1, budget * weights[i] // whole), spare)
            holding[i] = holding[i] + extra
            spare = spare - extra
    return np.array([limit] + holding)


def ragged(key, number_of, total, limit, skew):
    if number_of == 2:
        one = jax.random.randint(key, (), max(1, total - limit), min(limit, total - 1) + 1)
        return jnp.stack([one, total - one])
    lengths = jnp.asarray(length_profile(number_of, total, limit, skew), jnp.int32)
    twos = (number_of - 1) // 2
    giver, receiver = lengths[1:1 + 2 * twos:2], lengths[2:2 + 2 * twos:2]
    room = jnp.minimum(giver - 1, limit - receiver)
    moved = jax.random.randint(jax.random.fold_in(key, 1), (twos,), 0, 1 << 20) % (room + 1)
    lengths = lengths.at[1:1 + 2 * twos:2].set(giver - moved).at[2:2 + 2 * twos:2].set(receiver + moved)
    return lengths[jax.random.permutation(jax.random.fold_in(key, 2), number_of)]


def bell_draw(key, shape, width, bound, pieces=(), kind=jnp.bfloat16):
    entries = jax.random.normal(key, shape, jnp.float32) * width
    if len(pieces) > 0:
        entries = levels(key, shape, pieces, -0.22, 0.18) * entries
    return jnp.clip(entries, min=-bound, max=bound).astype(kind)


def setup_inputs(seed: int = 0) -> dict:
    keys = jax.random.split(jax.random.key(seed), 19)
    tokens = bell_draw(keys[0], (SEQ, D), 1.0, 6.0, ((0, 32),))
    segments = jnp.searchsorted(jnp.cumsum(ragged(keys[1], DOCS, SEQ, MOST, 2)), jnp.arange(SEQ), side="right").astype(jnp.int32)
    cotangent = bell_draw(keys[2], (SEQ, D), 1.0, 6.0, ((0, 32),))
    w_query = bell_draw(keys[3], (D, D), D ** -0.5, 0.1875, ((0, 32),))
    w_key = bell_draw(keys[4], (D, D), D ** -0.5, 0.1875, ((0, 32),))
    w_value = bell_draw(keys[5], (D, D), D ** -0.5, 0.1875, ((0, 32),))
    b_query = bell_draw(keys[6], (D,), 0.5, 3.0, ((0, 32),))
    b_value = bell_draw(keys[7], (D,), 0.5, 3.0, ((0, 32),))
    w_output = bell_draw(keys[8], (D, D), (D // 64) ** -0.5, 1.5, ((0, 32),))
    b_output = bell_draw(keys[9], (D,), 0.5, 3.0, ((0, 32),))
    gain_attn = jnp.clip(1.0 + 0.1 * jax.random.normal(keys[10], (D,), jnp.float32), 0.5, 1.5).astype(jnp.bfloat16)
    shift_attn = bell_draw(keys[11], (D,), 0.3, 2.0, ((0, 32),))
    w_inner = bell_draw(keys[12], (D, FF), D ** -0.5, 0.1875, ((0, 32),))
    b_inner = bell_draw(keys[13], (FF,), 0.5, 3.0, ((0, 32),))
    w_outer = bell_draw(keys[14], (FF, D), FF ** -0.5, 0.09375, ((0, 32),))
    b_outer = bell_draw(keys[15], (D,), 0.5, 3.0, ((0, 32),))
    gain_ffn = jnp.clip(1.0 + 0.1 * jax.random.normal(keys[16], (D,), jnp.float32), 0.5, 1.5).astype(jnp.bfloat16)
    shift_ffn = bell_draw(keys[17], (D,), 0.3, 2.0, ((0, 32),))
    return dict(tokens=tokens, segments=segments, cotangent=cotangent, w_query=w_query, w_key=w_key, w_value=w_value, b_query=b_query, b_value=b_value, w_output=w_output, b_output=b_output, gain_attn=gain_attn, shift_attn=shift_attn, w_inner=w_inner, b_inner=b_inner, w_outer=w_outer, b_outer=b_outer, gain_ffn=gain_ffn, shift_ffn=shift_ffn)


EPS = 1e-05
NEG = -1e+30

@jax.custom_vjp
def low(v):
    return lax.optimization_barrier(v.astype(jnp.bfloat16)).astype(jnp.float32)

@jax.custom_vjp
def low_back(v):
    return v

def low_keep(v):
    return (low(v), None)

def low_pass(kept, grad):
    return (grad,)

def back_keep(v):
    return (v, None)

def back_low(kept, grad):
    return (low(grad),)
low.defvjp(low_keep, low_pass)
low_back.defvjp(back_keep, back_low)

def matmul(former, latter):
    return jnp.dot(former, latter, precision=lax.Precision.HIGHEST, preferred_element_type=jnp.float32)

def layer_norm(hidden, gain_row, shift_row):
    centre = hidden - lax.optimization_barrier(jnp.mean(hidden, axis=-1, keepdims=True))
    spread = lax.optimization_barrier(jnp.mean(centre * centre, axis=-1, keepdims=True))
    return centre * lax.rsqrt(spread + EPS) * gain_row + shift_row

def attend(queries, key_rows, value_rows, segments):
    total = queries.shape[0]
    block_rows = math.gcd(total, 512)
    score_scale = HD ** (-0.5)
    query_blocks = queries.reshape(total // block_rows, block_rows, H, HD)
    seg_blocks = segments.reshape(total // block_rows, block_rows)
    key_heads = key_rows.reshape(total, H, HD)
    value_heads = value_rows.reshape(total, H, HD)

    def one_block(block_args):
        query_part, seg_part = block_args
        raw = jnp.einsum('qhd,khd->hqk', query_part, key_heads, precision=lax.Precision.HIGHEST) * score_scale
        raw = low_back(raw)
        same = seg_part[:, None] == segments[None, :]
        scores = jnp.where(same[None], raw, NEG)
        running_max = lax.optimization_barrier(jnp.max(scores, axis=-1, keepdims=True))
        expo = jnp.exp(scores - running_max)
        weight_sum = lax.optimization_barrier(jnp.sum(expo, axis=-1))
        mixed = jnp.einsum('hqk,khd->qhd', low(expo), value_heads, precision=lax.Precision.HIGHEST)
        return mixed / jnp.transpose(weight_sum)[:, :, None]
    result = lax.map(jax.checkpoint(one_block), (query_blocks, seg_blocks))
    return result.reshape(total, H * HD)

def reference(tokens, segments, cotangent, w_query, w_key, w_value, b_query, b_value, w_output, b_output, gain_attn, shift_attn, w_inner, b_inner, w_outer, b_outer, gain_ffn, shift_ffn):
    weight_list = tuple((weight_arg.astype(jnp.float32) for weight_arg in (w_query, w_key, w_value, b_query, b_value, w_output, b_output, gain_attn, shift_attn, w_inner, b_inner, w_outer, b_outer, gain_ffn, shift_ffn)))

    def forward(inputs, mat_query, mat_key, mat_value, vec_query, vec_value, mat_output, vec_output, gain_one, shift_one, mat_inner, vec_inner, mat_outer, vec_outer, gain_two, shift_two):
        queries = low_back(low(matmul(inputs, mat_query) + vec_query))
        key_rows = low_back(low(matmul(inputs, mat_key)))
        value_rows = low_back(low(matmul(inputs, mat_value) + vec_value))
        context = low_back(low(attend(queries, key_rows, value_rows, segments)))
        attn_out = low_back(matmul(context, mat_output) + vec_output)
        norm_one = layer_norm(inputs + attn_out, gain_one, shift_one)
        pre_act = low_back(matmul(low(norm_one), mat_inner) + vec_inner)
        activation = low(jax.nn.gelu(pre_act, approximate=False))
        outer_out = low_back(matmul(activation, mat_outer) + vec_outer)
        return layer_norm(norm_one + outer_out, gain_two, shift_two)
    result, pull_back = jax.vjp(forward, tokens.astype(jnp.float32), *weight_list)
    grads = pull_back(cotangent.astype(jnp.float32))
    return (result.astype(jnp.bfloat16), grads[0], grads[1], grads[2], grads[3], grads[4], grads[5], grads[6], grads[7], grads[8], grads[9], grads[10], grads[11], grads[12], grads[13], grads[14], grads[15])
```

```python
import functools

import jax
import jax.numpy as jnp
from jax import lax
from jax.experimental import pallas as pl
from jax.experimental.pallas import tpu as pltpu
from jax.sharding import Mesh, PartitionSpec as P

H = 16
HD = 64
DOCS = 24
EPS = 1e-05
NEG = -1e30
LANE = 128
TQ = 256
KB = 512

HEAD = ("hg", "hh")
BLK = ("zz", "xg", "xx", "cc")
ALL = HEAD + BLK
TP = ("hh", "xx", "cc")
DG = ("hg", "zz", "xg")
ZG = ("zz", "xg")
BF = jnp.bfloat16
F32 = jnp.float32


def shift(value, axes, count, steps):
    if steps % count == 0:
        return value
    return lax.ppermute(value, axes, [(i, (i + steps) % count) for i in range(count)])


def swap(value, axis):
    return lax.ppermute(value, axis, [(0, 1), (1, 0)])


def across(value):
    return lax.ppermute(value, ("hh", "xx"), [(i, 3 - i) for i in range(4)])


def pick(value, index, axis):
    return lax.dynamic_index_in_dim(value, index, axis, keepdims=False)


def plane_gather(rows):
    own = jnp.concatenate([rows, swap(rows, "xx"), swap(rows, "hh"), across(rows)])
    return jnp.concatenate([own, swap(own, "cc")])


def plane_scatter(partial):
    part = partial.reshape(2, 4, partial.shape[0] // 8, partial.shape[1])
    mine = part[0] + swap(part[1].astype(BF), "cc").astype(F32)
    low = mine[1:].astype(BF)
    return (
        mine[0]
        + swap(low[0], "xx").astype(F32)
        + swap(low[1], "hh").astype(F32)
        + across(low[2]).astype(F32)
    )


def left_product(former, latter):
    return lax.dot_general(
        former, latter, (((0,), (0,)), ((), ())), preferred_element_type=F32
    )


def right_product(former, latter):
    return lax.dot_general(
        former, latter, (((1,), (1,)), ((), ())), preferred_element_type=F32
    )


def product(former, latter):
    return jnp.dot(former, latter, preferred_element_type=F32)


def norm_parts(hidden):
    centre = hidden - jnp.mean(hidden, axis=-1, keepdims=True)
    rstd = lax.rsqrt(jnp.mean(centre * centre, axis=-1, keepdims=True) + EPS)
    return centre * rstd, rstd


def norm_back(unit, rstd, gain, grad):
    inner = grad * gain
    return rstd * (
        inner
        - jnp.mean(inner, axis=-1, keepdims=True)
        - unit * jnp.mean(inner * unit, axis=-1, keepdims=True)
    )


def same_doc(low_ref, high_ref, first, keys):
    place = first + lax.broadcasted_iota(jnp.int32, (keys, TQ), 0)
    return jnp.logical_and(place >= low_ref[...], place < high_ref[...])


def nt(former, latter):
    return lax.dot_general(
        former, latter, (((1,), (1,)), ((), ())), preferred_element_type=F32
    )


def attend_kernel(
    blocks, keys_total, tab, q0, q1, kv_rel, low, high, ctx, out, lse, kv, kvt, acc
):
    tile = pl.program_id(0)
    tiles = pl.num_programs(0)
    nb = keys_total // LANE

    @pl.when(tile == 0)
    def _():
        def place(j, carry):
            block = kv_rel[tab[blocks + j]]
            kv[pl.ds(pl.multiple_of(j * LANE, LANE), LANE), :] = block
            kvt[:, pl.ds(pl.multiple_of(j * LANE, LANE), LANE)] = (
                block.astype(F32).T.astype(BF)
            )
            return carry

        lax.fori_loop(0, nb, place, 0)

    query = jnp.concatenate([q0[...], q1[...]], axis=0)
    query_t = query.astype(F32).T.astype(BF)
    acc[...] = jnp.zeros_like(acc)

    def step(j, carry):
        top, total = carry
        first = pl.multiple_of(j * KB, KB)
        scores = product(kv[pl.ds(first, KB), :], query_t)
        scores = jnp.where(same_doc(low, high, first, KB), scores, NEG)
        new_top = jnp.maximum(top, jnp.max(scores, axis=0, keepdims=True))
        factor = jnp.exp(top - new_top)
        expo = jnp.exp(scores - new_top)
        total = total * factor + jnp.sum(expo, axis=0, keepdims=True)
        acc[...] = acc[...] * factor + product(kvt[:, pl.ds(first, KB)], expo.astype(BF))
        return new_top, total

    start = tab[blocks + nb + tile]
    stop = tab[blocks + nb + tiles + tile]
    top, total = lax.fori_loop(
        start,
        stop,
        step,
        (jnp.full((1, TQ), NEG, F32), jnp.zeros((1, TQ), F32)),
    )
    mixed = acc[HD:, :] / total
    lse[...] = top + jnp.log(total)
    for half in range(2):
        part = mixed[:, half * LANE : (half + 1) * LANE]
        out[half] = part
        ctx[half] = part.astype(BF)


def attend_back_kernel(
    blocks,
    heads,
    keys_total,
    tab,
    q0,
    q1,
    kv,
    kvt,
    low,
    high,
    lse,
    out,
    grad,
    grad_q,
    mine,
    others,
    acc,
    acc_kv,
):
    tile = pl.program_id(0)
    tiles = pl.num_programs(0)
    nb = keys_total // LANE

    @pl.when(tile == 0)
    def _():
        def clear(j, carry):
            acc_kv[pl.ds(pl.multiple_of(j * KB, KB), KB), :] = jnp.zeros((KB, LANE), F32)
            return carry

        lax.fori_loop(0, keys_total // KB, clear, 0)

    query = jnp.concatenate([q0[...], q1[...]], axis=0)
    query_t = query.astype(F32).T.astype(BF)
    grad_t = jnp.concatenate([grad[0], grad[1]], axis=1).astype(F32)
    out_t = jnp.concatenate([out[0], out[1]], axis=1)
    delta = jnp.sum(grad_t * out_t, axis=0, keepdims=True)
    grad_pad = jnp.concatenate([jnp.zeros((HD, TQ), F32), grad_t], axis=0)
    grad_row = grad_pad.T.astype(BF)
    grad_pad = grad_pad.astype(BF)
    log_sum = lse[...]
    acc[...] = jnp.zeros_like(acc)

    def step(j, carry):
        first = pl.multiple_of(j * KB, KB)
        keys = kv[pl.ds(first, KB), :]
        scores = product(keys, query_t)
        scores = jnp.where(same_doc(low, high, first, KB), scores, NEG)
        prob = jnp.exp(scores - log_sum)
        grad_prob = product(keys, grad_pad)
        grad_score = (prob * (grad_prob - delta)).astype(BF)
        acc_kv[pl.ds(first, KB), :] += product(grad_score, query) + product(
            prob.astype(BF), grad_row
        )
        acc[...] += product(kvt[:, pl.ds(first, KB)], grad_score)
        return carry

    start = tab[blocks + nb + tile]
    stop = tab[blocks + nb + tiles + tile]
    lax.fori_loop(start, stop, step, 0)
    result = (acc[:HD, :] * (HD**-0.5)).astype(BF)
    grad_q[0] = result[:, :LANE]
    grad_q[1] = result[:, LANE:]

    @pl.when(tile == tiles - 1)
    def _():
        head = tab[blocks + nb + 2 * tiles]

        def write(b, carry):
            for k in range(heads):
                at = b * heads + lax.rem(head + k, heads)
                block = acc_kv[pl.ds(pl.multiple_of(at * LANE, LANE), LANE), :].T
                if k == 0:
                    mine[b] = block
                else:
                    others[k - 1, b] = block.astype(BF)
            return carry

        lax.fori_loop(0, blocks, write, 0)


def whole_spec(shape):
    return pl.BlockSpec(shape, lambda t, tab: (0,) * len(shape))


def tile_specs():
    return (
        pl.BlockSpec((None, LANE, LANE), lambda t, tab: (tab[2 * t], 0, 0)),
        pl.BlockSpec((None, LANE, LANE), lambda t, tab: (tab[2 * t + 1], 0, 0)),
        pl.BlockSpec((None, 1, TQ), lambda t, tab: (t, 0, 0)),
        pl.BlockSpec((2, HD, LANE), lambda t, tab: (t, 0, 0)),
    )


def attend(tab, query, kv_rel, low, high):
    blocks, nb = query.shape[0], kv_rel.shape[0]
    tiles, total = blocks // 2, nb * LANE
    first, second, row, pair = tile_specs()
    return pl.pallas_call(
        functools.partial(attend_kernel, blocks, total),
        out_shape=(
            jax.ShapeDtypeStruct((blocks, HD, LANE), BF),
            jax.ShapeDtypeStruct((blocks, HD, LANE), F32),
            jax.ShapeDtypeStruct((tiles, 1, TQ), F32),
            jax.ShapeDtypeStruct((total, LANE), BF),
            jax.ShapeDtypeStruct((LANE, total), BF),
        ),
        grid_spec=pltpu.PrefetchScalarGridSpec(
            num_scalar_prefetch=1,
            grid=(tiles,),
            in_specs=[first, second, whole_spec((nb, LANE, LANE)), row, row],
            out_specs=[
                pair,
                pair,
                row,
                whole_spec((total, LANE)),
                whole_spec((LANE, total)),
            ],
            scratch_shapes=[pltpu.VMEM((LANE, TQ), F32)],
        ),
        compiler_params=pltpu.CompilerParams(vmem_limit_bytes=56 << 20),
        cost_estimate=pl.CostEstimate(
            flops=12 * 10**9, bytes_accessed=6 * 10**6, transcendentals=4 * 10**6
        ),
    )(tab, query, query, kv_rel, low, high)


def attend_back(tab, heads, query, kv, kvt, low, high, lse, out, grad):
    blocks, total = query.shape[0], kv.shape[0]
    tiles = blocks // 2
    first, second, row, pair = tile_specs()
    return pl.pallas_call(
        functools.partial(attend_back_kernel, blocks, heads, total),
        out_shape=(
            jax.ShapeDtypeStruct((blocks, HD, LANE), BF),
            jax.ShapeDtypeStruct((blocks, LANE, LANE), F32),
            jax.ShapeDtypeStruct((heads - 1, blocks, LANE, LANE), BF),
        ),
        grid_spec=pltpu.PrefetchScalarGridSpec(
            num_scalar_prefetch=1,
            grid=(tiles,),
            in_specs=[
                first,
                second,
                whole_spec((total, LANE)),
                whole_spec((LANE, total)),
                row,
                row,
                row,
                pair,
                pair,
            ],
            out_specs=[
                pair,
                whole_spec((blocks, LANE, LANE)),
                whole_spec((heads - 1, blocks, LANE, LANE)),
            ],
            scratch_shapes=[
                pltpu.VMEM((LANE, TQ), F32),
                pltpu.VMEM((total, LANE), F32),
            ],
        ),
        compiler_params=pltpu.CompilerParams(vmem_limit_bytes=60 << 20),
        cost_estimate=pl.CostEstimate(
            flops=30 * 10**9, bytes_accessed=10 * 10**6, transcendentals=4 * 10**6
        ),
    )(tab, query, query, kv, kvt, low, high, lse, out, grad)


def padded(rows):
    extra = -rows.shape[-1] % LANE
    rows = jnp.pad(rows, ((0, 0), (0, extra)))
    return rows.reshape(rows.shape[0], rows.shape[1] // LANE, LANE)


def make_body(size):
    n_head = size["hg"] * size["hh"]
    gz = size["zz"] * size["xg"]
    n_blk = gz * 4
    n_all = n_head * n_blk
    n_dg = size["hg"] * gz
    hg = size["hg"]
    repl = n_blk // H
    part = HD // repl

    def body(
        tokens,
        segments,
        cotangent,
        w_query,
        w_key,
        w_value,
        b_query,
        b_value,
        w_output,
        b_output,
        gain_attn,
        shift_attn,
        w_inner,
        b_inner,
        w_outer,
        b_outer,
        gain_ffn,
        shift_ffn,
    ):
        rows, width = tokens.shape
        rw = w_query.shape[0]
        ffl = w_outer.shape[0]
        hi, zi = lax.axis_index(HEAD), lax.axis_index(ZG)
        xi, ci, yi = lax.axis_index("xx"), lax.axis_index("cc"), lax.axis_index("hh")
        gi = lax.axis_index(DG)
        bi = lax.axis_index(BLK)
        head, sub = bi // repl, bi % repl

        small = jnp.concatenate(
            [
                b_query,
                b_value,
                b_output,
                gain_attn,
                shift_attn,
                b_outer,
                gain_ffn,
                shift_ffn,
                b_inner,
            ]
        )
        n_small = small.shape[0]
        cols = jnp.stack([w.reshape(rw, H, HD) for w in (w_query, w_key, w_value)], axis=2)
        cols = jnp.transpose(cols, (1, 0, 2, 3)).reshape(H, rw * 3 * HD)
        cols = jnp.broadcast_to(cols[None, :, None], (n_head, H, repl, rw * 3 * HD))
        cols = cols.reshape(n_all, rw * 3 * HD // LANE, LANE)
        smalls = jnp.broadcast_to(padded(small[None]), (n_all,) + padded(small[None]).shape[1:])
        got = lax.all_to_all(
            jnp.concatenate([cols, smalls], axis=1), ALL, 0, 0, tiled=True
        )
        w_head = got[:, : cols.shape[1]].reshape(n_all * rw, 3 * HD)
        vecs = got[:, cols.shape[1] :].reshape(n_all, -1)[:, :n_small]
        named = [
            vecs[:, i * rw : (i + 1) * rw].reshape(width).astype(F32) for i in range(8)
        ]
        full_bq, full_bv, full_bo, full_g1, full_n1, full_b2, full_g2, full_n2 = named
        full_b1 = vecs[:, 8 * rw :].reshape(hg, 2, gz, 2, 2, ffl).astype(F32)
        b1_at = pick(pick(pick(full_b1, ci, 4), xi, 3), yi, 1).reshape(n_dg, ffl)
        b1_mine = jnp.concatenate([pick(b1_at, (gi - m) % n_dg, 0) for m in range(n_dg)])

        near = jnp.concatenate([shift(tokens, ZG, gz, k) for k in range(gz)])
        near = jnp.concatenate([near, swap(near, "xx")])
        stream = jnp.concatenate([near, swap(near, "cc")])

        full_wo = lax.all_gather(w_output, ALL, axis=0, tiled=True)
        full_wqkv = lax.all_gather(
            jnp.concatenate([w_query, w_key, w_value], axis=1), ALL, axis=0, tiled=True
        )

        w1_cut = w_inner.reshape(rw, hg, 2, gz, 2, 2, ffl)
        w1_cut = jnp.stack(
            [
                pick(pick(w1_cut, ((gi - m) % n_dg) // gz, 1), (gi - m) % gz, 2)
                for m in range(n_dg)
            ]
        )
        w1_cut = jnp.transpose(w1_cut, (2, 3, 4, 0, 1, 5)).reshape(8, n_dg, rw, ffl)
        w1_got = lax.all_to_all(w1_cut, TP, 0, 0, tiled=True)
        w1_all = jnp.stack(
            [jnp.roll(shift(w1_got, DG, n_dg, k), k, axis=1) for k in range(n_dg)]
        )
        w1_all = jnp.stack([pick(w1_all, (gi - g) % n_dg, 0) for g in range(n_dg)])
        w1_mine = jnp.transpose(
            w1_all.reshape(hg, gz, 2, 4, n_dg, rw, ffl), (0, 2, 1, 3, 5, 4, 6)
        ).reshape(width, n_dg * ffl)
        w2_mine = jnp.concatenate([shift(w_outer, DG, n_dg, k) for k in range(n_dg)])

        spot = jnp.arange(n_blk)
        slot = (
            ((spot % 2) ^ ci) * (2 * gz)
            + (((spot // 2) % 2) ^ xi) * gz
            + (zi - spot // 4) % gz
        )
        key_at = jnp.arange(n_blk * n_head)
        key_slot = (
            (hi - key_at % n_head) % n_head
        ) * n_blk + jnp.repeat(slot, n_head)
        ids = jnp.arange(DOCS)[:, None]
        below = jnp.sum((segments[None] < ids).astype(jnp.int32), axis=1)
        upto = jnp.sum((segments[None] <= ids).astype(jnp.int32), axis=1)
        own_segs = pick(segments.reshape(n_blk, n_head, LANE), hi, 1).reshape(
            n_blk // 2, 1, TQ
        )
        member = own_segs[None] == ids[:, :, None, None]
        low = jnp.sum(jnp.where(member, below[:, None, None, None], 0), axis=0)
        high = jnp.sum(jnp.where(member, upto[:, None, None, None], 0), axis=0)
        tab = jnp.concatenate(
            [
                slot,
                key_slot,
                low[:, 0, 0] // KB,
                (high[:, 0, -1] + KB - 1) // KB,
                hi[None],
            ]
        ).astype(jnp.int32)

        bias = jnp.concatenate(
            [
                pick(full_bq.reshape(H, HD), head, 0),
                jnp.zeros((HD,), F32),
                pick(full_bv.reshape(H, HD), head, 0),
            ]
        )
        qkv = (product(stream, w_head) + bias).astype(BF)
        query = jnp.pad(qkv[:, :HD] * (HD**-0.5), ((0, 0), (0, LANE - HD)))
        query = query.reshape(n_blk, LANE, LANE)
        kv_own = qkv[:, HD:].reshape(n_blk, LANE, LANE)
        kv_rel = jnp.concatenate([shift(kv_own, HEAD, n_head, k) for k in range(n_head)])
        ctx, out, lse, kv, kvt = attend(tab, query, kv_rel, low, high)

        if repl > 1:
            ctx = lax.dynamic_slice_in_dim(ctx, sub * part, part, axis=1)
        ctx_t = lax.all_to_all(ctx, BLK, 0, 0, tiled=True).reshape(width, rows)

        inputs = tokens.astype(F32)
        unit_one, rstd_one = norm_parts(inputs + left_product(ctx_t, full_wo) + full_bo)
        norm_one = unit_one * full_g1 + full_n1

        inner_in = plane_gather(norm_one.astype(BF))
        pre = product(inner_in, w1_mine) + b1_mine
        phi = 0.5 * (1.0 + lax.erf(pre * (0.5**0.5)))
        act = (pre * phi).astype(BF)
        slope = phi + pre * (jnp.exp(-0.5 * pre * pre) * ((2 * jnp.pi) ** -0.5))
        unit_two, rstd_two = norm_parts(
            norm_one + plane_scatter(product(act, w2_mine)) + full_b2
        )
        out_rows = (unit_two * full_g2 + full_n2).astype(BF)

        up = cotangent.astype(F32)
        grad_n2 = jnp.sum(up, axis=0)
        grad_g2 = jnp.sum(up * unit_two, axis=0)
        grad_two = norm_back(unit_two, rstd_two, full_g2, up)
        dz = grad_two.astype(BF)
        grad_b2 = jnp.sum(dz.astype(F32), axis=0)
        dz_all = plane_gather(dz)
        grad_pre = (slope * right_product(dz_all, w2_mine)).astype(BF)
        grad_b1 = jnp.sum(grad_pre.astype(F32), axis=0).reshape(n_dg, ffl)
        grad_norm = grad_two + plane_scatter(right_product(grad_pre, w1_mine))
        grad_w2_part = left_product(act, dz_all).reshape(n_dg, ffl, width)
        grad_w1_part = left_product(inner_in, grad_pre)

        grad_n1 = jnp.sum(grad_norm, axis=0)
        grad_g1 = jnp.sum(grad_norm * unit_one, axis=0)
        grad_one = norm_back(unit_one, rstd_one, full_g1, grad_norm)
        da = grad_one.astype(BF)
        grad_bo = jnp.sum(da.astype(F32), axis=0)
        grad_ctx = right_product(full_wo, da).astype(BF).reshape(H, 1, HD, rows)
        grad_ctx = jnp.broadcast_to(grad_ctx, (H, repl, HD, rows)).reshape(n_blk, HD, rows)
        grad_heads = lax.all_to_all(grad_ctx, BLK, 0, 0, tiled=True)

        grad_w2 = grad_w2_part[0]
        for m in range(1, n_dg):
            grad_w2 = grad_w2 + shift(grad_w2_part[m].astype(BF), DG, n_dg, -m).astype(F32)
        w1_rows = grad_w1_part.astype(BF).reshape(hg, 2, gz, 4 * rw, n_dg * ffl)
        grad_w1 = 0.0
        for k in range(n_dg):
            to = (gi + k) % n_dg
            sent = shift(pick(pick(w1_rows, to // gz, 0), to % gz, 1), DG, n_dg, k)
            sent = jnp.roll(sent.reshape(8 * rw, n_dg, ffl), k, axis=1)
            grad_w1 = grad_w1 + sent.astype(F32)
        grad_w1 = lax.all_to_all(
            grad_w1.astype(BF).reshape(8, rw, n_dg, ffl), TP, 0, 0, tiled=True
        )
        grad_w1 = jnp.stack([pick(grad_w1, (gi - g) % n_dg, 2) for g in range(n_dg)])
        grad_w1 = jnp.transpose(
            grad_w1.reshape(hg, gz, 2, 4, rw, ffl), (4, 0, 2, 1, 3, 5)
        ).reshape(rw, n_all * ffl).astype(F32)

        wo_part = product(ctx_t, da).reshape(hg, 2, gz, 2, 2, rw, width)
        for axis, name, me in ((4, "cc", ci), (3, "xx", xi), (1, "hh", yi)):
            wo_part = pick(wo_part, me, axis) + swap(
                pick(wo_part, 1 - me, axis).astype(BF), name
            ).astype(F32)
        wo_part = wo_part.reshape(n_dg, rw, width)
        grad_wo = pick(wo_part, gi, 0)
        for k in range(1, n_dg):
            grad_wo = grad_wo + shift(
                pick(wo_part, (gi + k) % n_dg, 0).astype(BF), DG, n_dg, k
            ).astype(F32)

        grad_q, grad_kv, grad_kv_others = attend_back(
            tab, n_head, query, kv, kvt, low, high, lse, out, grad_heads
        )
        for k in range(1, n_head):
            grad_kv = grad_kv + shift(grad_kv_others[k - 1], HEAD, n_head, k).astype(F32)
        grad_qkv = jnp.concatenate([grad_q, grad_kv.astype(BF)], axis=1)
        sent = grad_qkv.reshape(n_blk, 3, HD, LANE)
        if repl > 1:
            sent = lax.dynamic_slice_in_dim(sent, sub * part, part, axis=2)
        back = lax.all_to_all(sent.reshape(n_blk, 3 * part, LANE), BLK, 0, 0, tiled=True)
        back = jnp.transpose(back.reshape(H, repl, 3, part, LANE), (2, 0, 1, 3, 4))
        grad_tokens = grad_one + lax.dot_general(
            back.reshape(3 * width, rows),
            full_wqkv,
            (((0,), (1,)), ((), ())),
            preferred_element_type=F32,
        )

        order = (
            ((zi - jnp.arange(gz)) % gz)[None, None] * 4
            + (xi ^ jnp.arange(2))[None, :, None] * 2
            + (ci ^ jnp.arange(2))[:, None, None]
        ).reshape(n_blk)
        turned = jnp.stack([pick(grad_qkv, order[i], 0) for i in range(n_blk)])
        grad_cols = lax.dot_general(
            stream.reshape(n_blk, LANE, width),
            turned,
            (((0, 1), (0, 2)), ((), ())),
            preferred_element_type=F32,
        )
        own = (jnp.arange(H) == head).astype(F32)[:, None] * (sub == 0).astype(F32)
        bias_rows = jnp.sum(grad_qkv.astype(F32), axis=(0, 2))
        grad_bq = (own * bias_rows[None, :HD]).reshape(width)
        grad_bv = (own * bias_rows[None, 2 * HD :]).reshape(width)
        b1_abs = jnp.stack([pick(grad_b1, (gi - g) % n_dg, 0) for g in range(n_dg)])
        mark = (jnp.arange(8) == yi * 4 + xi * 2 + ci).astype(F32).reshape(1, 2, 1, 4, 1)
        b1_abs = (b1_abs.reshape(hg, 1, gz, 1, ffl) * mark).reshape(n_all, ffl)
        smalls = jnp.concatenate(
            [
                v.reshape(n_all, rw)
                for v in (
                    grad_bq,
                    grad_bv,
                    grad_bo,
                    grad_g1,
                    grad_n1,
                    grad_b2,
                    grad_g2,
                    grad_n2,
                )
            ]
            + [b1_abs],
            axis=1,
        )
        smalls = padded(smalls.astype(BF))
        cut = grad_cols.astype(BF).reshape(width, 3, HD)
        if repl > 1:
            cut = lax.dynamic_slice_in_dim(cut, sub * part, part, axis=2)
        cut = cut.reshape(n_all, rw * 3 * part // LANE, LANE)
        got = lax.all_to_all(jnp.concatenate([cut, smalls], axis=1), ALL, 0, 0, tiled=True)
        got = got.astype(F32)
        mats = jnp.sum(
            got[:, : cut.shape[1]].reshape(n_head, H, repl, rw, 3, part), axis=0
        )
        mats = jnp.transpose(mats, (3, 2, 0, 1, 4)).reshape(3, rw, width)
        vecs = jnp.sum(got[:, cut.shape[1] :], axis=0).reshape(-1)
        grad_bq, grad_bv, grad_bo, grad_g1, grad_n1, grad_b2, grad_g2, grad_n2 = (
            vecs[i * rw : (i + 1) * rw] for i in range(8)
        )
        grad_b1 = vecs[8 * rw : 8 * rw + ffl]
        return (
            out_rows,
            grad_tokens,
            mats[0],
            mats[1],
            mats[2],
            grad_bq,
            grad_bv,
            grad_wo,
            grad_bo,
            grad_g1,
            grad_n1,
            grad_w1,
            grad_b1,
            grad_w2,
            grad_b2,
            grad_g2,
            grad_n2,
        )

    return body


def solution(mesh):
    n_head, n_blk = mesh.shape["head"], mesh.shape["blk"]
    size = {"hg": n_head // 2, "hh": 2, "zz": 4, "xg": n_blk // 16, "xx": 2, "cc": 2}
    fine = Mesh(mesh.devices.reshape(tuple(size.values())), tuple(size))
    by_token, by_row, by_entry = P(BLK + HEAD, None), P(ALL, None), P(ALL)
    placed = (
        by_token,
        P(),
        by_token,
        by_row,
        by_row,
        by_row,
        by_entry,
        by_entry,
        by_row,
        by_entry,
        by_entry,
        by_entry,
        by_row,
        by_entry,
        by_row,
        by_entry,
        by_entry,
        by_entry,
    )
    given = (
        by_token,
        by_token,
        by_row,
        by_row,
        by_row,
        by_entry,
        by_entry,
        by_row,
        by_entry,
        by_entry,
        by_entry,
        by_row,
        by_entry,
        by_row,
        by_entry,
        by_entry,
        by_entry,
    )
    return jax.shard_map(
        make_body(size),
        mesh=fine,
        in_specs=placed,
        out_specs=given,
        check_vma=False,
    )
```

```python
import functools

import jax
import jax.numpy as jnp
from jax import lax
from jax.experimental import pallas as pl
from jax.experimental.pallas import tpu as pltpu
from jax.sharding import Mesh, PartitionSpec as P

H = 16
HD = 64
DOCS = 24
EPS = 1e-05
NEG = -1e30
LANE = 128
TQ = 256
KB = 512
KB_LOG = KB.bit_length() - 1

BF = jnp.bfloat16
F32 = jnp.float32


def swap(value, axis):
    return lax.ppermute(value, axis, [(0, 1), (1, 0)])


def pick(value, index, axis):
    return lax.dynamic_index_in_dim(
        value, index, axis, keepdims=False, allow_negative_indices=False
    )


def placed_at(pieces, places, axis):
    first = jnp.expand_dims(pieces[0], axis)
    shape = first.shape[:axis] + (len(pieces),) + first.shape[axis + 1 :]
    whole = jnp.zeros(shape, first.dtype)
    for piece, place in zip(pieces, places, strict=True):
        whole = lax.dynamic_update_slice_in_dim(
            whole, jnp.expand_dims(piece, axis), place, axis, allow_negative_indices=False
        )
    return whole


def after(value, *others):
    return lax.optimization_barrier((value,) + others)[0]


def with_other(value, axis, gate=None):
    sent = value if gate is None else after(value, gate)
    return jnp.concatenate([sent, swap(sent, axis)])


def left_product(former, latter):
    return lax.dot_general(
        former, latter, (((0,), (0,)), ((), ())), preferred_element_type=F32
    )


def right_product(former, latter):
    return lax.dot_general(
        former, latter, (((1,), (1,)), ((), ())), preferred_element_type=F32
    )


def left_wide(former, latter):
    return lax.dot_general(
        former, latter, (((0,), (1,)), ((), ())), preferred_element_type=F32
    )


def product(former, latter):
    return jnp.dot(former, latter, preferred_element_type=F32)


def norm_parts(hidden):
    centre = hidden - jnp.mean(hidden, axis=-1, keepdims=True)
    rstd = lax.rsqrt(jnp.mean(centre * centre, axis=-1, keepdims=True) + EPS)
    return centre * rstd, rstd


def norm_back(unit, rstd, gain, grad):
    inner = grad * gain
    return rstd * (
        inner
        - jnp.mean(inner, axis=-1, keepdims=True)
        - unit * jnp.mean(inner * unit, axis=-1, keepdims=True)
    )


def same_doc(low_ref, high_ref, first, keys):
    place = first + lax.broadcasted_iota(jnp.int32, (keys, TQ), 0)
    return jnp.logical_and(place >= low_ref[...], place < high_ref[...])


def attend_kernel(
    blocks, nb, tab, q0, q1, q2, q3, kv_a, kv_b, low, high, ctx, out, lse, kv, kvt, acc
):
    tile = pl.program_id(0)
    tiles = pl.num_programs(0)
    base = 2 * blocks

    @pl.when(tile == 0)
    def _():
        def place(j, carry):
            block = jnp.concatenate([kv_a[tab[base + j]], kv_b[tab[base + nb + j]]], axis=0)
            kv[pl.ds(pl.multiple_of(j * LANE, LANE), LANE), :] = block
            kvt[:, pl.ds(pl.multiple_of(j * LANE, LANE), LANE)] = (
                block.astype(F32).T.astype(BF)
            )
            return carry

        lax.fori_loop(0, nb, place, 0)

    query = jnp.concatenate([q0[...], q1[...], q2[...], q3[...]], axis=0)
    query_t = query.astype(F32).T.astype(BF)
    acc[...] = jnp.zeros_like(acc)

    def step(j, carry):
        top, total = carry
        first = pl.multiple_of(j * KB, KB)
        scores = product(kv[pl.ds(first, KB), :], query_t)
        scores = jnp.where(same_doc(low, high, first, KB), scores, NEG)
        new_top = jnp.maximum(top, jnp.max(scores, axis=0, keepdims=True))
        factor = jnp.exp(top - new_top)
        expo = jnp.exp(scores - new_top)
        total = total * factor + jnp.sum(expo, axis=0, keepdims=True)
        acc[...] = acc[...] * factor + product(kvt[:, pl.ds(first, KB)], expo.astype(BF))
        return new_top, total

    start = tab[base + 2 * nb + tile]
    stop = tab[base + 2 * nb + tiles + tile]
    top, total = lax.fori_loop(
        start,
        stop,
        step,
        (jnp.full((1, TQ), NEG, F32), jnp.zeros((1, TQ), F32)),
    )
    mixed = acc[HD:, :] / total
    lse[...] = top + jnp.log(total)
    for half in range(2):
        part = mixed[:, half * LANE : (half + 1) * LANE]
        out[half] = part
        ctx[half] = part.astype(BF)


def attend_back_kernel(
    blocks,
    heads,
    nb,
    tab,
    q0,
    q1,
    q2,
    q3,
    kv,
    kvt,
    low,
    high,
    lse,
    out,
    grad,
    grad_q,
    mine,
    others,
    acc,
    acc_kv,
):
    tile = pl.program_id(0)
    tiles = pl.num_programs(0)
    base = 2 * blocks

    @pl.when(tile == 0)
    def _():
        def clear(j, carry):
            acc_kv[pl.ds(pl.multiple_of(j * KB, KB), KB), :] = jnp.zeros((KB, LANE), F32)
            return carry

        lax.fori_loop(0, nb * LANE // KB, clear, 0)

    query = jnp.concatenate([q0[...], q1[...], q2[...], q3[...]], axis=0)
    query_t = query.astype(F32).T.astype(BF)
    grad_t = jnp.concatenate([grad[0], grad[1]], axis=1).astype(F32)
    out_t = jnp.concatenate([out[0], out[1]], axis=1)
    delta = jnp.sum(grad_t * out_t, axis=0, keepdims=True)
    grad_pad = jnp.concatenate([jnp.zeros((HD, TQ), F32), grad_t], axis=0)
    grad_row = grad_pad.T.astype(BF)
    grad_pad = grad_pad.astype(BF)
    log_sum = lse[...]
    acc[...] = jnp.zeros_like(acc)

    def step(j, carry):
        first = pl.multiple_of(j * KB, KB)
        keys = kv[pl.ds(first, KB), :]
        scores = product(keys, query_t)
        scores = jnp.where(same_doc(low, high, first, KB), scores, NEG)
        prob = jnp.exp(scores - log_sum)
        grad_prob = product(keys, grad_pad)
        grad_score = (prob * (grad_prob - delta)).astype(BF)
        acc_kv[pl.ds(first, KB), :] += product(grad_score, query) + product(
            prob.astype(BF), grad_row
        )
        acc[...] += product(kvt[:, pl.ds(first, KB)], grad_score)
        return carry

    start = tab[base + 2 * nb + tile]
    stop = tab[base + 2 * nb + tiles + tile]
    lax.fori_loop(start, stop, step, 0)
    result = (acc[:HD, :] * (HD**-0.5)).astype(BF)
    grad_q[0] = result[:, :LANE]
    grad_q[1] = result[:, LANE:]

    @pl.when(tile == tiles - 1)
    def _():
        head = tab[base + 2 * nb + 2 * tiles]

        def write(b, carry):
            for k in range(heads):
                at = b * heads + lax.bitwise_xor(head, k)
                block = acc_kv[pl.ds(pl.multiple_of(at * LANE, LANE), LANE), :].T
                if k == 0:
                    mine[b] = block
                else:
                    others[k - 1, b] = block.astype(BF)
            return carry

        lax.fori_loop(0, blocks, write, 0)


def whole_spec(shape):
    return pl.BlockSpec(shape, lambda t, tab: (0,) * len(shape))


def tile_specs(blocks):
    def half(at):
        return pl.BlockSpec((None, LANE // 2, LANE), lambda t, tab: (tab[at(t)], 0, 0))

    return (
        [
            half(lambda t: 2 * t),
            half(lambda t: blocks + 2 * t),
            half(lambda t: 2 * t + 1),
            half(lambda t: blocks + 2 * t + 1),
        ],
        pl.BlockSpec((None, 1, TQ), lambda t, tab: (t, 0, 0)),
        pl.BlockSpec((2, HD, LANE), lambda t, tab: (t, 0, 0)),
    )


def attend(tab, query, kv_rel, low, high):
    blocks, nb = query[0].shape[0], kv_rel[0].shape[0]
    tiles, total = blocks // 2, nb * LANE
    halves, row, pair = tile_specs(blocks)
    return pl.pallas_call(
        functools.partial(attend_kernel, blocks, nb),
        out_shape=(
            jax.ShapeDtypeStruct((blocks, HD, LANE), BF),
            jax.ShapeDtypeStruct((blocks, HD, LANE), F32),
            jax.ShapeDtypeStruct((tiles, 1, TQ), F32),
            jax.ShapeDtypeStruct((total, LANE), BF),
            jax.ShapeDtypeStruct((LANE, total), BF),
        ),
        grid_spec=pltpu.PrefetchScalarGridSpec(
            num_scalar_prefetch=1,
            grid=(tiles,),
            in_specs=halves + [whole_spec((nb, LANE // 2, LANE))] * 2 + [row, row],
            out_specs=[
                pair,
                pair,
                row,
                whole_spec((total, LANE)),
                whole_spec((LANE, total)),
            ],
            scratch_shapes=[pltpu.VMEM((LANE, TQ), F32)],
        ),
        compiler_params=pltpu.CompilerParams(vmem_limit_bytes=56 << 20),
        cost_estimate=pl.CostEstimate(
            flops=20 * 10**9, bytes_accessed=6 * 10**6, transcendentals=4 * 10**6
        ),
    )(tab, query[0], query[1], query[0], query[1], kv_rel[0], kv_rel[1], low, high)


def attend_back(tab, heads, query, kv, kvt, low, high, lse, out, grad):
    blocks, total = query[0].shape[0], kv.shape[0]
    halves, row, pair = tile_specs(blocks)
    return pl.pallas_call(
        functools.partial(attend_back_kernel, blocks, heads, total // LANE),
        out_shape=(
            jax.ShapeDtypeStruct((blocks, HD, LANE), BF),
            jax.ShapeDtypeStruct((blocks, LANE, LANE), F32),
            jax.ShapeDtypeStruct((heads - 1, blocks, LANE, LANE), BF),
        ),
        grid_spec=pltpu.PrefetchScalarGridSpec(
            num_scalar_prefetch=1,
            grid=(blocks // 2,),
            in_specs=halves
            + [
                whole_spec((total, LANE)),
                whole_spec((LANE, total)),
                row,
                row,
                row,
                pair,
                pair,
            ],
            out_specs=[
                pair,
                whole_spec((blocks, LANE, LANE)),
                whole_spec((heads - 1, blocks, LANE, LANE)),
            ],
            scratch_shapes=[
                pltpu.VMEM((LANE, TQ), F32),
                pltpu.VMEM((total, LANE), F32),
            ],
        ),
        compiler_params=pltpu.CompilerParams(vmem_limit_bytes=60 << 20),
        cost_estimate=pl.CostEstimate(
            flops=30 * 10**9, bytes_accessed=10 * 10**6, transcendentals=4 * 10**6
        ),
    )(
        tab,
        query[0],
        query[1],
        query[0],
        query[1],
        kv,
        kvt,
        low,
        high,
        lse,
        out,
        grad,
    )


def cols_kernel(parts, tab, *refs):
    halves, (grad, cols, acc) = refs[:8], refs[8:]
    step = pl.program_id(0)
    rows = jnp.concatenate([half[...] for half in halves], axis=0)
    wide = jnp.concatenate([grad[i] for i in range(4)], axis=1)
    term = product(wide, rows)

    @pl.when(step == 0)
    def _():
        acc[...] = term

    @pl.when(step > 0)
    def _():
        acc[...] += term

    @pl.when(step == pl.num_programs(0) - 1)
    def _():
        for p in range(parts):
            block = acc[p * HD : (p + 1) * HD, :].T
            if len(cols.shape) == 2:
                cols[:, p * HD : (p + 1) * HD] = block.astype(BF)
            else:
                halves = block.reshape(cols.shape[0], 2, 16, HD)
                cols[:, p * 16 : (p + 1) * 16, :] = jnp.concatenate(
                    [halves[:, 0], halves[:, 1]], axis=-1
                ).astype(BF)


def head_columns(tab, stream, grad, shape):
    blocks, deep, _ = grad.shape
    width = stream[0].shape[-1]

    def half(at):
        return pl.BlockSpec(
            (None, LANE // 2, width), lambda t, tab: (tab[at + 4 * t], 0, 0)
        )

    return pl.pallas_call(
        functools.partial(cols_kernel, deep // HD),
        out_shape=jax.ShapeDtypeStruct(shape, BF),
        grid_spec=pltpu.PrefetchScalarGridSpec(
            num_scalar_prefetch=1,
            grid=(blocks // 4,),
            in_specs=[half(i + blocks * j) for i in range(4) for j in range(2)]
            + [pl.BlockSpec((4, deep, LANE), lambda t, tab: (t, 0, 0))],
            out_specs=whole_spec(shape),
            scratch_shapes=[pltpu.VMEM((deep, width), F32)],
        ),
        compiler_params=pltpu.CompilerParams(vmem_limit_bytes=24 << 20),
        cost_estimate=pl.CostEstimate(
            flops=4 * 10**9, bytes_accessed=2 * stream[0].size * 2, transcendentals=0
        ),
    )(tab, *(stream * 4), grad)


def owner_kernel(got, mats, vec):
    rows = got.shape[1]
    low = lax.broadcasted_iota(jnp.int32, (16, LANE), 1) < HD
    total = jnp.zeros(vec.shape, F32)
    for n in range(got.shape[0]):
        total = total + got[n, 48:rows, :].astype(F32)
    vec[...] = total
    for p in range(3):
        for pair in range(H // 2):
            even, odd = jnp.zeros((16, LANE), F32), jnp.zeros((16, LANE), F32)
            for base in range(0, got.shape[0], H):
                even = even + got[base + 2 * pair, p * 16 : (p + 1) * 16, :].astype(F32)
                odd = odd + got[base + 2 * pair + 1, p * 16 : (p + 1) * 16, :].astype(F32)
            at = slice(pair * LANE, (pair + 1) * LANE)
            mats[p, :16, at] = jnp.where(low, even, pltpu.roll(odd, HD, 1))
            mats[p, 16:, at] = jnp.where(low, pltpu.roll(even, HD, 1), odd)


def owner_sums(got, width):
    return pl.pallas_call(
        owner_kernel,
        out_shape=(
            jax.ShapeDtypeStruct((3, 32, width), F32),
            jax.ShapeDtypeStruct((got.shape[1] - 48, LANE), F32),
        ),
        compiler_params=pltpu.CompilerParams(vmem_limit_bytes=16 << 20),
        cost_estimate=pl.CostEstimate(
            flops=got.size, bytes_accessed=got.size * 2 + width * 400, transcendentals=0
        ),
    )(got)


def padded(rows):
    extra = -rows.shape[-1] % LANE
    rows = jnp.pad(rows, ((0, 0), (0, extra)))
    return rows.reshape(rows.shape[0], rows.shape[1] // LANE, LANE)


def make_body(head_bits, blk_bits):
    n_head, n_blk = 1 << len(head_bits), 1 << len(blk_bits)
    n_all = n_head * n_blk
    every = head_bits + blk_bits
    z_bits, x_bit, c_bit = blk_bits[:-2], blk_bits[-2], blk_bits[-1]
    outer = head_bits + z_bits
    repl = n_blk // H
    part = HD // repl
    n_out = 1 << len(outer)

    def body(
        tokens,
        segments,
        cotangent,
        w_query,
        w_key,
        w_value,
        b_query,
        b_value,
        w_output,
        b_output,
        gain_attn,
        shift_attn,
        w_inner,
        b_inner,
        w_outer,
        b_outer,
        gain_ffn,
        shift_ffn,
    ):
        rows, width = tokens.shape
        rw = w_query.shape[0]
        ffl = w_outer.shape[0]
        my = {bit: lax.axis_index(bit) for bit in every}
        hi, bi = lax.axis_index(head_bits), lax.axis_index(blk_bits)
        head = bi if repl == 1 else lax.div(bi, repl)
        sub = bi - head * repl

        def summed(value, bit, axis):
            sent = pick(value, 1 - my[bit], axis).astype(BF)
            return pick(value, my[bit], axis).astype(F32) + swap(sent, bit).astype(F32)

        def traded(value, bits):
            for axis, bit in enumerate(bits):
                other = swap(pick(value, 1 - my[bit], axis), bit)
                kept = pick(value, my[bit], axis)
                value = placed_at([kept, other], [my[bit], 1 - my[bit]], axis)
            return value

        def group_gather(part_rows):
            return with_other(with_other(part_rows, x_bit), c_bit)

        def group_scatter(partial):
            part_rows = partial.reshape(2, 2, rows, width)
            mine = part_rows[0] + swap(part_rows[1].astype(BF), c_bit).astype(F32)
            return mine[0] + swap(mine[1].astype(BF), x_bit).astype(F32)

        ways = (z_bits + (x_bit,), (x_bit,) + z_bits)
        flows = [tokens[: rows // 2], tokens[rows // 2 :]]
        hops = [[flow] for flow in flows]
        for i in range(len(ways[0])):
            for flow, way in zip(hops, ways, strict=True):
                flow.append(with_other(flow[-1], way[i]))

        small = jnp.concatenate(
            [
                b_query,
                b_value,
                b_output,
                gain_attn,
                shift_attn,
                b_outer,
                gain_ffn,
                shift_ffn,
                b_inner,
            ]
        )
        n_small = small.shape[0]
        scale = HD**-0.5
        cut_q, cut_k, cut_v = (
            w.reshape(rw, H, HD) for w in (w_query * BF(scale), w_key, w_value)
        )
        cols = jnp.concatenate(
            [
                jnp.concatenate([cut_k, cut_v], axis=2),
                jnp.concatenate([cut_q, jnp.zeros_like(cut_q)], axis=2),
            ]
        )
        cols = jnp.transpose(cols, (1, 0, 2))[None, :, None]
        cols = jnp.broadcast_to(cols, (n_head, H, repl, 2 * rw, LANE))
        smalls = padded(small[None])
        smalls = jnp.broadcast_to(smalls, (n_all,) + smalls.shape[1:])
        cols_all = jnp.concatenate([cols.reshape(n_all, 2 * rw, LANE), smalls], axis=1)
        got = lax.all_to_all(cols_all, every, 0, 0, tiled=True)

        stream = [with_other(flow[-1], c_bit, got) for flow in hops]
        w_kv = got[:, :rw].reshape(width, LANE)
        w_q = got[:, rw : 2 * rw].reshape(width, LANE)
        vecs = got[:, 2 * rw :].reshape(n_all, -1)[:, :n_small]
        named = [
            vecs[:, i * rw : (i + 1) * rw].reshape(width).astype(F32) for i in range(8)
        ]
        full_bq, full_bv, full_bo, full_g1, full_n1, full_b2, full_g2, full_n2 = named
        full_b1 = vecs[:, 8 * rw :].reshape(n_out, 4, ffl).astype(F32)
        b1_mine = pick(full_b1, my[x_bit] * 2 + my[c_bit], 1).reshape(n_out * ffl)

        full_wo = lax.all_gather(w_output, every, axis=0, tiled=True)
        w1_cut = jnp.transpose(w_inner.reshape(rw, n_out, 2, 2, ffl), (2, 3, 0, 1, 4))
        w1_cut = traded(w1_cut.reshape(2, 2, rw, n_out * ffl), (x_bit, c_bit))
        w1_cut = w1_cut.reshape(4 * rw, n_out * ffl)
        w_pair = lax.all_gather(jnp.concatenate([w1_cut, w_outer]), outer)
        w1_mine = w_pair[:, : 4 * rw].reshape(width, n_out * ffl)
        w2_mine = w_pair[:, 4 * rw :].reshape(n_out * ffl, width)
        wqkv = lax.all_gather(
            after(jnp.concatenate([w_query, w_key, w_value], axis=1), w_pair),
            every,
            axis=0,
            tiled=True,
        )

        spot = jnp.arange(n_blk)

        def slots(way):
            apart = spot ^ bi
            total = 0
            for i, bit in enumerate(way + (c_bit,)):
                total = total + (((apart >> (len(blk_bits) - 1 - blk_bits.index(bit))) & 1) << i)
            return total

        slot = [slots(way) for way in ways]
        key_at = jnp.arange(n_blk * n_head)
        key_slot = [
            ((hi ^ key_at) & (n_head - 1)) * n_blk + jnp.repeat(s, n_head) for s in slot
        ]
        ids = jnp.arange(DOCS)[:, None]
        below = jnp.sum((segments[None] < ids).astype(jnp.int32), axis=1)
        upto = jnp.sum((segments[None] <= ids).astype(jnp.int32), axis=1)
        own_segs = pick(segments.reshape(n_blk, n_head, LANE), hi, 1).reshape(
            n_blk // 2, 1, TQ
        )
        member = own_segs[None] == ids[:, :, None, None]
        low = jnp.sum(jnp.where(member, below[:, None, None, None], 0), axis=0)
        high = jnp.sum(jnp.where(member, upto[:, None, None, None], 0), axis=0)
        tab = jnp.concatenate(
            slot
            + key_slot
            + [
                low[:, 0, 0] >> KB_LOG,
                (high[:, 0, -1] + (KB - 1)) >> KB_LOG,
                hi[None],
            ]
        ).astype(jnp.int32)

        bias = jnp.concatenate(
            [
                pick(full_bq.reshape(H, HD), head, 0) * scale,
                jnp.zeros((HD,), F32),
                jnp.zeros((HD,), F32),
                pick(full_bv.reshape(H, HD), head, 0),
            ]
        )
        kv_rel, query = [], []
        for flow in stream:
            kv_own = (product(flow, w_kv) + bias[LANE:]).astype(BF)
            kv_rel.append(kv_own.reshape(n_blk, rows // 2, LANE))
        kv_pair = jnp.concatenate(kv_rel, axis=1)
        for bit in head_bits[::-1]:
            kv_pair = with_other(kv_pair, bit)
        kv_rel = [kv_pair[:, : rows // 2], kv_pair[:, rows // 2 :]]
        for flow in stream:
            own_q = (product(flow, w_q) + bias[:LANE]).astype(BF)
            query.append(own_q.reshape(n_blk, rows // 2, LANE))
        ctx, out, lse, kv, kvt = attend(tab, query, kv_rel, low, high)

        if repl > 1:
            ctx = lax.dynamic_slice_in_dim(ctx, sub * part, part, axis=1)
        ctx_t = lax.all_to_all(ctx, blk_bits, 0, 0, tiled=True).reshape(width, rows)

        inputs = tokens.astype(F32)
        unit_one, rstd_one = norm_parts(inputs + left_product(ctx_t, full_wo) + full_bo)
        norm_one = unit_one * full_g1 + full_n1
        low_one = norm_one.astype(BF)

        inner_in = group_gather(low_one)
        pre = product(inner_in, w1_mine) + b1_mine
        phi = 0.5 * (1.0 + lax.erf(pre * (0.5**0.5)))
        act = (pre * phi).astype(BF)
        slope = phi + pre * (jnp.exp(-0.5 * pre * pre) * ((2 * jnp.pi) ** -0.5))
        unit_two, rstd_two = norm_parts(
            norm_one + group_scatter(product(act, w2_mine)) + full_b2
        )
        out_rows = (unit_two * full_g2 + full_n2).astype(BF)

        up = cotangent.astype(F32)
        grad_n2 = jnp.sum(up, axis=0)
        grad_g2 = jnp.sum(up * unit_two, axis=0)
        grad_two = norm_back(unit_two, rstd_two, full_g2, up)
        dz = grad_two.astype(BF)
        grad_b2 = jnp.sum(dz.astype(F32), axis=0)
        dz_all = group_gather(dz)
        grad_pre = (slope * right_product(dz_all, w2_mine)).astype(BF)
        grad_b1 = jnp.sum(grad_pre.astype(F32), axis=0).reshape(n_out, 1, ffl)
        grad_norm = grad_two + group_scatter(right_product(grad_pre, w1_mine))

        grad_w2 = left_product(act, dz_all).astype(BF).reshape(n_out, ffl, width)
        grad_w1 = left_product(inner_in, grad_pre).astype(BF).reshape(n_out, 4 * rw, width)

        grad_n1 = jnp.sum(grad_norm, axis=0)
        grad_g1 = jnp.sum(grad_norm * unit_one, axis=0)
        grad_one = norm_back(unit_one, rstd_one, full_g1, grad_norm)
        da = grad_one.astype(BF)
        grad_bo = jnp.sum(da.astype(F32), axis=0)
        grad_ctx = right_product(full_wo, da).astype(BF).reshape(H, 1, HD, rows)
        grad_ctx = jnp.broadcast_to(grad_ctx, (H, repl, HD, rows)).reshape(n_blk, HD, rows)
        grad_heads = lax.all_to_all(grad_ctx, blk_bits, 0, 0, tiled=True)

        grad_wo = product(ctx_t, da).reshape((2,) * len(every) + (rw, width))
        grad_wo = summed(grad_wo, c_bit, len(every) - 1)
        grad_wo = summed(grad_wo, x_bit, len(every) - 2).astype(BF)
        grads = jnp.concatenate(
            [grad_w1, grad_w2, grad_wo.reshape(n_out, rw, width)], axis=1
        )
        grads = lax.psum_scatter(grads, outer, scatter_dimension=0).astype(F32)

        grad_q, grad_kv, others = attend_back(
            tab, n_head, query, kv, kvt, low, high, lse, out, grad_heads
        )
        terms = [grad_kv] + [others[k] for k in range(n_head - 1)]
        for i, bit in list(enumerate(head_bits[::-1]))[::-1]:
            terms = [
                terms[k].astype(F32) + swap(terms[k + (1 << i)].astype(BF), bit).astype(F32)
                for k in range(1 << i)
            ]
        grad_kv = terms[0].astype(BF)

        grad_w1, grad_w2, grad_wo = (
            grads[: 4 * rw],
            grads[4 * rw : 4 * rw + ffl],
            grads[4 * rw + ffl :],
        )

        def to_tokens(grad, count):
            sent = grad.reshape(n_blk, count, HD, LANE)
            if repl > 1:
                sent = lax.dynamic_slice_in_dim(sent, sub * part, part, axis=2)
            came = lax.all_to_all(
                sent.reshape(n_blk, count * part, LANE), blk_bits, 0, 0, tiled=True
            )
            came = jnp.transpose(came.reshape(H, repl, count, part, LANE), (2, 0, 1, 3, 4))
            return came.reshape(count * width, rows)

        back_q = to_tokens(grad_q, 1)
        back_kv = to_tokens(after(grad_kv, back_q), 2)
        grad_tokens = grad_one + left_wide(back_q, wqkv[:, :width])
        grad_tokens = grad_tokens + left_wide(back_kv, wqkv[:, width:])

        packed = rw == 32 and repl == 1
        shape = (n_all, 48, LANE) if packed else (width, 3 * HD)
        grad_qkv = jnp.concatenate([grad_q, grad_kv], axis=1)
        halves = tuple(flow.reshape(n_blk, rows // 2, width) for flow in stream)
        cut = head_columns(tab, halves, grad_qkv, shape)
        if not packed:
            cut = cut.reshape(width, 3, HD)
            if repl > 1:
                cut = lax.dynamic_slice_in_dim(cut, sub * part, part, axis=2)
            cut = cut.reshape(n_all, rw * 3 * part // LANE, LANE)
        own = (jnp.arange(H) == head).astype(F32)[:, None]
        if repl > 1:
            own = own * (sub == 0).astype(F32)
        bias_rows = jnp.sum(grad_qkv.astype(F32), axis=(0, 2))
        grad_bq = (own * bias_rows[None, :HD]).reshape(width)
        grad_bv = (own * bias_rows[None, 2 * HD :]).reshape(width)
        mark = (jnp.arange(4) == my[x_bit] * 2 + my[c_bit]).astype(F32)[None, :, None]
        b1_abs = (grad_b1 * mark).reshape(n_all, ffl)
        smalls = jnp.concatenate(
            [
                v.reshape(n_all, rw)
                for v in (
                    grad_bq,
                    grad_bv,
                    grad_bo,
                    grad_g1,
                    grad_n1,
                    grad_b2,
                    grad_g2,
                    grad_n2,
                )
            ]
            + [b1_abs],
            axis=1,
        )
        smalls = padded(smalls.astype(BF))
        sent = after(jnp.concatenate([cut, smalls], axis=1), back_kv)
        got = lax.all_to_all(sent, every, 0, 0, tiled=True)
        if packed:
            mats, vecs = owner_sums(got, width)
            vecs = vecs.reshape(-1)
        else:
            got = got.astype(F32)
            mats = jnp.sum(
                got[:, : cut.shape[1]].reshape(n_head, H, repl, rw, 3, part), axis=0
            )
            mats = jnp.transpose(mats, (3, 2, 0, 1, 4)).reshape(3, rw, width)
            vecs = jnp.sum(got[:, cut.shape[1] :], axis=0).reshape(-1)
        grad_bq, grad_bv, grad_bo, grad_g1, grad_n1, grad_b2, grad_g2, grad_n2 = (
            vecs[i * rw : (i + 1) * rw] for i in range(8)
        )
        grad_b1 = vecs[8 * rw : 8 * rw + ffl]

        grad_w1 = traded(
            grad_w1.astype(BF).reshape(2, 2, rw, n_out * ffl), (x_bit, c_bit)
        )
        grad_w1 = (
            jnp.transpose(grad_w1.reshape(4, rw, n_out, ffl), (1, 2, 0, 3))
            .reshape(rw, n_all * ffl)
            .astype(F32)
        )
        return (
            out_rows,
            grad_tokens,
            mats[0],
            mats[1],
            mats[2],
            grad_bq,
            grad_bv,
            grad_wo,
            grad_bo,
            grad_g1,
            grad_n1,
            grad_w1,
            grad_b1,
            grad_w2,
            grad_b2,
            grad_g2,
            grad_n2,
        )

    return body


def solution(mesh):
    n_head, n_blk = mesh.shape["head"], mesh.shape["blk"]
    head_bits = tuple(f"h{i}" for i in range(n_head.bit_length() - 1))
    blk_bits = tuple(f"b{i}" for i in range(n_blk.bit_length() - 1))
    fine = Mesh(
        mesh.devices.reshape((2,) * len(head_bits + blk_bits)), head_bits + blk_bits
    )
    by_token = P(blk_bits + head_bits, None)
    by_row, by_entry = P(head_bits + blk_bits, None), P(head_bits + blk_bits)
    placed = (
        by_token,
        P(),
        by_token,
        by_row,
        by_row,
        by_row,
        by_entry,
        by_entry,
        by_row,
        by_entry,
        by_entry,
        by_entry,
        by_row,
        by_entry,
        by_row,
        by_entry,
        by_entry,
        by_entry,
    )
    given = (
        by_token,
        by_token,
        by_row,
        by_row,
        by_row,
        by_entry,
        by_entry,
        by_row,
        by_entry,
        by_entry,
        by_entry,
        by_row,
        by_entry,
        by_row,
        by_entry,
        by_entry,
        by_entry,
    )
    return jax.shard_map(
        make_body(head_bits, blk_bits),
        mesh=fine,
        in_specs=placed,
        out_specs=given,
        check_vma=False,
    )
```

```python
import functools

import jax
import jax.numpy as jnp
from jax import lax
from jax.experimental import pallas as pl
from jax.experimental.pallas import tpu as pltpu
from jax.sharding import Mesh, PartitionSpec as P

H = 16
HD = 64
DOCS = 24
EPS = 1e-05
NEG = -1e30
LANE = 128
TQ = 256
KB = 512
KB_LOG = KB.bit_length() - 1

BF = jnp.bfloat16
F32 = jnp.float32


def swap(value, axis):
    return lax.ppermute(value, axis, [(0, 1), (1, 0)])


def pick(value, index, axis):
    return lax.dynamic_index_in_dim(
        value, index, axis, keepdims=False, allow_negative_indices=False
    )


def placed_at(value, other, place, axis):
    value, other = jnp.expand_dims(value, axis), jnp.expand_dims(other, axis)
    twice = jnp.broadcast_to(
        value, value.shape[:axis] + (2,) + value.shape[axis + 1 :]
    )
    return lax.dynamic_update_slice_in_dim(
        twice, other, 1 - place, axis, allow_negative_indices=False
    )


def after(value, *others):
    return lax.optimization_barrier((value,) + others)[0]


def together(*values):
    return lax.optimization_barrier(values)


def with_other(value, axis, gate=None):
    sent = value if gate is None else after(value, gate)
    return jnp.concatenate([sent, swap(sent, axis)])


def left_product(former, latter):
    return lax.dot_general(
        former, latter, (((0,), (0,)), ((), ())), preferred_element_type=F32
    )


def right_product(former, latter):
    return lax.dot_general(
        former, latter, (((1,), (1,)), ((), ())), preferred_element_type=F32
    )


def product(former, latter):
    return jnp.dot(former, latter, preferred_element_type=F32)


def norm_parts(hidden):
    centre = hidden - jnp.mean(hidden, axis=-1, keepdims=True)
    rstd = lax.rsqrt(jnp.mean(centre * centre, axis=-1, keepdims=True) + EPS)
    return centre * rstd, rstd


def norm_back(unit, rstd, gain, grad):
    inner = grad * gain
    return rstd * (
        inner
        - jnp.mean(inner, axis=-1, keepdims=True)
        - unit * jnp.mean(inner * unit, axis=-1, keepdims=True)
    )


def same_doc(low_ref, high_ref, first, heads):
    row = lax.broadcasted_iota(jnp.int32, (KB, TQ), 0)
    place = first + row + (row >> 7) * (LANE * (heads - 1))
    return jnp.logical_and(place >= low_ref[...], place < high_ref[...])


def over_groups(tab, blocks, step, state):
    tile, tiles = pl.program_id(0), pl.num_programs(0)
    start, stop, inner, outer = (
        tab[2 * blocks + i * tiles + tile] for i in range(4)
    )
    state = lax.fori_loop(start, inner, functools.partial(step, True), state)
    state = lax.fori_loop(inner, outer, functools.partial(step, False), state)
    return lax.fori_loop(outer, stop, functools.partial(step, True), state)


def attend_kernel(blocks, heads, turns, first, last, tab, *refs):
    q0, q1, q2, q3, kv_a, kv_b, low, high = refs[:8]
    refs = refs[8:]
    if not first:
        (top_in, total_in, mixed_in), refs = refs[:3], refs[3:]
    kv, kvt = refs[:2]
    made, (acc, raw) = refs[2:5], refs[5:]
    tile, tiles = pl.program_id(0), pl.num_programs(0)
    head = tab[2 * blocks + 4 * tiles]
    start = tab[2 * blocks + tile]
    stop = tab[2 * blocks + tiles + tile]

    @pl.when(tile == 0)
    def _():
        for n in range(len(turns)):

            def place(i, carry):
                halves = []
                for j in range(4):
                    halves.append(kv_a[n * blocks + tab[4 * i + j]])
                    halves.append(kv_b[n * blocks + tab[blocks + 4 * i + j]])
                block = jnp.concatenate(halves, axis=0)
                at = (n * blocks + i * 4) * LANE
                at = pl.ds(pl.multiple_of(at, 4 * LANE), 4 * LANE)
                kv[at, :] = block
                kvt[:, at] = block.T
                return carry

            lax.fori_loop(0, blocks // 4, place, 0)

    query = jnp.concatenate([q0[...], q1[...], q2[...], q3[...]], axis=0)
    query_t = query.T
    if first:
        acc[...] = jnp.zeros_like(acc)
        state = (jnp.full((1, TQ), NEG, F32), jnp.zeros((1, TQ), F32))
    else:
        acc[...] = jnp.concatenate([jnp.zeros((HD, TQ), F32), mixed_in[...]], axis=0)
        state = (top_in[...], total_in[...])
    for n, turn in enumerate(turns):
        base = n * blocks * LANE
        parity = lax.bitwise_xor(head, turn) * LANE

        def ahead(j):
            at = pl.multiple_of(base + lax.min(j, stop - 1) * KB, KB)
            raw[lax.bitwise_and(j, 1)] = product(kv[pl.ds(at, KB), :], query_t)

        def step(masked, j, carry):
            top, total = carry
            scores = raw[lax.bitwise_and(j, 1)]
            ahead(j + 1)
            if masked:
                inside = same_doc(low, high, j * (KB * heads) + parity, heads)
                scores = jnp.where(inside, scores, NEG)
            new_top = jnp.maximum(top, jnp.max(scores, axis=0, keepdims=True))
            factor = jnp.exp(top - new_top)
            expo = jnp.exp(scores - new_top)
            total = total * factor + jnp.sum(expo, axis=0, keepdims=True)
            at = pl.ds(pl.multiple_of(base + j * KB, KB), KB)
            acc[...] = acc[...] * factor + product(kvt[:, at], expo.astype(BF))
            return new_top, total

        ahead(start)
        state = over_groups(tab, blocks, step, state)
    top, total = state
    if last:
        ctx, out, lse = made
        mixed = acc[HD:, :] / total
        lse[...] = top + jnp.log(total)
        for half in range(2):
            part = mixed[:, half * LANE : (half + 1) * LANE]
            out[half] = part
            ctx[half] = part.astype(BF)
    else:
        made[0][...], made[1][...], made[2][...] = top, total, acc[HD:, :]


def attend_back_kernel(blocks, heads, turns, first, tab, *refs):
    q0, q1, q2, q3, kv, kvt, low, high, lse, out, grad = refs[:11]
    refs = refs[11:]
    if not first:
        part_in, refs = refs[0], refs[1:]
    grad_q, grad_kv, acc, acc_kv = refs
    tile, tiles = pl.program_id(0), pl.num_programs(0)
    head = tab[2 * blocks + 4 * tiles]

    @pl.when(tile == 0)
    def _():
        def clear(j, carry):
            acc_kv[pl.ds(pl.multiple_of(j * KB, KB), KB), :] = jnp.zeros((KB, LANE), F32)
            return carry

        lax.fori_loop(0, len(turns) * blocks * LANE // KB, clear, 0)

    query = jnp.concatenate([q0[...], q1[...], q2[...], q3[...]], axis=0)
    query_t = query.T
    grad_t = jnp.concatenate([grad[0], grad[1]], axis=1).astype(F32)
    out_t = jnp.concatenate([out[0], out[1]], axis=1)
    delta = jnp.sum(grad_t * out_t, axis=0, keepdims=True)
    grad_pad = jnp.concatenate([jnp.zeros((HD, TQ), F32), grad_t], axis=0).astype(BF)
    grad_row = grad_pad.T
    log_sum = lse[...]
    acc[...] = jnp.zeros_like(acc)
    for n, turn in enumerate(turns):
        base = n * blocks * LANE
        parity = lax.bitwise_xor(head, turn) * LANE

        def step(masked, j, carry):
            at = pl.ds(pl.multiple_of(base + j * KB, KB), KB)
            keys = kv[at, :]
            scores = product(keys, query_t)
            if masked:
                inside = same_doc(low, high, j * (KB * heads) + parity, heads)
                scores = jnp.where(inside, scores, NEG)
            prob = jnp.exp(scores - log_sum)
            grad_prob = product(keys, grad_pad)
            grad_score = (prob * (grad_prob - delta)).astype(BF)
            acc_kv[at, :] += product(grad_score, query) + product(prob.astype(BF), grad_row)
            acc[...] += product(kvt[:, at], grad_score)
            return carry

        over_groups(tab, blocks, step, 0)
    if first:
        grad_q[...] = acc[:HD, :]
    else:
        result = ((acc[:HD, :] + part_in[...]) * (HD**-0.5)).astype(BF)
        grad_q[0] = result[:, :LANE]
        grad_q[1] = result[:, LANE:]

    @pl.when(tile == tiles - 1)
    def _():
        def write(b, carry):
            block = acc_kv[pl.ds(pl.multiple_of(b * LANE, LANE), LANE), :]
            grad_kv[b] = block.astype(grad_kv.dtype).T
            return carry

        lax.fori_loop(0, len(turns) * blocks, write, 0, unroll=4)


def whole_spec(shape):
    return pl.BlockSpec(shape, lambda t, tab: (0,) * len(shape))


def tile_specs(blocks):
    def half(at):
        return pl.BlockSpec((None, LANE // 2, LANE), lambda t, tab: (tab[at(t)], 0, 0))

    return (
        [
            half(lambda t: 2 * t),
            half(lambda t: blocks + 2 * t),
            half(lambda t: 2 * t + 1),
            half(lambda t: blocks + 2 * t + 1),
        ],
        pl.BlockSpec((None, 1, TQ), lambda t, tab: (t, 0, 0)),
        pl.BlockSpec((2, HD, LANE), lambda t, tab: (t, 0, 0)),
        pl.BlockSpec((None, HD, TQ), lambda t, tab: (t, 0, 0)),
    )


def attend(tab, heads, turns, query, kv_rel, low, high, state, last):
    blocks, nb = query[0].shape[0], kv_rel[0].shape[0]
    tiles, total = blocks // 2, nb * LANE
    halves, row, pair, tall = tile_specs(blocks)
    row_shape = jax.ShapeDtypeStruct((tiles, 1, TQ), F32)
    tall_shape = jax.ShapeDtypeStruct((tiles, HD, TQ), F32)
    if last:
        made = (
            jax.ShapeDtypeStruct((blocks, HD, LANE), BF),
            jax.ShapeDtypeStruct((blocks, HD, LANE), F32),
            row_shape,
        )
    return pl.pallas_call(
        functools.partial(attend_kernel, blocks, heads, turns, not state, last),
        out_shape=(
            jax.ShapeDtypeStruct((total, LANE), BF),
            jax.ShapeDtypeStruct((LANE, total), BF),
        )
        + (made if last else (row_shape, row_shape, tall_shape)),
        grid_spec=pltpu.PrefetchScalarGridSpec(
            num_scalar_prefetch=1,
            grid=(tiles,),
            in_specs=halves
            + [whole_spec((nb, LANE // 2, LANE))] * 2
            + [row, row]
            + ([row, row, tall] if state else []),
            out_specs=[whole_spec((total, LANE)), whole_spec((LANE, total))]
            + ([pair, pair, row] if last else [row, row, tall]),
            scratch_shapes=[
                pltpu.VMEM((LANE, TQ), F32),
                pltpu.VMEM((2, KB, TQ), F32),
            ],
        ),
        compiler_params=pltpu.CompilerParams(vmem_limit_bytes=56 << 20),
        cost_estimate=pl.CostEstimate(
            flops=20 * 10**9, bytes_accessed=6 * 10**6, transcendentals=4 * 10**6
        ),
    )(
        tab,
        query[0],
        query[1],
        query[0],
        query[1],
        kv_rel[0],
        kv_rel[1],
        low,
        high,
        *state,
    )


def attend_back(tab, heads, turns, query, kv, kvt, low, high, lse, out, grad, part):
    blocks, total = query[0].shape[0], kv.shape[0]
    halves, row, pair, tall = tile_specs(blocks)
    first = part is None
    if first:
        q_shape = jax.ShapeDtypeStruct((blocks // 2, HD, TQ), F32)
    else:
        q_shape = jax.ShapeDtypeStruct((blocks, HD, LANE), BF)
    return pl.pallas_call(
        functools.partial(attend_back_kernel, blocks, heads, turns, first),
        out_shape=(
            q_shape,
            jax.ShapeDtypeStruct((total // LANE, LANE, LANE), BF if first else F32),
        ),
        grid_spec=pltpu.PrefetchScalarGridSpec(
            num_scalar_prefetch=1,
            grid=(blocks // 2,),
            in_specs=halves
            + [
                whole_spec((total, LANE)),
                whole_spec((LANE, total)),
                row,
                row,
                row,
                pair,
                pair,
            ]
            + ([] if first else [tall]),
            out_specs=[
                tall if first else pair,
                whole_spec((total // LANE, LANE, LANE)),
            ],
            scratch_shapes=[
                pltpu.VMEM((LANE, TQ), F32),
                pltpu.VMEM((total, LANE), F32),
            ],
        ),
        compiler_params=pltpu.CompilerParams(vmem_limit_bytes=60 << 20),
        cost_estimate=pl.CostEstimate(
            flops=30 * 10**9, bytes_accessed=10 * 10**6, transcendentals=4 * 10**6
        ),
    )(
        tab,
        query[0],
        query[1],
        query[0],
        query[1],
        kv,
        kvt,
        low,
        high,
        lse,
        out,
        grad,
        *(() if first else (part,)),
    )


def cols_kernel(parts, tab, *refs):
    halves, (grad, cols, acc) = refs[:8], refs[8:]
    step = pl.program_id(0)
    rows = jnp.concatenate([half[...] for half in halves], axis=0)
    wide = jnp.concatenate([grad[i] for i in range(4)], axis=1)
    term = product(wide, rows)

    @pl.when(step == 0)
    def _():
        acc[...] = term

    @pl.when(step > 0)
    def _():
        acc[...] += term

    @pl.when(step == pl.num_programs(0) - 1)
    def _():
        for p in range(parts):
            block = acc[p * HD : (p + 1) * HD, :].T
            if len(cols.shape) == 2:
                cols[:, p * HD : (p + 1) * HD] = block.astype(BF)
            else:
                halves = block.reshape(cols.shape[0], 2, 16, HD)
                cols[:, p * 16 : (p + 1) * 16, :] = jnp.concatenate(
                    [halves[:, 0], halves[:, 1]], axis=-1
                ).astype(BF)


def head_columns(tab, stream, grad, shape):
    blocks, deep, _ = grad.shape
    width = stream[0].shape[-1]

    def half(at):
        return pl.BlockSpec(
            (None, LANE // 2, width), lambda t, tab: (tab[at + 4 * t], 0, 0)
        )

    return pl.pallas_call(
        functools.partial(cols_kernel, deep // HD),
        out_shape=jax.ShapeDtypeStruct(shape, BF),
        grid_spec=pltpu.PrefetchScalarGridSpec(
            num_scalar_prefetch=1,
            grid=(blocks // 4,),
            in_specs=[half(i + blocks * j) for i in range(4) for j in range(2)]
            + [pl.BlockSpec((4, deep, LANE), lambda t, tab: (t, 0, 0))],
            out_specs=whole_spec(shape),
            scratch_shapes=[pltpu.VMEM((deep, width), F32)],
        ),
        compiler_params=pltpu.CompilerParams(vmem_limit_bytes=24 << 20),
        cost_estimate=pl.CostEstimate(
            flops=4 * 10**9, bytes_accessed=2 * stream[0].size * 2, transcendentals=0
        ),
    )(tab, *(stream * 4), grad)


def owner_kernel(got, mats, vec):
    rows = got.shape[1]
    low = lax.broadcasted_iota(jnp.int32, (16, LANE), 1) < HD
    total = jnp.zeros(vec.shape, F32)
    for n in range(got.shape[0]):
        total = total + got[n, 48:rows, :].astype(F32)
    vec[...] = total
    for p in range(3):
        for pair in range(H // 2):
            even, odd = jnp.zeros((16, LANE), F32), jnp.zeros((16, LANE), F32)
            for base in range(0, got.shape[0], H):
                even = even + got[base + 2 * pair, p * 16 : (p + 1) * 16, :].astype(F32)
                odd = odd + got[base + 2 * pair + 1, p * 16 : (p + 1) * 16, :].astype(F32)
            at = slice(pair * LANE, (pair + 1) * LANE)
            mats[p, :16, at] = jnp.where(low, even, pltpu.roll(odd, HD, 1))
            mats[p, 16:, at] = jnp.where(low, pltpu.roll(even, HD, 1), odd)


def owner_sums(got, width):
    return pl.pallas_call(
        owner_kernel,
        out_shape=(
            jax.ShapeDtypeStruct((3, 32, width), F32),
            jax.ShapeDtypeStruct((got.shape[1] - 48, LANE), F32),
        ),
        compiler_params=pltpu.CompilerParams(vmem_limit_bytes=16 << 20),
        cost_estimate=pl.CostEstimate(
            flops=got.size, bytes_accessed=got.size * 2 + width * 400, transcendentals=0
        ),
    )(got)


def as_rows(vectors):
    return jnp.stack(
        [jnp.pad(v, ((0, 0), (0, LANE - v.shape[1]))) for v in vectors], axis=1
    )


def make_body(head_bits, blk_bits):
    n_head, n_blk = 1 << len(head_bits), 1 << len(blk_bits)
    n_all = n_head * n_blk
    every = head_bits + blk_bits
    z_bits, x_bit, c_bit = blk_bits[:-2], blk_bits[-2], blk_bits[-1]
    outer = head_bits + z_bits
    repl = n_blk // H
    part = HD // repl
    n_out, n_head_z = 1 << len(outer), len(outer)

    def body(
        tokens,
        segments,
        cotangent,
        w_query,
        w_key,
        w_value,
        b_query,
        b_value,
        w_output,
        b_output,
        gain_attn,
        shift_attn,
        w_inner,
        b_inner,
        w_outer,
        b_outer,
        gain_ffn,
        shift_ffn,
    ):
        rows, width = tokens.shape
        rw = w_query.shape[0]
        ffl = w_outer.shape[0]
        my = {bit: lax.axis_index(bit) for bit in every}
        hi, bi = lax.axis_index(head_bits), lax.axis_index(blk_bits)
        head = bi if repl == 1 else lax.div(bi, repl)
        sub = bi - head * repl

        def both(value, bit, axis, then=None):
            other = swap(value, bit)
            if then is not None:
                other = after(other, then)
            return placed_at(value, other, my[bit], axis)

        def summed(value, bit, axis, then=None):
            other = swap(pick(value, 1 - my[bit], axis).astype(BF), bit)
            if then is not None:
                other = after(other, then)
            return pick(value, my[bit], axis).astype(F32) + other.astype(F32)

        def traded(value, bits, thens=(None, None)):
            for axis, bit in enumerate(bits):
                other = swap(pick(value, 1 - my[bit], axis), bit)
                if thens[axis] is not None:
                    other = after(other, thens[axis])
                kept = pick(value, my[bit], axis)
                value = placed_at(kept, other, my[bit], axis)
            return value

        def over(value, bits, at, thens):
            for i, bit in enumerate(bits):
                value = both(value, bit, at + i, thens[i])
            return value

        def group_gather(part_rows):
            return with_other(with_other(part_rows, x_bit), c_bit)

        def group_scatter(partial):
            part_rows = partial.reshape(2, 2, rows, width)
            mine = part_rows[0] + swap(part_rows[1].astype(BF), c_bit).astype(F32)
            return mine[0] + swap(mine[1].astype(BF), x_bit).astype(F32)

        ways = (z_bits + (x_bit,), (x_bit,) + z_bits)
        flows = [tokens[: rows // 2], tokens[rows // 2 :]]
        hops = [[flow] for flow in flows]
        for i in range(len(ways[0])):
            for flow, way in zip(hops, ways, strict=True):
                flow.append(with_other(flow[-1], way[i]))

        small = as_rows(
            [
                v[None]
                for v in (
                    b_query,
                    b_value,
                    b_output,
                    gain_attn,
                    shift_attn,
                    b_outer,
                    gain_ffn,
                    shift_ffn,
                    b_inner,
                )
            ]
        )
        scale = HD**-0.5
        cut_q, cut_k, cut_v = (
            w.reshape(rw, H, HD) for w in (w_query * BF(scale), w_key, w_value)
        )
        cols = jnp.concatenate(
            [
                jnp.concatenate([cut_k, cut_v], axis=2),
                jnp.concatenate([cut_q, jnp.zeros_like(cut_q)], axis=2),
            ]
        )
        cols = jnp.transpose(cols, (1, 0, 2))[:, None]
        cols = jnp.broadcast_to(cols, (H, repl, 2 * rw, LANE))
        smalls = jnp.broadcast_to(small, (n_blk,) + small.shape[1:])
        cols_all = jnp.concatenate([cols.reshape(n_blk, 2 * rw, LANE), smalls], axis=1)
        got = lax.all_to_all(after(cols_all, hops[1][1]), blk_bits, 0, 0, tiled=True)
        for i, bit in enumerate(head_bits):
            got = both(got, bit, i, hops[1][-1])
        got = got.reshape((n_all,) + got.shape[len(head_bits) + 1 :])

        stream = [with_other(flow[-1], c_bit, got) for flow in hops]
        w_kv = got[:, :rw].reshape(width, LANE)
        w_q = got[:, rw : 2 * rw].reshape(width, LANE)
        vecs = got[:, 2 * rw :].astype(F32)
        named = [vecs[:, i, :rw].reshape(width) for i in range(8)]
        full_bq, full_bv, full_bo, full_g1, full_n1, full_b2, full_g2, full_n2 = named
        full_b1 = vecs[:, 8, :ffl].reshape(n_out, 4, ffl)
        b1_mine = pick(full_b1, my[x_bit] * 2 + my[c_bit], 1).reshape(n_out * ffl)

        n_z = len(z_bits)
        wo_row = over(w_output, z_bits, 0, hops[0][1 : 1 + n_z])
        wo_row = over(wo_row, head_bits, 0, [None] * (len(head_bits) - 1) + [hops[0][-1]])
        w1_cut = jnp.transpose(w_inner.reshape(rw, n_out, 2, 2, ffl), (2, 3, 0, 1, 4))
        w1_cut = traded(
            w1_cut.reshape(2, 2, rw, n_out * ffl), (x_bit, c_bit), hops[0][1:3]
        ).reshape(4 * rw, n_out * ffl)
        w_pair = after(jnp.concatenate([w1_cut, w_outer]), hops[1][2])
        w_pair = lax.all_gather(w_pair, outer)
        w1_mine = w_pair[:, : 4 * rw].reshape(width, n_out * ffl)
        w2_mine = w_pair[:, 4 * rw :].reshape(n_out * ffl, width)

        spot = jnp.arange(n_blk)

        def slots(way):
            apart = spot ^ bi
            total = 0
            for i, bit in enumerate(way + (c_bit,)):
                total = total + (((apart >> (len(blk_bits) - 1 - blk_bits.index(bit))) & 1) << i)
            return total

        slot = [slots(way) for way in ways]
        ids = jnp.arange(DOCS)[:, None]
        below = jnp.sum((segments[None] < ids).astype(jnp.int32), axis=1)
        upto = jnp.sum((segments[None] <= ids).astype(jnp.int32), axis=1)
        own_segs = pick(segments.reshape(n_blk, n_head, LANE), hi, 1).reshape(
            n_blk // 2, 1, TQ
        )
        member = own_segs[None] == ids[:, :, None, None]
        low = jnp.sum(jnp.where(member, below[:, None, None, None], 0), axis=0)
        high = jnp.sum(jnp.where(member, upto[:, None, None, None], 0), axis=0)
        far = KB_LOG + len(head_bits)
        start = low[:, 0, 0] >> far
        stop = (high[:, 0, -1] + ((1 << far) - 1)) >> far
        inner = (jnp.max(low, axis=(1, 2)) + ((1 << far) - 1)) >> far
        inner = jnp.clip(inner, start, stop)
        outer_end = jnp.clip(jnp.min(high, axis=(1, 2)) >> far, inner, stop)
        tab = jnp.concatenate(slot + [start, stop, inner, outer_end, hi[None]])
        tab = tab.astype(jnp.int32)

        bias = jnp.concatenate(
            [
                pick(full_bq.reshape(H, HD), head, 0) * scale,
                jnp.zeros((HD,), F32),
                jnp.zeros((HD,), F32),
                pick(full_bv.reshape(H, HD), head, 0),
            ]
        )
        kv_rel, query = [], []
        for flow in stream:
            kv_own = (product(flow, w_kv) + bias[LANE:]).astype(BF)
            kv_rel.append(kv_own.reshape(n_blk, rows // 2, LANE))
        kv_pair = kv_near = jnp.concatenate(kv_rel, axis=1)
        wo_row = both(wo_row, x_bit, n_head_z, kv_near)
        w_line = jnp.concatenate([w_q[:, :HD] * BF(1.0 / scale), w_kv], axis=1)
        if repl > 1:
            w_line = lax.dynamic_slice_in_dim(
                w_line.reshape(width, 3, HD), sub * part, part, axis=2
            ).reshape(width, 3 * part)
        group_other = swap(after(w_line, kv_near), x_bit)
        for bit in head_bits[::-1]:
            kv_pair = with_other(kv_pair, bit) if n_head > 2 else swap(kv_pair, bit)
        kv_far = kv_pair[n_blk:] if n_head > 2 else kv_pair
        kv_far = [kv_far[:, : rows // 2], kv_far[:, rows // 2 :]]
        for flow in stream:
            own_q = (product(flow, w_q) + bias[:LANE]).astype(BF)
            query.append(own_q.reshape(n_blk, rows // 2, LANE))
        near_turn, far_turns = (0,), tuple(range(1, n_head))
        kv, kvt, *state = attend(
            tab, n_head, near_turn, query, kv_rel, low, high, (), False
        )
        kv_two, kvt_two, ctx, out, lse = attend(
            tab, n_head, far_turns, query, kv_far, low, high, state, True
        )
        ctx = after(ctx, group_other)
        if repl > 1:
            ctx = lax.dynamic_slice_in_dim(ctx, sub * part, part, axis=1)
        ctx_t = lax.all_to_all(ctx, blk_bits, 0, 0, tiled=True).reshape(width, rows)

        full_wo = both(wo_row, c_bit, n_head_z + 1, ctx_t).reshape(width, width)

        w_line = placed_at(w_line, after(group_other, ctx), my[x_bit], 0)
        ctx_t = after(ctx_t, w_line)

        inputs = tokens.astype(F32)
        unit_one, rstd_one = norm_parts(inputs + left_product(ctx_t, full_wo) + full_bo)
        norm_one = unit_one * full_g1 + full_n1
        low_one = norm_one.astype(BF)

        inner_in = group_gather(low_one)
        pre = product(inner_in, w1_mine) + b1_mine
        phi = 0.5 * (1.0 + lax.erf(pre * (0.5**0.5)))
        act = (pre * phi).astype(BF)
        slope = phi + pre * (jnp.exp(-0.5 * pre * pre) * ((2 * jnp.pi) ** -0.5))
        unit_two, rstd_two = norm_parts(
            norm_one + group_scatter(product(act, w2_mine)) + full_b2
        )
        out_rows = (unit_two * full_g2 + full_n2).astype(BF)

        up = cotangent.astype(F32)
        grad_n2 = jnp.sum(up, axis=0)
        grad_g2 = jnp.sum(up * unit_two, axis=0)
        grad_two = norm_back(unit_two, rstd_two, full_g2, up)
        dz = grad_two.astype(BF)
        grad_b2 = jnp.sum(dz.astype(F32), axis=0)
        dz_all = group_gather(dz)
        grad_pre = (slope * right_product(dz_all, w2_mine)).astype(BF)
        grad_b1 = jnp.sum(grad_pre.astype(F32), axis=0).reshape(n_out, 1, ffl)

        grad_w2 = left_product(act, dz_all).astype(BF).reshape(n_out, ffl, width)
        grad_w1 = left_product(inner_in, grad_pre).astype(BF).reshape(n_out, 4 * rw, width)
        grads = jnp.concatenate([grad_w1, grad_w2], axis=1)
        grads = grads.reshape(n_head, n_out // n_head, 4 * rw + ffl, width)
        grads = jnp.swapaxes(grads, 0, 1)
        grad_norm = right_product(grad_pre, w1_mine)
        grad_norm = grad_two + group_scatter(grad_norm)
        grads = lax.psum_scatter(grads, z_bits, scatter_dimension=0)
        grads = grads.reshape((2,) * len(head_bits) + (4 * rw + ffl, width))

        grad_n1 = jnp.sum(grad_norm, axis=0)
        grad_g1 = jnp.sum(grad_norm * unit_one, axis=0)
        grad_one = norm_back(unit_one, rstd_one, full_g1, grad_norm)
        da = grad_one.astype(BF)
        grad_bo = jnp.sum(da.astype(F32), axis=0)
        grad_ctx = right_product(full_wo, da).astype(BF).reshape(H, 1, HD, rows)
        grad_ctx = jnp.broadcast_to(grad_ctx, (H, repl, HD, rows)).reshape(n_blk, HD, rows)
        grad_heads = lax.all_to_all(grad_ctx, blk_bits, 0, 0, tiled=True)

        by_core = ctx_t.reshape(n_all // 2, 2, rw, rows)

        def core_half(core):
            return product(pick(by_core, core, 1).reshape(width // 2, rows), da)

        wo_other = swap(core_half(1 - my[c_bit]).astype(BF), c_bit)
        grad_wo = core_half(my[c_bit]) + after(wo_other, grad_ctx).astype(F32)
        grad_wo = grad_wo.reshape((2,) * (len(every) - 1) + (rw, width))
        w_line = both(w_line, c_bit, 1, grad_ctx)
        grad_heads = after(grad_heads, grad_wo, w_line)
        w_line = w_line.reshape(4, width, 3 * part)
        wo_at = len(every) - 2
        wo_other = swap(pick(grad_wo, 1 - my[x_bit], wo_at).astype(BF), x_bit)

        part_q, others = attend_back(
            tab,
            n_head,
            far_turns,
            query,
            kv_two,
            kvt_two,
            low,
            high,
            lse,
            out,
            grad_heads,
            None,
        )
        others = others.reshape(n_head - 1, n_blk, LANE, LANE)
        part_q, wo_other = together(part_q, wo_other)
        grad_q, grad_kv = attend_back(
            tab, n_head, near_turn, query, kv, kvt, low, high, lse, out, grad_heads, part_q
        )
        terms = [grad_kv] + [others[k] for k in range(n_head - 1)]
        for i, bit in list(enumerate(head_bits[::-1]))[::-1]:
            terms = [
                terms[k].astype(F32) + swap(terms[k + (1 << i)].astype(BF), bit).astype(F32)
                for k in range(1 << i)
            ]
        grad_kv = terms[0].astype(BF)
        grad_wo = pick(grad_wo, my[x_bit], wo_at) + wo_other.astype(F32)

        def own_part(grad, count):
            grad = grad.reshape(n_blk, count, HD, LANE)
            if repl > 1:
                grad = lax.dynamic_slice_in_dim(grad, sub * part, part, axis=2)
            return grad.reshape(n_blk, count * part, LANE)

        def line_rows(grad, count):
            sent = own_part(grad, count).reshape(n_blk // 4, 4, count * part, rows)
            sent = jnp.swapaxes(sent, 0, 1)
            return lax.all_to_all(sent, (x_bit, c_bit), 0, 0, tiled=True)

        def line_product(weights, came):
            deep = 4 * weights.shape[2]
            weights = jnp.transpose(weights, (1, 0, 2)).reshape(width, deep)
            came = jnp.transpose(came, (0, 2, 1, 3)).reshape(deep, n_blk // 4 * rows)
            return product(weights, came)

        grad_qkv = jnp.concatenate([grad_q, grad_kv], axis=1)
        line_kv = line_rows(grad_qkv, 3)
        for bit in head_bits:
            grad_wo = summed(grad_wo, bit, 0, grad_kv)
        wo_half = grad_wo

        grad_in = line_product(w_line, line_kv)

        packed = rw == 32 and repl == 1
        shape = (n_all, 48, LANE) if packed else (width, 3 * HD)
        halves = tuple(flow.reshape(n_blk, rows // 2, width) for flow in stream)
        cut = head_columns(tab, halves, grad_qkv, shape)
        if not packed:
            cut = cut.reshape(width, 3, HD)
            if repl > 1:
                cut = lax.dynamic_slice_in_dim(cut, sub * part, part, axis=2)
            cut = cut.reshape(n_all, rw * 3 * part // LANE, LANE)
        own = (jnp.arange(H) == head).astype(F32)[:, None]
        if repl > 1:
            own = own * (sub == 0).astype(F32)
        bias_rows = jnp.sum(grad_qkv.astype(F32), axis=(0, 2))
        grad_bq = (own * bias_rows[None, :HD]).reshape(width)
        grad_bv = (own * bias_rows[None, 2 * HD :]).reshape(width)
        mark = (jnp.arange(4) == my[x_bit] * 2 + my[c_bit]).astype(F32)[None, :, None]
        b1_abs = (grad_b1 * mark).reshape(n_all, ffl)
        smalls = as_rows(
            [
                v.reshape(n_all, -1)
                for v in (
                    grad_bq,
                    grad_bv,
                    *after((grad_bo, grad_g1, grad_n1, grad_b2, grad_g2, grad_n2), grad_q),
                    b1_abs,
                )
            ]
        )
        cut = jnp.concatenate([cut, smalls.astype(BF)], axis=1)
        n_cut = cut.shape[1]
        cut = cut.reshape((2,) * len(head_bits) + (n_blk, n_cut, LANE))
        for bit in head_bits:
            cut = summed(cut, bit, 0, grad_in)
        sent = cut.astype(BF)
        got = lax.all_to_all(sent, blk_bits, 0, 0, tiled=True)
        grads = after(grads, grad_in)
        for bit in head_bits[1:]:
            grads = summed(grads, bit, 1)
        other = swap(pick(grads, 1 - my[head_bits[0]], 0).astype(BF), head_bits[0])
        grad_in = grad_in.reshape((width,) + (2,) * n_z + (rows,))
        for i in range(1, n_z)[::-1]:
            grad_in = summed(grad_in, z_bits[i], 1 + i)
        grad_wo = after(wo_half, grad_in)
        for bit in z_bits:
            grad_wo = summed(grad_wo, bit, 0)
        grad_in, other = together(grad_in, other)
        grads = pick(grads, my[head_bits[0]], 0).astype(F32) + other.astype(F32)
        grad_w2 = grads[4 * rw :]
        first = grads[: 4 * rw].astype(BF).reshape(2, 2, rw, n_out * ffl)
        first_other = swap(pick(first, 1 - my[x_bit], 0), x_bit)
        grad_in = summed(grad_in, z_bits[0], 1)
        grad_w1 = placed_at(pick(first, my[x_bit], 0), first_other, my[x_bit], 0)
        came = swap(pick(grad_w1, 1 - my[c_bit], 1), c_bit)
        grad_w1 = placed_at(pick(grad_w1, my[c_bit], 1), came, my[c_bit], 1)
        grad_tokens = grad_one + grad_in.T
        grad_w1 = (
            jnp.transpose(grad_w1.reshape(4, rw, n_out, ffl), (1, 2, 0, 3))
            .reshape(rw, n_all * ffl)
            .astype(F32)
        )
        if packed:
            mats, vecs = owner_sums(got, width)
        else:
            got = got.astype(F32)
            mats = got[:, : n_cut - 9].reshape(H, repl, rw, 3, part)
            mats = jnp.transpose(mats, (3, 2, 0, 1, 4)).reshape(3, rw, width)
            vecs = jnp.sum(got[:, n_cut - 9 :], axis=0)
        grad_bq, grad_bv, grad_bo, grad_g1, grad_n1, grad_b2, grad_g2, grad_n2 = (
            vecs[i, :rw] for i in range(8)
        )
        grad_b1 = vecs[8, :ffl]
        return (
            out_rows,
            grad_tokens,
            mats[0],
            mats[1],
            mats[2],
            grad_bq,
            grad_bv,
            grad_wo,
            grad_bo,
            grad_g1,
            grad_n1,
            grad_w1,
            grad_b1,
            grad_w2,
            grad_b2,
            grad_g2,
            grad_n2,
        )

    return body


def solution(mesh):
    n_head, n_blk = mesh.shape["head"], mesh.shape["blk"]
    head_bits = tuple(f"h{i}" for i in range(n_head.bit_length() - 1))
    blk_bits = tuple(f"b{i}" for i in range(n_blk.bit_length() - 1))
    fine = Mesh(
        mesh.devices.reshape((2,) * len(head_bits + blk_bits)), head_bits + blk_bits
    )
    by_token = P(blk_bits + head_bits, None)
    by_row, by_entry = P(head_bits + blk_bits, None), P(head_bits + blk_bits)
    placed = (
        by_token,
        P(),
        by_token,
        by_row,
        by_row,
        by_row,
        by_entry,
        by_entry,
        by_row,
        by_entry,
        by_entry,
        by_entry,
        by_row,
        by_entry,
        by_row,
        by_entry,
        by_entry,
        by_entry,
    )
    given = (
        by_token,
        by_token,
        by_row,
        by_row,
        by_row,
        by_entry,
        by_entry,
        by_row,
        by_entry,
        by_entry,
        by_entry,
        by_row,
        by_entry,
        by_row,
        by_entry,
        by_entry,
        by_entry,
    )
    return jax.shard_map(
        make_body(head_bits, blk_bits),
        mesh=fine,
        in_specs=placed,
        out_specs=given,
        check_vma=False,
    )
```

```python
import functools

import jax
import jax.numpy as jnp
from jax import lax
from jax.experimental import pallas as pl
from jax.experimental.pallas import tpu as pltpu
from jax.sharding import Mesh, PartitionSpec as P

H = 16
HD = 64
DOCS = 24
EPS = 1e-05
NEG = -1e30
LANE = 128
TQ = 256
KB = 512
KB_LOG = KB.bit_length() - 1

BF = jnp.bfloat16
F32 = jnp.float32


def swap(value, axis):
    return lax.ppermute(value, axis, [(0, 1), (1, 0)])


def pick(value, index, axis):
    return lax.dynamic_index_in_dim(
        value, index, axis, keepdims=False, allow_negative_indices=False
    )


def placed_at(value, other, place, axis):
    value, other = jnp.expand_dims(value, axis), jnp.expand_dims(other, axis)
    twice = jnp.broadcast_to(
        value, value.shape[:axis] + (2,) + value.shape[axis + 1 :]
    )
    return lax.dynamic_update_slice_in_dim(
        twice, other, 1 - place, axis, allow_negative_indices=False
    )


def after(value, *others):
    return lax.optimization_barrier((value,) + others)[0]


def together(*values):
    return lax.optimization_barrier(values)


def with_other(value, axis, gate=None):
    sent = value if gate is None else after(value, gate)
    return jnp.concatenate([sent, swap(sent, axis)])


def left_product(former, latter):
    return lax.dot_general(
        former, latter, (((0,), (0,)), ((), ())), preferred_element_type=F32
    )


def right_product(former, latter):
    return lax.dot_general(
        former, latter, (((1,), (1,)), ((), ())), preferred_element_type=F32
    )


def product(former, latter):
    return jnp.dot(former, latter, preferred_element_type=F32)


def norm_parts(hidden):
    centre = hidden - jnp.mean(hidden, axis=-1, keepdims=True)
    rstd = lax.rsqrt(jnp.mean(centre * centre, axis=-1, keepdims=True) + EPS)
    return centre * rstd, rstd


def norm_back(unit, rstd, gain, grad):
    inner = grad * gain
    return rstd * (
        inner
        - jnp.mean(inner, axis=-1, keepdims=True)
        - unit * jnp.mean(inner * unit, axis=-1, keepdims=True)
    )


def same_doc(low_ref, high_ref, first, heads):
    row = lax.broadcasted_iota(jnp.int32, (KB, TQ), 0)
    place = first + row + (row >> 7) * (LANE * (heads - 1))
    return jnp.logical_and(place >= low_ref[...], place < high_ref[...])


def over_groups(tab, blocks, step, state):
    tile, tiles = pl.program_id(0), pl.num_programs(0)
    start, stop, inner, outer = (
        tab[2 * blocks + i * tiles + tile] for i in range(4)
    )
    state = lax.fori_loop(start, inner, functools.partial(step, True), state)
    state = lax.fori_loop(inner, outer, functools.partial(step, False), state)
    return lax.fori_loop(outer, stop, functools.partial(step, True), state)


def attend_kernel(blocks, heads, turns, first, last, tab, *refs):
    q0, q1, q2, q3, kv_a, kv_b, low, high = refs[:8]
    refs = refs[8:]
    if not first:
        (top_in, total_in, mixed_in), refs = refs[:3], refs[3:]
    kv, kvt = refs[:2]
    made, (acc, raw) = refs[2:5], refs[5:]
    tile, tiles = pl.program_id(0), pl.num_programs(0)
    head = tab[2 * blocks + 4 * tiles]
    start = tab[2 * blocks + tile]
    stop = tab[2 * blocks + tiles + tile]

    @pl.when(tile == 0)
    def _():
        for n in range(len(turns)):

            def place(i, carry):
                halves = []
                for j in range(4):
                    halves.append(kv_a[n * blocks + tab[4 * i + j]])
                    halves.append(kv_b[n * blocks + tab[blocks + 4 * i + j]])
                block = jnp.concatenate(halves, axis=0)
                at = (n * blocks + i * 4) * LANE
                at = pl.ds(pl.multiple_of(at, 4 * LANE), 4 * LANE)
                kv[at, :] = block
                kvt[:, at] = block.T
                return carry

            lax.fori_loop(0, blocks // 4, place, 0)

    query = jnp.concatenate([q0[...], q1[...], q2[...], q3[...]], axis=0)
    query_t = query.T
    if first:
        acc[...] = jnp.zeros_like(acc)
        state = (jnp.full((1, TQ), NEG, F32), jnp.zeros((1, TQ), F32))
    else:
        acc[...] = jnp.concatenate([jnp.zeros((HD, TQ), F32), mixed_in[...]], axis=0)
        state = (top_in[...], total_in[...])
    for n, turn in enumerate(turns):
        base = n * blocks * LANE
        parity = lax.bitwise_xor(head, turn) * LANE

        def ahead(j):
            at = pl.multiple_of(base + lax.min(j, stop - 1) * KB, KB)
            raw[lax.bitwise_and(j, 1)] = product(kv[pl.ds(at, KB), :], query_t)

        def step(masked, j, carry):
            top, total = carry
            scores = raw[lax.bitwise_and(j, 1)]
            ahead(j + 1)
            if masked:
                inside = same_doc(low, high, j * (KB * heads) + parity, heads)
                scores = jnp.where(inside, scores, NEG)
            new_top = jnp.maximum(top, jnp.max(scores, axis=0, keepdims=True))
            factor = jnp.exp(top - new_top)
            expo = jnp.exp(scores - new_top)
            total = total * factor + jnp.sum(expo, axis=0, keepdims=True)
            at = pl.ds(pl.multiple_of(base + j * KB, KB), KB)
            acc[...] = acc[...] * factor + product(kvt[:, at], expo.astype(BF))
            return new_top, total

        ahead(start)
        state = over_groups(tab, blocks, step, state)
    top, total = state
    if last:
        ctx, out, lse = made
        mixed = acc[HD:, :] / total
        lse[...] = top + jnp.log(total)
        for half in range(2):
            part = mixed[:, half * LANE : (half + 1) * LANE]
            out[half] = part
            ctx[half] = part.astype(BF)
    else:
        made[0][...], made[1][...], made[2][...] = top, total, acc[HD:, :]


def attend_back_kernel(blocks, heads, turns, first, tab, *refs):
    q0, q1, q2, q3, kv, kvt, low, high, lse, out, grad = refs[:11]
    refs = refs[11:]
    if not first:
        part_in, refs = refs[0], refs[1:]
    grad_q, grad_kv, acc, acc_kv = refs
    tile, tiles = pl.program_id(0), pl.num_programs(0)
    head = tab[2 * blocks + 4 * tiles]

    @pl.when(tile == 0)
    def _():
        def clear(j, carry):
            acc_kv[pl.ds(pl.multiple_of(j * KB, KB), KB), :] = jnp.zeros((KB, LANE), F32)
            return carry

        lax.fori_loop(0, len(turns) * blocks * LANE // KB, clear, 0)

    query = jnp.concatenate([q0[...], q1[...], q2[...], q3[...]], axis=0)
    query_t = query.T
    grad_t = jnp.concatenate([grad[0], grad[1]], axis=1).astype(F32)
    out_t = jnp.concatenate([out[0], out[1]], axis=1)
    delta = jnp.sum(grad_t * out_t, axis=0, keepdims=True)
    grad_pad = jnp.concatenate([jnp.zeros((HD, TQ), F32), grad_t], axis=0).astype(BF)
    grad_row = grad_pad.T
    log_sum = lse[...]
    acc[...] = jnp.zeros_like(acc)
    for n, turn in enumerate(turns):
        base = n * blocks * LANE
        parity = lax.bitwise_xor(head, turn) * LANE

        def step(masked, j, carry):
            at = pl.ds(pl.multiple_of(base + j * KB, KB), KB)
            keys = kv[at, :]
            scores = product(keys, query_t)
            if masked:
                inside = same_doc(low, high, j * (KB * heads) + parity, heads)
                scores = jnp.where(inside, scores, NEG)
            prob = jnp.exp(scores - log_sum)
            grad_prob = product(keys, grad_pad)
            grad_score = (prob * (grad_prob - delta)).astype(BF)
            acc_kv[at, :] += product(grad_score, query) + product(prob.astype(BF), grad_row)
            acc[...] += product(kvt[:, at], grad_score)
            return carry

        over_groups(tab, blocks, step, 0)
    if first:
        grad_q[...] = acc[:HD, :]
    else:
        result = ((acc[:HD, :] + part_in[...]) * (HD**-0.5)).astype(BF)
        grad_q[0] = result[:, :LANE]
        grad_q[1] = result[:, LANE:]

    @pl.when(tile == tiles - 1)
    def _():
        def write(b, carry):
            block = acc_kv[pl.ds(pl.multiple_of(b * LANE, LANE), LANE), :]
            grad_kv[b] = block.astype(grad_kv.dtype).T
            return carry

        lax.fori_loop(0, len(turns) * blocks, write, 0, unroll=4)


def whole_spec(shape):
    return pl.BlockSpec(shape, lambda t, tab: (0,) * len(shape))


def tile_specs(blocks):
    def half(at):
        return pl.BlockSpec((None, LANE // 2, LANE), lambda t, tab: (tab[at(t)], 0, 0))

    return (
        [
            half(lambda t: 2 * t),
            half(lambda t: blocks + 2 * t),
            half(lambda t: 2 * t + 1),
            half(lambda t: blocks + 2 * t + 1),
        ],
        pl.BlockSpec((None, 1, TQ), lambda t, tab: (t, 0, 0)),
        pl.BlockSpec((2, HD, LANE), lambda t, tab: (t, 0, 0)),
        pl.BlockSpec((None, HD, TQ), lambda t, tab: (t, 0, 0)),
    )


def attend(tab, heads, turns, query, kv_rel, low, high, state, last):
    blocks, nb = query[0].shape[0], kv_rel[0].shape[0]
    tiles, total = blocks // 2, nb * LANE
    halves, row, pair, tall = tile_specs(blocks)
    row_shape = jax.ShapeDtypeStruct((tiles, 1, TQ), F32)
    tall_shape = jax.ShapeDtypeStruct((tiles, HD, TQ), F32)
    if last:
        made = (
            jax.ShapeDtypeStruct((blocks, HD, LANE), BF),
            jax.ShapeDtypeStruct((blocks, HD, LANE), F32),
            row_shape,
        )
    return pl.pallas_call(
        functools.partial(attend_kernel, blocks, heads, turns, not state, last),
        out_shape=(
            jax.ShapeDtypeStruct((total, LANE), BF),
            jax.ShapeDtypeStruct((LANE, total), BF),
        )
        + (made if last else (row_shape, row_shape, tall_shape)),
        grid_spec=pltpu.PrefetchScalarGridSpec(
            num_scalar_prefetch=1,
            grid=(tiles,),
            in_specs=halves
            + [whole_spec((nb, LANE // 2, LANE))] * 2
            + [row, row]
            + ([row, row, tall] if state else []),
            out_specs=[whole_spec((total, LANE)), whole_spec((LANE, total))]
            + ([pair, pair, row] if last else [row, row, tall]),
            scratch_shapes=[
                pltpu.VMEM((LANE, TQ), F32),
                pltpu.VMEM((2, KB, TQ), F32),
            ],
        ),
        compiler_params=pltpu.CompilerParams(vmem_limit_bytes=56 << 20),
        cost_estimate=pl.CostEstimate(
            flops=20 * 10**9, bytes_accessed=6 * 10**6, transcendentals=4 * 10**6
        ),
    )(
        tab,
        query[0],
        query[1],
        query[0],
        query[1],
        kv_rel[0],
        kv_rel[1],
        low,
        high,
        *state,
    )


def attend_back(tab, heads, turns, query, kv, kvt, low, high, lse, out, grad, part):
    blocks, total = query[0].shape[0], kv.shape[0]
    halves, row, pair, tall = tile_specs(blocks)
    first = part is None
    if first:
        q_shape = jax.ShapeDtypeStruct((blocks // 2, HD, TQ), F32)
    else:
        q_shape = jax.ShapeDtypeStruct((blocks, HD, LANE), BF)
    return pl.pallas_call(
        functools.partial(attend_back_kernel, blocks, heads, turns, first),
        out_shape=(
            q_shape,
            jax.ShapeDtypeStruct((total // LANE, LANE, LANE), BF if first else F32),
        ),
        grid_spec=pltpu.PrefetchScalarGridSpec(
            num_scalar_prefetch=1,
            grid=(blocks // 2,),
            in_specs=halves
            + [
                whole_spec((total, LANE)),
                whole_spec((LANE, total)),
                row,
                row,
                row,
                pair,
                pair,
            ]
            + ([] if first else [tall]),
            out_specs=[
                tall if first else pair,
                whole_spec((total // LANE, LANE, LANE)),
            ],
            scratch_shapes=[
                pltpu.VMEM((LANE, TQ), F32),
                pltpu.VMEM((total, LANE), F32),
            ],
        ),
        compiler_params=pltpu.CompilerParams(vmem_limit_bytes=60 << 20),
        cost_estimate=pl.CostEstimate(
            flops=30 * 10**9, bytes_accessed=10 * 10**6, transcendentals=4 * 10**6
        ),
    )(
        tab,
        query[0],
        query[1],
        query[0],
        query[1],
        kv,
        kvt,
        low,
        high,
        lse,
        out,
        grad,
        *(() if first else (part,)),
    )


def cols_kernel(parts, tab, *refs):
    halves, (grad, cols, acc) = refs[:8], refs[8:]
    step = pl.program_id(0)
    rows = jnp.concatenate([half[...] for half in halves], axis=0)
    wide = jnp.concatenate([grad[i] for i in range(4)], axis=1)
    term = product(wide, rows)

    @pl.when(step == 0)
    def _():
        acc[...] = term

    @pl.when(step > 0)
    def _():
        acc[...] += term

    @pl.when(step == pl.num_programs(0) - 1)
    def _():
        for p in range(parts):
            block = acc[p * HD : (p + 1) * HD, :].T
            if len(cols.shape) == 2:
                cols[:, p * HD : (p + 1) * HD] = block.astype(BF)
            else:
                halves = block.reshape(cols.shape[0], 2, 16, HD)
                cols[:, p * 16 : (p + 1) * 16, :] = jnp.concatenate(
                    [halves[:, 0], halves[:, 1]], axis=-1
                ).astype(BF)


def head_columns(tab, stream, grad, shape):
    blocks, deep, _ = grad.shape
    width = stream[0].shape[-1]

    def half(at):
        return pl.BlockSpec(
            (None, LANE // 2, width), lambda t, tab: (tab[at + 4 * t], 0, 0)
        )

    return pl.pallas_call(
        functools.partial(cols_kernel, deep // HD),
        out_shape=jax.ShapeDtypeStruct(shape, BF),
        grid_spec=pltpu.PrefetchScalarGridSpec(
            num_scalar_prefetch=1,
            grid=(blocks // 4,),
            in_specs=[half(i + blocks * j) for i in range(4) for j in range(2)]
            + [pl.BlockSpec((4, deep, LANE), lambda t, tab: (t, 0, 0))],
            out_specs=whole_spec(shape),
            scratch_shapes=[pltpu.VMEM((deep, width), F32)],
        ),
        compiler_params=pltpu.CompilerParams(vmem_limit_bytes=24 << 20),
        cost_estimate=pl.CostEstimate(
            flops=4 * 10**9, bytes_accessed=2 * stream[0].size * 2, transcendentals=0
        ),
    )(tab, *(stream * 4), grad)


def owner_kernel(got, mats, vec):
    rows = got.shape[1]
    low = lax.broadcasted_iota(jnp.int32, (16, LANE), 1) < HD
    total = jnp.zeros(vec.shape, F32)
    for n in range(got.shape[0]):
        total = total + got[n, 48:rows, :].astype(F32)
    vec[...] = total
    for p in range(3):
        for pair in range(H // 2):
            even, odd = jnp.zeros((16, LANE), F32), jnp.zeros((16, LANE), F32)
            for base in range(0, got.shape[0], H):
                even = even + got[base + 2 * pair, p * 16 : (p + 1) * 16, :].astype(F32)
                odd = odd + got[base + 2 * pair + 1, p * 16 : (p + 1) * 16, :].astype(F32)
            at = slice(pair * LANE, (pair + 1) * LANE)
            mats[p, :16, at] = jnp.where(low, even, pltpu.roll(odd, HD, 1))
            mats[p, 16:, at] = jnp.where(low, pltpu.roll(even, HD, 1), odd)


def owner_sums(got, width):
    return pl.pallas_call(
        owner_kernel,
        out_shape=(
            jax.ShapeDtypeStruct((3, 32, width), F32),
            jax.ShapeDtypeStruct((got.shape[1] - 48, LANE), F32),
        ),
        compiler_params=pltpu.CompilerParams(vmem_limit_bytes=16 << 20),
        cost_estimate=pl.CostEstimate(
            flops=got.size, bytes_accessed=got.size * 2 + width * 400, transcendentals=0
        ),
    )(got)


def as_rows(vectors):
    return jnp.stack(
        [jnp.pad(v, ((0, 0), (0, LANE - v.shape[1]))) for v in vectors], axis=1
    )


def make_body(head_bits, blk_bits):
    n_head, n_blk = 1 << len(head_bits), 1 << len(blk_bits)
    n_all = n_head * n_blk
    every = head_bits + blk_bits
    z_bits, x_bit, c_bit = blk_bits[:-2], blk_bits[-2], blk_bits[-1]
    outer = head_bits + z_bits
    repl = n_blk // H
    part = HD // repl
    n_out, n_head_z = 1 << len(outer), len(outer)

    def body(
        tokens,
        segments,
        cotangent,
        w_query,
        w_key,
        w_value,
        b_query,
        b_value,
        w_output,
        b_output,
        gain_attn,
        shift_attn,
        w_inner,
        b_inner,
        w_outer,
        b_outer,
        gain_ffn,
        shift_ffn,
    ):
        rows, width = tokens.shape
        rw = w_query.shape[0]
        ffl = w_outer.shape[0]
        my = {bit: lax.axis_index(bit) for bit in every}
        hi, bi = lax.axis_index(head_bits), lax.axis_index(blk_bits)
        head = bi if repl == 1 else lax.div(bi, repl)
        sub = bi - head * repl

        def both(value, bit, axis, then=None):
            other = swap(value, bit)
            if then is not None:
                other = after(other, then)
            return placed_at(value, other, my[bit], axis)

        def summed(value, bit, axis, then=None):
            other = swap(pick(value, 1 - my[bit], axis).astype(BF), bit)
            if then is not None:
                other = after(other, then)
            return pick(value, my[bit], axis).astype(F32) + other.astype(F32)

        def traded(value, bits, thens=(None, None)):
            for axis, bit in enumerate(bits):
                other = swap(pick(value, 1 - my[bit], axis), bit)
                if thens[axis] is not None:
                    other = after(other, thens[axis])
                kept = pick(value, my[bit], axis)
                value = placed_at(kept, other, my[bit], axis)
            return value

        def over(value, bits, at, thens):
            for i, bit in enumerate(bits):
                value = both(value, bit, at + i, thens[i])
            return value

        def group_gather(part_rows):
            return with_other(with_other(part_rows, x_bit), c_bit)

        def group_scatter(partial):
            part_rows = partial.reshape(2, 2, rows, width)
            mine = part_rows[0] + swap(part_rows[1].astype(BF), c_bit).astype(F32)
            return mine[0] + swap(mine[1].astype(BF), x_bit).astype(F32)

        ways = (z_bits + (x_bit,), (x_bit,) + z_bits)
        flows = [tokens[: rows // 2], tokens[rows // 2 :]]
        hops = [[flow] for flow in flows]
        for i in range(len(ways[0])):
            for flow, way in zip(hops, ways, strict=True):
                flow.append(with_other(flow[-1], way[i]))

        small = as_rows(
            [
                v[None]
                for v in (
                    b_query,
                    b_value,
                    b_output,
                    gain_attn,
                    shift_attn,
                    b_outer,
                    gain_ffn,
                    shift_ffn,
                    b_inner,
                )
            ]
        )
        scale = HD**-0.5
        cut_q, cut_k, cut_v = (
            w.reshape(rw, H, HD) for w in (w_query * BF(scale), w_key, w_value)
        )
        cols = jnp.concatenate(
            [
                jnp.concatenate([cut_k, cut_v], axis=2),
                jnp.concatenate([cut_q, jnp.zeros_like(cut_q)], axis=2),
            ]
        )
        cols = jnp.transpose(cols, (1, 0, 2))[:, None]
        cols = jnp.broadcast_to(cols, (H, repl, 2 * rw, LANE))
        smalls = jnp.broadcast_to(small, (n_blk,) + small.shape[1:])
        cols_all = jnp.concatenate([cols.reshape(n_blk, 2 * rw, LANE), smalls], axis=1)
        got = lax.all_to_all(after(cols_all, hops[1][1]), blk_bits, 0, 0, tiled=True)
        for i, bit in enumerate(head_bits):
            got = both(got, bit, i, hops[1][-1])
        got = got.reshape((n_all,) + got.shape[len(head_bits) + 1 :])

        stream = [with_other(flow[-1], c_bit, got) for flow in hops]
        w_kv = got[:, :rw].reshape(width, LANE)
        w_q = got[:, rw : 2 * rw].reshape(width, LANE)
        vecs = got[:, 2 * rw :].astype(F32)
        named = [vecs[:, i, :rw].reshape(width) for i in range(8)]
        full_bq, full_bv, full_bo, full_g1, full_n1, full_b2, full_g2, full_n2 = named
        full_b1 = vecs[:, 8, :ffl].reshape(n_out, 4, ffl)
        b1_mine = pick(full_b1, my[x_bit] * 2 + my[c_bit], 1).reshape(n_out * ffl)

        n_z = len(z_bits)
        wo_row = over(w_output, z_bits, 0, hops[0][1 : 1 + n_z])
        wo_row = over(wo_row, head_bits, 0, [None] * (len(head_bits) - 1) + [hops[0][-1]])
        w1_cut = jnp.transpose(w_inner.reshape(rw, n_out, 2, 2, ffl), (2, 3, 0, 1, 4))
        w1_cut = traded(
            w1_cut.reshape(2, 2, rw, n_out * ffl), (x_bit, c_bit), hops[0][1:3]
        ).reshape(4 * rw, n_out * ffl)
        w_pair = after(jnp.concatenate([w1_cut, w_outer]), hops[1][2])
        w_pair = lax.all_gather(w_pair, outer)
        w1_mine = w_pair[:, : 4 * rw].reshape(width, n_out * ffl)
        w2_mine = w_pair[:, 4 * rw :].reshape(n_out * ffl, width)

        spot = jnp.arange(n_blk)

        def slots(way):
            apart = spot ^ bi
            total = 0
            for i, bit in enumerate(way + (c_bit,)):
                total = total + (((apart >> (len(blk_bits) - 1 - blk_bits.index(bit))) & 1) << i)
            return total

        slot = [slots(way) for way in ways]
        ids = jnp.arange(DOCS)[:, None]
        below = jnp.sum((segments[None] < ids).astype(jnp.int32), axis=1)
        upto = jnp.sum((segments[None] <= ids).astype(jnp.int32), axis=1)
        own_segs = pick(segments.reshape(n_blk, n_head, LANE), hi, 1).reshape(
            n_blk // 2, 1, TQ
        )
        member = own_segs[None] == ids[:, :, None, None]
        low = jnp.sum(jnp.where(member, below[:, None, None, None], 0), axis=0)
        high = jnp.sum(jnp.where(member, upto[:, None, None, None], 0), axis=0)
        far = KB_LOG + len(head_bits)
        start = low[:, 0, 0] >> far
        stop = (high[:, 0, -1] + ((1 << far) - 1)) >> far
        inner = (jnp.max(low, axis=(1, 2)) + ((1 << far) - 1)) >> far
        inner = jnp.clip(inner, start, stop)
        outer_end = jnp.clip(jnp.min(high, axis=(1, 2)) >> far, inner, stop)
        tab = jnp.concatenate(slot + [start, stop, inner, outer_end, hi[None]])
        tab = tab.astype(jnp.int32)

        bias = jnp.concatenate(
            [
                pick(full_bq.reshape(H, HD), head, 0) * scale,
                jnp.zeros((HD,), F32),
                jnp.zeros((HD,), F32),
                pick(full_bv.reshape(H, HD), head, 0),
            ]
        )
        kv_rel, query = [], []
        for flow in stream:
            kv_own = (product(flow, w_kv) + bias[LANE:]).astype(BF)
            kv_rel.append(kv_own.reshape(n_blk, rows // 2, LANE))
        kv_pair = kv_near = jnp.concatenate(kv_rel, axis=1)
        wo_row = both(wo_row, x_bit, n_head_z, kv_near)
        w_line = jnp.concatenate([w_q[:, :HD] * BF(1.0 / scale), w_kv], axis=1).T
        if repl > 1:
            w_line = lax.dynamic_slice_in_dim(
                w_line.reshape(3, HD, width), sub * part, part, axis=1
            ).reshape(3 * part, width)
        group_other = swap(after(w_line, kv_near), x_bit)
        for bit in head_bits[::-1]:
            kv_pair = with_other(kv_pair, bit) if n_head > 2 else swap(kv_pair, bit)
        kv_far = kv_pair[n_blk:] if n_head > 2 else kv_pair
        kv_far = [kv_far[:, : rows // 2], kv_far[:, rows // 2 :]]
        for flow in stream:
            own_q = (product(flow, w_q) + bias[:LANE]).astype(BF)
            query.append(own_q.reshape(n_blk, rows // 2, LANE))
        near_turn, far_turns = (0,), tuple(range(1, n_head))
        kv, kvt, *state = attend(
            tab, n_head, near_turn, query, kv_rel, low, high, (), False
        )
        kv_two, kvt_two, ctx, out, lse = attend(
            tab, n_head, far_turns, query, kv_far, low, high, state, True
        )
        ctx = after(ctx, group_other)
        if repl > 1:
            ctx = lax.dynamic_slice_in_dim(ctx, sub * part, part, axis=1)
        ctx_t = lax.all_to_all(ctx, blk_bits, 0, 0, tiled=True).reshape(width, rows)

        full_wo = both(wo_row, c_bit, n_head_z + 1, ctx_t).reshape(width, width)

        w_line = placed_at(w_line, after(group_other, ctx), my[x_bit], 0)
        ctx_t = after(ctx_t, w_line)

        inputs = tokens.astype(F32)
        unit_one, rstd_one = norm_parts(inputs + left_product(ctx_t, full_wo) + full_bo)
        norm_one = unit_one * full_g1 + full_n1
        low_one = norm_one.astype(BF)

        inner_in = group_gather(low_one)
        pre = product(inner_in, w1_mine) + b1_mine
        phi = 0.5 * (1.0 + lax.erf(pre * (0.5**0.5)))
        act = (pre * phi).astype(BF)
        slope = phi + pre * (jnp.exp(-0.5 * pre * pre) * ((2 * jnp.pi) ** -0.5))
        unit_two, rstd_two = norm_parts(
            norm_one + group_scatter(product(act, w2_mine)) + full_b2
        )
        out_rows = (unit_two * full_g2 + full_n2).astype(BF)

        up = cotangent.astype(F32)
        grad_n2 = jnp.sum(up, axis=0)
        grad_g2 = jnp.sum(up * unit_two, axis=0)
        grad_two = norm_back(unit_two, rstd_two, full_g2, up)
        dz = grad_two.astype(BF)
        grad_b2 = jnp.sum(dz.astype(F32), axis=0)
        dz_all = group_gather(dz)
        grad_pre = (slope * right_product(dz_all, w2_mine)).astype(BF)
        grad_b1 = jnp.sum(grad_pre.astype(F32), axis=0).reshape(n_out, 1, ffl)

        grad_w2 = left_product(act, dz_all).astype(BF).reshape(n_out, ffl, width)
        grad_w1 = left_product(inner_in, grad_pre).astype(BF).reshape(n_out, 4 * rw, width)
        grads = jnp.concatenate([grad_w1, grad_w2], axis=1)
        grads = grads.reshape(n_head, n_out // n_head, 4 * rw + ffl, width)
        grads = jnp.swapaxes(grads, 0, 1)
        grad_norm = right_product(grad_pre, w1_mine)
        grad_norm = grad_two + group_scatter(grad_norm)
        grads = lax.psum_scatter(grads, z_bits, scatter_dimension=0)
        grads = grads.reshape((2,) * len(head_bits) + (4 * rw + ffl, width))

        grad_n1 = jnp.sum(grad_norm, axis=0)
        grad_g1 = jnp.sum(grad_norm * unit_one, axis=0)
        grad_one = norm_back(unit_one, rstd_one, full_g1, grad_norm)
        da = grad_one.astype(BF)
        grad_bo = jnp.sum(da.astype(F32), axis=0)
        grad_ctx = right_product(full_wo, da).astype(BF).reshape(H, 1, HD, rows)
        grad_ctx = jnp.broadcast_to(grad_ctx, (H, repl, HD, rows)).reshape(n_blk, HD, rows)
        grad_heads = lax.all_to_all(grad_ctx, blk_bits, 0, 0, tiled=True)

        later = after(da, grad_ctx)

        by_core = ctx_t.reshape(n_all // 2, 2, rw, rows)

        def core_half(core):
            return product(pick(by_core, core, 1).reshape(width // 2, rows), later)

        wo_other = swap(core_half(1 - my[c_bit]).astype(BF), c_bit)
        grad_wo = core_half(my[c_bit]) + after(wo_other, grad_ctx).astype(F32)
        grad_wo = grad_wo.reshape((2,) * (len(every) - 1) + (rw, width))
        w_line = both(w_line, c_bit, 0, grad_ctx)
        grad_heads = after(grad_heads, grad_wo, w_line)
        w_line = w_line.reshape(4 * 3 * part, width)
        wo_at = len(every) - 2
        wo_other = swap(pick(grad_wo, 1 - my[x_bit], wo_at).astype(BF), x_bit)

        part_q, others = attend_back(
            tab,
            n_head,
            far_turns,
            query,
            kv_two,
            kvt_two,
            low,
            high,
            lse,
            out,
            grad_heads,
            None,
        )
        others = others.reshape(n_head - 1, n_blk, LANE, LANE)
        part_q, wo_other = together(part_q, wo_other)
        grad_q, grad_kv = attend_back(
            tab, n_head, near_turn, query, kv, kvt, low, high, lse, out, grad_heads, part_q
        )
        terms = [grad_kv] + [others[k] for k in range(n_head - 1)]
        for i, bit in list(enumerate(head_bits[::-1]))[::-1]:
            terms = [
                terms[k].astype(F32) + swap(terms[k + (1 << i)].astype(BF), bit).astype(F32)
                for k in range(1 << i)
            ]
        grad_kv = terms[0].astype(BF)
        grad_wo = pick(grad_wo, my[x_bit], wo_at) + wo_other.astype(F32)

        def own_part(grad, count):
            grad = grad.reshape(n_blk, count, HD, LANE)
            if repl > 1:
                grad = lax.dynamic_slice_in_dim(grad, sub * part, part, axis=2)
            return grad.reshape(n_blk, count * part, LANE)

        def line_rows(grad, count):
            sent = own_part(grad, count).reshape(n_blk // 4, 2, 2, count * part, rows)
            sent = jnp.transpose(sent, (2, 1, 0, 3, 4)).reshape(
                4, n_blk // 4, count * part, rows
            )
            return lax.all_to_all(sent, (c_bit, x_bit), 0, 0, tiled=True)

        def line_product(weights, came):
            came = jnp.transpose(came, (0, 2, 1, 3)).reshape(12 * part, n_blk // 4 * rows)
            return left_product(came, weights)

        grad_qkv = jnp.concatenate([grad_q, grad_kv], axis=1)
        line_kv = line_rows(grad_qkv, 3)
        for bit in head_bits:
            grad_wo = summed(grad_wo, bit, 0, grad_kv)
        wo_half = grad_wo

        grad_in = line_product(w_line, line_kv)

        packed = rw == 32 and repl == 1
        shape = (n_all, 48, LANE) if packed else (width, 3 * HD)
        halves = tuple(flow.reshape(n_blk, rows // 2, width) for flow in stream)
        cut = head_columns(tab, halves, grad_qkv, shape)
        if not packed:
            cut = cut.reshape(width, 3, HD)
            if repl > 1:
                cut = lax.dynamic_slice_in_dim(cut, sub * part, part, axis=2)
            cut = cut.reshape(n_all, rw * 3 * part // LANE, LANE)
        own = (jnp.arange(H) == head).astype(F32)[:, None]
        if repl > 1:
            own = own * (sub == 0).astype(F32)
        bias_rows = jnp.sum(grad_qkv.astype(F32), axis=(0, 2))
        grad_bq = (own * bias_rows[None, :HD]).reshape(width)
        grad_bv = (own * bias_rows[None, 2 * HD :]).reshape(width)
        mark = (jnp.arange(4) == my[x_bit] * 2 + my[c_bit]).astype(F32)[None, :, None]
        b1_abs = (grad_b1 * mark).reshape(n_all, ffl)
        smalls = jnp.stack(
            [
                grad_bq,
                grad_bv,
                *after((grad_bo, grad_g1, grad_n1, grad_b2, grad_g2, grad_n2), grad_q),
            ]
        ).reshape(8, width // LANE, 1, LANE)
        share = LANE // rw
        smalls = jnp.swapaxes(smalls, 0, 1).reshape(width // LANE, 1, 8, LANE)
        smalls = jnp.broadcast_to(smalls, (width // LANE, share, 8, LANE))
        smalls = jnp.concatenate(
            [smalls.reshape(n_all, 8, LANE), as_rows([b1_abs])], axis=1
        )
        cut = jnp.concatenate([cut, smalls.astype(BF)], axis=1)
        n_cut = cut.shape[1]
        cut = cut.reshape((2,) * len(head_bits) + (n_blk, n_cut, LANE))
        for bit in head_bits:
            cut = summed(cut, bit, 0, grad_in)
        sent = cut.astype(BF)
        got = lax.all_to_all(sent, blk_bits, 0, 0, tiled=True)
        grads = after(grads, grad_in)
        for bit in head_bits[1:]:
            grads = summed(grads, bit, 1)
        other = swap(pick(grads, 1 - my[head_bits[0]], 0).astype(BF), head_bits[0])
        grad_in = grad_in.reshape((2,) * n_z + (rows, width))
        for i in range(1, n_z)[::-1]:
            grad_in = summed(grad_in, z_bits[i], i)
        grad_wo = after(wo_half, grad_in)
        for bit in z_bits:
            grad_wo = summed(grad_wo, bit, 0)
        grad_in = summed(grad_in, z_bits[0], 0)
        grads = pick(grads, my[head_bits[0]], 0).astype(F32) + other.astype(F32)
        grad_w2 = grads[4 * rw :]
        first = grads[: 4 * rw].astype(BF).reshape(2, 2, rw, n_out * ffl)
        first_other = swap(pick(first, 1 - my[x_bit], 0), x_bit)
        grad_w1 = placed_at(pick(first, my[x_bit], 0), first_other, my[x_bit], 0)
        grad_w1 = after(grad_w1, grad_in)
        came = swap(pick(grad_w1, 1 - my[c_bit], 1), c_bit)
        grad_w1 = placed_at(pick(grad_w1, my[c_bit], 1), came, my[c_bit], 1)
        grad_tokens = grad_one + grad_in
        grad_w1 = (
            jnp.transpose(grad_w1.reshape(4, rw, n_out, ffl), (1, 2, 0, 3))
            .reshape(rw, n_all * ffl)
            .astype(F32)
        )
        if packed:
            mats, vecs = owner_sums(got, width)
        else:
            got = got.astype(F32)
            mats = got[:, : n_cut - 9].reshape(H, repl, rw, 3, part)
            mats = jnp.transpose(mats, (3, 2, 0, 1, 4)).reshape(3, rw, width)
            vecs = jnp.sum(got[:, n_cut - 9 :], axis=0)
        lane = ((hi * n_blk + bi) & (share - 1)) * rw
        own_vecs = lax.dynamic_slice_in_dim(
            vecs[:8], lane, rw, 1, allow_negative_indices=False
        )
        grad_bq, grad_bv, grad_bo, grad_g1, grad_n1, grad_b2, grad_g2, grad_n2 = (
            own_vecs[i] for i in range(8)
        )
        grad_b1 = vecs[8, :ffl]
        return (
            out_rows,
            grad_tokens,
            mats[0],
            mats[1],
            mats[2],
            grad_bq,
            grad_bv,
            grad_wo,
            grad_bo,
            grad_g1,
            grad_n1,
            grad_w1,
            grad_b1,
            grad_w2,
            grad_b2,
            grad_g2,
            grad_n2,
        )

    return body


def solution(mesh):
    n_head, n_blk = mesh.shape["head"], mesh.shape["blk"]
    head_bits = tuple(f"h{i}" for i in range(n_head.bit_length() - 1))
    blk_bits = tuple(f"b{i}" for i in range(n_blk.bit_length() - 1))
    fine = Mesh(
        mesh.devices.reshape((2,) * len(head_bits + blk_bits)), head_bits + blk_bits
    )
    by_token = P(blk_bits + head_bits, None)
    by_row, by_entry = P(head_bits + blk_bits, None), P(head_bits + blk_bits)
    placed = (
        by_token,
        P(),
        by_token,
        by_row,
        by_row,
        by_row,
        by_entry,
        by_entry,
        by_row,
        by_entry,
        by_entry,
        by_entry,
        by_row,
        by_entry,
        by_row,
        by_entry,
        by_entry,
        by_entry,
    )
    given = (
        by_token,
        by_token,
        by_row,
        by_row,
        by_row,
        by_entry,
        by_entry,
        by_row,
        by_entry,
        by_entry,
        by_entry,
        by_row,
        by_entry,
        by_row,
        by_entry,
        by_entry,
        by_entry,
    )
    return jax.shard_map(
        make_body(head_bits, blk_bits),
        mesh=fine,
        in_specs=placed,
        out_specs=given,
        check_vma=False,
    )
```

```python
import functools

import jax
import jax.numpy as jnp
from jax import lax
from jax.experimental import pallas as pl
from jax.experimental.pallas import tpu as pltpu
from jax.sharding import Mesh, PartitionSpec as P

H = 16
HD = 64
DOCS = 24
EPS = 1e-05
NEG = -1e30
LANE = 128
TQ = 256
KB = 512
KB_LOG = KB.bit_length() - 1

BF = jnp.bfloat16
F32 = jnp.float32


def swap(value, axis):
    return lax.ppermute(value, axis, [(0, 1), (1, 0)])


def pick(value, index, axis):
    return lax.dynamic_index_in_dim(
        value, index, axis, keepdims=False, allow_negative_indices=False
    )


def placed_at(value, other, place, axis):
    value, other = jnp.expand_dims(value, axis), jnp.expand_dims(other, axis)
    twice = jnp.broadcast_to(
        value, value.shape[:axis] + (2,) + value.shape[axis + 1 :]
    )
    return lax.dynamic_update_slice_in_dim(
        twice, other, 1 - place, axis, allow_negative_indices=False
    )


def after(value, *others):
    return lax.optimization_barrier((value,) + others)[0]


def together(*values):
    return lax.optimization_barrier(values)


def with_other(value, axis, gate=None):
    sent = value if gate is None else after(value, gate)
    return jnp.concatenate([sent, swap(sent, axis)])


def left_product(former, latter):
    return lax.dot_general(
        former, latter, (((0,), (0,)), ((), ())), preferred_element_type=F32
    )


def right_product(former, latter):
    return lax.dot_general(
        former, latter, (((1,), (1,)), ((), ())), preferred_element_type=F32
    )


def product(former, latter):
    return jnp.dot(former, latter, preferred_element_type=F32)


def norm_parts(hidden):
    centre = hidden - jnp.mean(hidden, axis=-1, keepdims=True)
    rstd = lax.rsqrt(jnp.mean(centre * centre, axis=-1, keepdims=True) + EPS)
    return centre * rstd, rstd


def norm_back(unit, rstd, gain, grad):
    inner = grad * gain
    return rstd * (
        inner
        - jnp.mean(inner, axis=-1, keepdims=True)
        - unit * jnp.mean(inner * unit, axis=-1, keepdims=True)
    )


def same_doc(low_ref, high_ref, first, heads):
    row = lax.broadcasted_iota(jnp.int32, (KB, TQ), 0)
    place = first + row + (row >> 7) * (LANE * (heads - 1))
    return jnp.logical_and(place >= low_ref[...], place < high_ref[...])


def over_groups(tab, blocks, step, state):
    tile, tiles = pl.program_id(0), pl.num_programs(0)
    start, stop, inner, outer = (
        tab[2 * blocks + i * tiles + tile] for i in range(4)
    )
    state = lax.fori_loop(start, inner, functools.partial(step, True), state)
    state = lax.fori_loop(inner, outer, functools.partial(step, False), state)
    return lax.fori_loop(outer, stop, functools.partial(step, True), state)


def attend_kernel(blocks, heads, turns, first, last, tab, *refs):
    q0, q1, q2, q3, kv_a, kv_b, low, high = refs[:8]
    refs = refs[8:]
    if not first:
        (top_in, total_in, mixed_in), refs = refs[:3], refs[3:]
    kv, kvt = refs[:2]
    made, (acc, raw) = refs[2:5], refs[5:]
    tile, tiles = pl.program_id(0), pl.num_programs(0)
    head = tab[2 * blocks + 4 * tiles]
    start = tab[2 * blocks + tile]
    stop = tab[2 * blocks + tiles + tile]

    @pl.when(tile == 0)
    def _():
        for n in range(len(turns)):

            def place(i, carry):
                halves = []
                for j in range(4):
                    halves.append(kv_a[n * blocks + tab[4 * i + j]])
                    halves.append(kv_b[n * blocks + tab[blocks + 4 * i + j]])
                block = jnp.concatenate(halves, axis=0)
                at = (n * blocks + i * 4) * LANE
                at = pl.ds(pl.multiple_of(at, 4 * LANE), 4 * LANE)
                kv[at, :] = block
                kvt[:, at] = block.T
                return carry

            lax.fori_loop(0, blocks // 4, place, 0)

    query = jnp.concatenate([q0[...], q1[...], q2[...], q3[...]], axis=0)
    query_t = query.T
    if first:
        acc[...] = jnp.zeros_like(acc)
        state = (jnp.full((1, TQ), NEG, F32), jnp.zeros((1, TQ), F32))
    else:
        acc[...] = jnp.concatenate([jnp.zeros((HD, TQ), F32), mixed_in[...]], axis=0)
        state = (top_in[...], total_in[...])
    for n, turn in enumerate(turns):
        base = n * blocks * LANE
        parity = lax.bitwise_xor(head, turn) * LANE

        def ahead(j):
            at = pl.multiple_of(base + lax.min(j, stop - 1) * KB, KB)
            raw[lax.bitwise_and(j, 1)] = product(kv[pl.ds(at, KB), :], query_t)

        def step(masked, j, carry):
            top, total = carry
            scores = raw[lax.bitwise_and(j, 1)]
            ahead(j + 1)
            if masked:
                inside = same_doc(low, high, j * (KB * heads) + parity, heads)
                scores = jnp.where(inside, scores, NEG)
            new_top = jnp.maximum(top, jnp.max(scores, axis=0, keepdims=True))
            factor = jnp.exp(top - new_top)
            expo = jnp.exp(scores - new_top)
            total = total * factor + jnp.sum(expo, axis=0, keepdims=True)
            at = pl.ds(pl.multiple_of(base + j * KB, KB), KB)
            acc[...] = acc[...] * factor + product(kvt[:, at], expo.astype(BF))
            return new_top, total

        ahead(start)
        state = over_groups(tab, blocks, step, state)
    top, total = state
    if last:
        ctx, out, lse = made
        mixed = acc[HD:, :] / total
        lse[...] = top + jnp.log(total)
        for half in range(2):
            part = mixed[:, half * LANE : (half + 1) * LANE]
            out[half] = part
            ctx[half] = part.astype(BF)
    else:
        made[0][...], made[1][...], made[2][...] = top, total, acc[HD:, :]


def attend_back_kernel(blocks, heads, turns, first, tab, *refs):
    q0, q1, q2, q3, kv, kvt, low, high, lse, out, grad = refs[:11]
    refs = refs[11:]
    if not first:
        part_in, refs = refs[0], refs[1:]
    grad_q, grad_kv, acc, acc_kv = refs
    tile, tiles = pl.program_id(0), pl.num_programs(0)
    head = tab[2 * blocks + 4 * tiles]

    @pl.when(tile == 0)
    def _():
        def clear(j, carry):
            acc_kv[pl.ds(pl.multiple_of(j * KB, KB), KB), :] = jnp.zeros((KB, LANE), F32)
            return carry

        lax.fori_loop(0, len(turns) * blocks * LANE // KB, clear, 0)

    query = jnp.concatenate([q0[...], q1[...], q2[...], q3[...]], axis=0)
    query_t = query.T
    grad_t = jnp.concatenate([grad[0], grad[1]], axis=1).astype(F32)
    out_t = jnp.concatenate([out[0], out[1]], axis=1)
    delta = jnp.sum(grad_t * out_t, axis=0, keepdims=True)
    grad_pad = jnp.concatenate([jnp.zeros((HD, TQ), F32), grad_t], axis=0).astype(BF)
    grad_row = grad_pad.T
    log_sum = lse[...]
    acc[...] = jnp.zeros_like(acc)
    for n, turn in enumerate(turns):
        base = n * blocks * LANE
        parity = lax.bitwise_xor(head, turn) * LANE

        def step(masked, j, carry):
            at = pl.ds(pl.multiple_of(base + j * KB, KB), KB)
            keys = kv[at, :]
            scores = product(keys, query_t)
            if masked:
                inside = same_doc(low, high, j * (KB * heads) + parity, heads)
                scores = jnp.where(inside, scores, NEG)
            prob = jnp.exp(scores - log_sum)
            grad_prob = product(keys, grad_pad)
            grad_score = (prob * (grad_prob - delta)).astype(BF)
            acc_kv[at, :] += product(grad_score, query) + product(prob.astype(BF), grad_row)
            acc[...] += product(kvt[:, at], grad_score)
            return carry

        over_groups(tab, blocks, step, 0)
    if first:
        grad_q[...] = acc[:HD, :]
    else:
        result = ((acc[:HD, :] + part_in[...]) * (HD**-0.5)).astype(BF)
        grad_q[0] = result[:, :LANE]
        grad_q[1] = result[:, LANE:]

    @pl.when(tile == tiles - 1)
    def _():
        def write(b, carry):
            block = acc_kv[pl.ds(pl.multiple_of(b * LANE, LANE), LANE), :]
            grad_kv[b] = block.astype(grad_kv.dtype).T
            return carry

        lax.fori_loop(0, len(turns) * blocks, write, 0, unroll=4)


def whole_spec(shape):
    return pl.BlockSpec(shape, lambda t, tab: (0,) * len(shape))


def tile_specs(blocks):
    def half(at):
        return pl.BlockSpec((None, LANE // 2, LANE), lambda t, tab: (tab[at(t)], 0, 0))

    return (
        [
            half(lambda t: 2 * t),
            half(lambda t: blocks + 2 * t),
            half(lambda t: 2 * t + 1),
            half(lambda t: blocks + 2 * t + 1),
        ],
        pl.BlockSpec((None, 1, TQ), lambda t, tab: (t, 0, 0)),
        pl.BlockSpec((2, HD, LANE), lambda t, tab: (t, 0, 0)),
        pl.BlockSpec((None, HD, TQ), lambda t, tab: (t, 0, 0)),
    )


def attend(tab, heads, turns, query, kv_rel, low, high, state, last):
    blocks, nb = query[0].shape[0], kv_rel[0].shape[0]
    tiles, total = blocks // 2, nb * LANE
    halves, row, pair, tall = tile_specs(blocks)
    row_shape = jax.ShapeDtypeStruct((tiles, 1, TQ), F32)
    tall_shape = jax.ShapeDtypeStruct((tiles, HD, TQ), F32)
    if last:
        made = (
            jax.ShapeDtypeStruct((blocks, HD, LANE), BF),
            jax.ShapeDtypeStruct((blocks, HD, LANE), F32),
            row_shape,
        )
    return pl.pallas_call(
        functools.partial(attend_kernel, blocks, heads, turns, not state, last),
        out_shape=(
            jax.ShapeDtypeStruct((total, LANE), BF),
            jax.ShapeDtypeStruct((LANE, total), BF),
        )
        + (made if last else (row_shape, row_shape, tall_shape)),
        grid_spec=pltpu.PrefetchScalarGridSpec(
            num_scalar_prefetch=1,
            grid=(tiles,),
            in_specs=halves
            + [whole_spec((nb, LANE // 2, LANE))] * 2
            + [row, row]
            + ([row, row, tall] if state else []),
            out_specs=[whole_spec((total, LANE)), whole_spec((LANE, total))]
            + ([pair, pair, row] if last else [row, row, tall]),
            scratch_shapes=[
                pltpu.VMEM((LANE, TQ), F32),
                pltpu.VMEM((2, KB, TQ), F32),
            ],
        ),
        compiler_params=pltpu.CompilerParams(vmem_limit_bytes=56 << 20),
        cost_estimate=pl.CostEstimate(
            flops=20 * 10**9, bytes_accessed=6 * 10**6, transcendentals=4 * 10**6
        ),
    )(
        tab,
        query[0],
        query[1],
        query[0],
        query[1],
        kv_rel[0],
        kv_rel[1],
        low,
        high,
        *state,
    )


def attend_back(tab, heads, turns, query, kv, kvt, low, high, lse, out, grad, part):
    blocks, total = query[0].shape[0], kv.shape[0]
    halves, row, pair, tall = tile_specs(blocks)
    first = part is None
    if first:
        q_shape = jax.ShapeDtypeStruct((blocks // 2, HD, TQ), F32)
    else:
        q_shape = jax.ShapeDtypeStruct((blocks, HD, LANE), BF)
    return pl.pallas_call(
        functools.partial(attend_back_kernel, blocks, heads, turns, first),
        out_shape=(
            q_shape,
            jax.ShapeDtypeStruct((total // LANE, LANE, LANE), BF if first else F32),
        ),
        grid_spec=pltpu.PrefetchScalarGridSpec(
            num_scalar_prefetch=1,
            grid=(blocks // 2,),
            in_specs=halves
            + [
                whole_spec((total, LANE)),
                whole_spec((LANE, total)),
                row,
                row,
                row,
                pair,
                pair,
            ]
            + ([] if first else [tall]),
            out_specs=[
                tall if first else pair,
                whole_spec((total // LANE, LANE, LANE)),
            ],
            scratch_shapes=[
                pltpu.VMEM((LANE, TQ), F32),
                pltpu.VMEM((total, LANE), F32),
            ],
        ),
        compiler_params=pltpu.CompilerParams(vmem_limit_bytes=60 << 20),
        cost_estimate=pl.CostEstimate(
            flops=30 * 10**9, bytes_accessed=10 * 10**6, transcendentals=4 * 10**6
        ),
    )(
        tab,
        query[0],
        query[1],
        query[0],
        query[1],
        kv,
        kvt,
        low,
        high,
        lse,
        out,
        grad,
        *(() if first else (part,)),
    )


def cols_kernel(parts, tab, *refs):
    halves, (grad, cols, acc) = refs[:8], refs[8:]
    step = pl.program_id(0)
    rows = jnp.concatenate([half[...] for half in halves], axis=0)
    wide = jnp.concatenate([grad[i] for i in range(4)], axis=1)
    term = product(wide, rows)

    @pl.when(step == 0)
    def _():
        acc[...] = term

    @pl.when(step > 0)
    def _():
        acc[...] += term

    @pl.when(step == pl.num_programs(0) - 1)
    def _():
        for p in range(parts):
            block = acc[p * HD : (p + 1) * HD, :].T
            if len(cols.shape) == 2:
                cols[:, p * HD : (p + 1) * HD] = block.astype(BF)
            else:
                halves = block.reshape(cols.shape[0], 2, 16, HD)
                cols[:, p * 16 : (p + 1) * 16, :] = jnp.concatenate(
                    [halves[:, 0], halves[:, 1]], axis=-1
                ).astype(BF)


def head_columns(tab, stream, grad, shape):
    blocks, deep, _ = grad.shape
    width = stream[0].shape[-1]

    def half(at):
        return pl.BlockSpec(
            (None, LANE // 2, width), lambda t, tab: (tab[at + 4 * t], 0, 0)
        )

    return pl.pallas_call(
        functools.partial(cols_kernel, deep // HD),
        out_shape=jax.ShapeDtypeStruct(shape, BF),
        grid_spec=pltpu.PrefetchScalarGridSpec(
            num_scalar_prefetch=1,
            grid=(blocks // 4,),
            in_specs=[half(i + blocks * j) for i in range(4) for j in range(2)]
            + [pl.BlockSpec((4, deep, LANE), lambda t, tab: (t, 0, 0))],
            out_specs=whole_spec(shape),
            scratch_shapes=[pltpu.VMEM((deep, width), F32)],
        ),
        compiler_params=pltpu.CompilerParams(vmem_limit_bytes=24 << 20),
        cost_estimate=pl.CostEstimate(
            flops=4 * 10**9, bytes_accessed=2 * stream[0].size * 2, transcendentals=0
        ),
    )(tab, *(stream * 4), grad)


def owner_kernel(got, mats, vec):
    rows = got.shape[1]
    low = lax.broadcasted_iota(jnp.int32, (16, LANE), 1) < HD
    total = jnp.zeros(vec.shape, F32)
    for n in range(got.shape[0]):
        total = total + got[n, 48:rows, :].astype(F32)
    vec[...] = total
    for p in range(3):
        for pair in range(H // 2):
            even, odd = jnp.zeros((16, LANE), F32), jnp.zeros((16, LANE), F32)
            for base in range(0, got.shape[0], H):
                even = even + got[base + 2 * pair, p * 16 : (p + 1) * 16, :].astype(F32)
                odd = odd + got[base + 2 * pair + 1, p * 16 : (p + 1) * 16, :].astype(F32)
            at = slice(pair * LANE, (pair + 1) * LANE)
            mats[p, :16, at] = jnp.where(low, even, pltpu.roll(odd, HD, 1))
            mats[p, 16:, at] = jnp.where(low, pltpu.roll(even, HD, 1), odd)


def owner_sums(got, width):
    return pl.pallas_call(
        owner_kernel,
        out_shape=(
            jax.ShapeDtypeStruct((3, 32, width), F32),
            jax.ShapeDtypeStruct((got.shape[1] - 48, LANE), F32),
        ),
        compiler_params=pltpu.CompilerParams(vmem_limit_bytes=16 << 20),
        cost_estimate=pl.CostEstimate(
            flops=got.size, bytes_accessed=got.size * 2 + width * 400, transcendentals=0
        ),
    )(got)


def as_rows(vectors):
    return jnp.stack(
        [jnp.pad(v, ((0, 0), (0, LANE - v.shape[1]))) for v in vectors], axis=1
    )


def make_body(head_bits, blk_bits):
    n_head, n_blk = 1 << len(head_bits), 1 << len(blk_bits)
    n_all = n_head * n_blk
    every = head_bits + blk_bits
    z_bits, x_bit, c_bit = blk_bits[:-2], blk_bits[-2], blk_bits[-1]
    outer = head_bits + z_bits
    repl = n_blk // H
    part = HD // repl
    n_out, n_head_z = 1 << len(outer), len(outer)

    def body(
        tokens,
        segments,
        cotangent,
        w_query,
        w_key,
        w_value,
        b_query,
        b_value,
        w_output,
        b_output,
        gain_attn,
        shift_attn,
        w_inner,
        b_inner,
        w_outer,
        b_outer,
        gain_ffn,
        shift_ffn,
    ):
        rows, width = tokens.shape
        rw = w_query.shape[0]
        ffl = w_outer.shape[0]
        my = {bit: lax.axis_index(bit) for bit in every}
        hi, bi = lax.axis_index(head_bits), lax.axis_index(blk_bits)
        head = bi if repl == 1 else lax.div(bi, repl)
        sub = bi - head * repl

        def both(value, bit, axis, then=None):
            other = swap(value, bit)
            if then is not None:
                other = after(other, then)
            return placed_at(value, other, my[bit], axis)

        def summed(value, bit, axis, then=None):
            other = swap(pick(value, 1 - my[bit], axis).astype(BF), bit)
            if then is not None:
                other = after(other, then)
            return pick(value, my[bit], axis).astype(F32) + other.astype(F32)

        def traded(value, bits, thens=(None, None)):
            for axis, bit in enumerate(bits):
                other = swap(pick(value, 1 - my[bit], axis), bit)
                if thens[axis] is not None:
                    other = after(other, thens[axis])
                kept = pick(value, my[bit], axis)
                value = placed_at(kept, other, my[bit], axis)
            return value

        def over(value, bits, at, thens):
            for i, bit in enumerate(bits):
                value = both(value, bit, at + i, thens[i])
            return value

        def group_gather(part_rows):
            return with_other(with_other(part_rows, x_bit), c_bit)

        def group_scatter(partial):
            part_rows = partial.reshape(2, 2, rows, width)
            mine = part_rows[0] + swap(part_rows[1].astype(BF), c_bit).astype(F32)
            return mine[0] + swap(mine[1].astype(BF), x_bit).astype(F32)

        ways = (z_bits + (x_bit,), (x_bit,) + z_bits)
        flows = [tokens[: rows // 2], tokens[rows // 2 :]]
        hops = [[flow] for flow in flows]
        for i in range(len(ways[0])):
            for flow, way in zip(hops, ways, strict=True):
                flow.append(with_other(flow[-1], way[i]))

        small = as_rows(
            [
                v[None]
                for v in (
                    b_query,
                    b_value,
                    b_output,
                    gain_attn,
                    shift_attn,
                    b_outer,
                    gain_ffn,
                    shift_ffn,
                    b_inner,
                )
            ]
        )
        scale = HD**-0.5
        cut_q, cut_k, cut_v = (
            w.reshape(rw, H, HD) for w in (w_query * BF(scale), w_key, w_value)
        )
        cols = jnp.concatenate(
            [
                jnp.concatenate([cut_k, cut_v], axis=2),
                jnp.concatenate([cut_q, jnp.zeros_like(cut_q)], axis=2),
            ]
        )
        cols = jnp.transpose(cols, (1, 0, 2))[:, None]
        cols = jnp.broadcast_to(cols, (H, repl, 2 * rw, LANE))
        smalls = jnp.broadcast_to(small, (n_blk,) + small.shape[1:])
        cols_all = jnp.concatenate([cols.reshape(n_blk, 2 * rw, LANE), smalls], axis=1)
        got = lax.all_to_all(after(cols_all, hops[1][1]), blk_bits, 0, 0, tiled=True)
        for i, bit in enumerate(head_bits):
            got = both(got, bit, i, hops[1][-1])
        got = got.reshape((n_all,) + got.shape[len(head_bits) + 1 :])

        stream = [with_other(flow[-1], c_bit, got) for flow in hops]
        w_kv = got[:, :rw].reshape(width, LANE)
        w_q = got[:, rw : 2 * rw].reshape(width, LANE)
        vecs = got[:, 2 * rw :].astype(F32)
        named = [vecs[:, i, :rw].reshape(width) for i in range(8)]
        full_bq, full_bv, full_bo, full_g1, full_n1, full_b2, full_g2, full_n2 = named
        full_b1 = vecs[:, 8, :ffl].reshape(n_out, 4, ffl)
        b1_mine = pick(full_b1, my[x_bit] * 2 + my[c_bit], 1).reshape(n_out * ffl)

        n_z = len(z_bits)
        wo_row = over(w_output, z_bits, 0, hops[0][1 : 1 + n_z])
        wo_row = over(wo_row, head_bits, 0, [None] * (len(head_bits) - 1) + [hops[0][-1]])
        w1_cut = jnp.transpose(w_inner.reshape(rw, n_out, 2, 2, ffl), (2, 3, 0, 1, 4))
        w1_cut = traded(
            w1_cut.reshape(2, 2, rw, n_out * ffl), (x_bit, c_bit), hops[0][1:3]
        ).reshape(4 * rw, n_out * ffl)
        w_pair = after(jnp.concatenate([w1_cut, w_outer]), hops[1][2])
        w_pair = lax.all_gather(w_pair, outer)
        w1_mine = w_pair[:, : 4 * rw].reshape(width, n_out * ffl)
        w2_mine = w_pair[:, 4 * rw :].reshape(n_out * ffl, width)

        spot = jnp.arange(n_blk)

        def slots(way):
            apart = spot ^ bi
            total = 0
            for i, bit in enumerate(way + (c_bit,)):
                total = total + (((apart >> (len(blk_bits) - 1 - blk_bits.index(bit))) & 1) << i)
            return total

        slot = [slots(way) for way in ways]
        ids = jnp.arange(DOCS)[:, None]
        below = jnp.sum((segments[None] < ids).astype(jnp.int32), axis=1)
        upto = jnp.sum((segments[None] <= ids).astype(jnp.int32), axis=1)
        own_segs = pick(segments.reshape(n_blk, n_head, LANE), hi, 1).reshape(
            n_blk // 2, 1, TQ
        )
        member = own_segs[None] == ids[:, :, None, None]
        low = jnp.sum(jnp.where(member, below[:, None, None, None], 0), axis=0)
        high = jnp.sum(jnp.where(member, upto[:, None, None, None], 0), axis=0)
        far = KB_LOG + len(head_bits)
        start = low[:, 0, 0] >> far
        stop = (high[:, 0, -1] + ((1 << far) - 1)) >> far
        inner = (jnp.max(low, axis=(1, 2)) + ((1 << far) - 1)) >> far
        inner = jnp.clip(inner, start, stop)
        outer_end = jnp.clip(jnp.min(high, axis=(1, 2)) >> far, inner, stop)
        tab = jnp.concatenate(slot + [start, stop, inner, outer_end, hi[None]])
        tab = tab.astype(jnp.int32)

        bias = jnp.concatenate(
            [
                pick(full_bq.reshape(H, HD), head, 0) * scale,
                jnp.zeros((HD,), F32),
                jnp.zeros((HD,), F32),
                pick(full_bv.reshape(H, HD), head, 0),
            ]
        )
        kv_rel, query = [], []
        for flow in stream:
            kv_own = (product(flow, w_kv) + bias[LANE:]).astype(BF)
            kv_rel.append(kv_own.reshape(n_blk, rows // 2, LANE))
        kv_pair = kv_near = jnp.concatenate(kv_rel, axis=1)
        wo_row = both(wo_row, x_bit, n_head_z, kv_near)
        w_line = jnp.concatenate([w_q[:, :HD] * BF(1.0 / scale), w_kv], axis=1).T
        if repl > 1:
            w_line = lax.dynamic_slice_in_dim(
                w_line.reshape(3, HD, width), sub * part, part, axis=1
            ).reshape(3 * part, width)
        group_other = swap(after(w_line, kv_near), x_bit)
        for bit in head_bits[::-1]:
            kv_pair = with_other(kv_pair, bit) if n_head > 2 else swap(kv_pair, bit)
        kv_far = kv_pair[n_blk:] if n_head > 2 else kv_pair
        kv_far = [kv_far[:, : rows // 2], kv_far[:, rows // 2 :]]
        for flow in stream:
            own_q = (product(flow, w_q) + bias[:LANE]).astype(BF)
            query.append(own_q.reshape(n_blk, rows // 2, LANE))
        near_turn, far_turns = (0,), tuple(range(1, n_head))
        kv, kvt, *state = attend(
            tab, n_head, near_turn, query, kv_rel, low, high, (), False
        )
        kv_two, kvt_two, ctx, out, lse = attend(
            tab, n_head, far_turns, query, kv_far, low, high, state, True
        )
        ctx = after(ctx, group_other)
        if repl > 1:
            ctx = lax.dynamic_slice_in_dim(ctx, sub * part, part, axis=1)
        ctx_t = lax.all_to_all(ctx, blk_bits, 0, 0, tiled=True).reshape(width, rows)

        full_wo = both(wo_row, c_bit, n_head_z + 1, ctx_t).reshape(width, width)

        w_line = placed_at(w_line, after(group_other, ctx), my[x_bit], 0)
        ctx_t = after(ctx_t, w_line)

        inputs = tokens.astype(F32)
        unit_one, rstd_one = norm_parts(inputs + left_product(ctx_t, full_wo) + full_bo)
        norm_one = unit_one * full_g1 + full_n1
        low_one = norm_one.astype(BF)

        near = with_other(low_one, x_bit)
        near, w1_mine, w2_mine = together(near, w1_mine, w2_mine)
        inner_in = with_other(near, c_bit)
        pre = product(inner_in, w1_mine) + b1_mine
        phi = 0.5 * (1.0 + lax.erf(pre * (0.5**0.5)))
        act = (pre * phi).astype(BF)
        slope = phi + pre * (jnp.exp(-0.5 * pre * pre) * ((2 * jnp.pi) ** -0.5))
        unit_two, rstd_two = norm_parts(
            norm_one + group_scatter(product(act, w2_mine)) + full_b2
        )
        out_rows = (unit_two * full_g2 + full_n2).astype(BF)

        up = cotangent.astype(F32)
        grad_n2 = jnp.sum(up, axis=0)
        grad_g2 = jnp.sum(up * unit_two, axis=0)
        grad_two = norm_back(unit_two, rstd_two, full_g2, up)
        dz = grad_two.astype(BF)
        grad_b2 = jnp.sum(dz.astype(F32), axis=0)
        dz_all = group_gather(dz)
        grad_pre = (slope * right_product(dz_all, w2_mine)).astype(BF)
        grad_b1 = jnp.sum(grad_pre.astype(F32), axis=0).reshape(n_out, 1, ffl)

        grad_w2 = left_product(act, dz_all).astype(BF).reshape(n_out, ffl, width)
        grad_w1 = left_product(inner_in, grad_pre).astype(BF).reshape(n_out, 4 * rw, width)
        grads = jnp.concatenate([grad_w1, grad_w2], axis=1)
        grads = grads.reshape(n_head, n_out // n_head, 4 * rw + ffl, width)
        grads = jnp.swapaxes(grads, 0, 1)
        grad_norm = right_product(grad_pre, w1_mine)
        grad_norm = grad_two + group_scatter(grad_norm)
        grads = lax.psum_scatter(grads, z_bits, scatter_dimension=0)
        grads = grads.reshape((2,) * len(head_bits) + (4 * rw + ffl, width))

        grad_n1 = jnp.sum(grad_norm, axis=0)
        grad_g1 = jnp.sum(grad_norm * unit_one, axis=0)
        grad_one = norm_back(unit_one, rstd_one, full_g1, grad_norm)
        da = grad_one.astype(BF)
        grad_bo = jnp.sum(da.astype(F32), axis=0)
        grad_ctx = right_product(full_wo, da).astype(BF).reshape(H, 1, HD, rows)
        grad_ctx = jnp.broadcast_to(grad_ctx, (H, repl, HD, rows)).reshape(n_blk, HD, rows)
        grad_heads = lax.all_to_all(grad_ctx, blk_bits, 0, 0, tiled=True)

        later = after(da, grad_ctx)

        by_core = ctx_t.reshape(n_all // 2, 2, rw, rows)

        def core_half(core):
            return product(pick(by_core, core, 1).reshape(width // 2, rows), later)

        wo_other = swap(core_half(1 - my[c_bit]).astype(BF), c_bit)
        grad_wo = core_half(my[c_bit]) + after(wo_other, grad_ctx).astype(F32)
        grad_wo = grad_wo.reshape((2,) * (len(every) - 1) + (rw, width))
        w_line = both(w_line, c_bit, 0, grad_ctx)
        grad_heads = after(grad_heads, grad_wo, w_line)
        w_line = w_line.reshape(4 * 3 * part, width)
        wo_at = len(every) - 2
        wo_other = swap(pick(grad_wo, 1 - my[x_bit], wo_at).astype(BF), x_bit)

        part_q, others = attend_back(
            tab,
            n_head,
            far_turns,
            query,
            kv_two,
            kvt_two,
            low,
            high,
            lse,
            out,
            grad_heads,
            None,
        )
        others = others.reshape(n_head - 1, n_blk, LANE, LANE)
        part_q, wo_other = together(part_q, wo_other)
        grad_q, grad_kv = attend_back(
            tab, n_head, near_turn, query, kv, kvt, low, high, lse, out, grad_heads, part_q
        )
        terms = [grad_kv] + [others[k] for k in range(n_head - 1)]
        for i, bit in list(enumerate(head_bits[::-1]))[::-1]:
            terms = [
                terms[k].astype(F32) + swap(terms[k + (1 << i)].astype(BF), bit).astype(F32)
                for k in range(1 << i)
            ]
        grad_kv = terms[0].astype(BF)
        grad_wo = pick(grad_wo, my[x_bit], wo_at) + wo_other.astype(F32)

        def own_part(grad, count):
            grad = grad.reshape(n_blk, count, HD, LANE)
            if repl > 1:
                grad = lax.dynamic_slice_in_dim(grad, sub * part, part, axis=2)
            return grad.reshape(n_blk, count * part, LANE)

        def line_rows(grad, count):
            sent = own_part(grad, count).reshape(n_blk // 4, 2, 2, count * part, rows)
            sent = jnp.transpose(sent, (2, 1, 0, 3, 4)).reshape(
                4, n_blk // 4, count * part, rows
            )
            return lax.all_to_all(sent, (c_bit, x_bit), 0, 0, tiled=True)

        def line_product(weights, came):
            came = jnp.transpose(came, (0, 2, 1, 3)).reshape(12 * part, n_blk // 4 * rows)
            return left_product(came, weights)

        grad_qkv = jnp.concatenate([grad_q, grad_kv], axis=1)
        line_kv = line_rows(grad_qkv, 3)
        for bit in head_bits:
            grad_wo = summed(grad_wo, bit, 0, grad_kv)
        wo_half = grad_wo

        grad_in = line_product(w_line, line_kv)

        packed = rw == 32 and repl == 1
        shape = (n_all, 48, LANE) if packed else (width, 3 * HD)
        halves = tuple(flow.reshape(n_blk, rows // 2, width) for flow in stream)
        cut = head_columns(tab, halves, grad_qkv, shape)
        if not packed:
            cut = cut.reshape(width, 3, HD)
            if repl > 1:
                cut = lax.dynamic_slice_in_dim(cut, sub * part, part, axis=2)
            cut = cut.reshape(n_all, rw * 3 * part // LANE, LANE)
        own = (jnp.arange(H) == head).astype(F32)[:, None]
        if repl > 1:
            own = own * (sub == 0).astype(F32)
        bias_rows = jnp.sum(grad_qkv.astype(F32), axis=(0, 2))
        grad_bq = (own * bias_rows[None, :HD]).reshape(width)
        grad_bv = (own * bias_rows[None, 2 * HD :]).reshape(width)
        mark = (jnp.arange(4) == my[x_bit] * 2 + my[c_bit]).astype(F32)[None, :, None]
        b1_abs = (grad_b1 * mark).reshape(n_all, ffl)
        smalls = jnp.stack(
            [
                grad_bq,
                grad_bv,
                *after((grad_bo, grad_g1, grad_n1, grad_b2, grad_g2, grad_n2), grad_q),
            ]
        ).reshape(8, width // LANE, 1, LANE)
        share = LANE // rw
        smalls = jnp.swapaxes(smalls, 0, 1).reshape(width // LANE, 1, 8, LANE)
        smalls = jnp.broadcast_to(smalls, (width // LANE, share, 8, LANE))
        smalls = jnp.concatenate(
            [smalls.reshape(n_all, 8, LANE), as_rows([b1_abs])], axis=1
        )
        cut = jnp.concatenate([cut, smalls.astype(BF)], axis=1)
        n_cut = cut.shape[1]
        cut = cut.reshape((2,) * len(head_bits) + (n_blk, n_cut, LANE))
        for bit in head_bits:
            cut = summed(cut, bit, 0, grad_in)
        sent = cut.astype(BF)
        got = lax.all_to_all(sent, blk_bits, 0, 0, tiled=True)
        grads = after(grads, grad_in)
        for bit in head_bits[1:]:
            grads = summed(grads, bit, 1)
        other = swap(pick(grads, 1 - my[head_bits[0]], 0).astype(BF), head_bits[0])
        grad_in = grad_in.reshape((2,) * n_z + (rows, width))
        for i in range(1, n_z)[::-1]:
            grad_in = summed(grad_in, z_bits[i], i)
        grad_wo = after(wo_half, line_kv)
        for bit in z_bits[:1]:
            grad_wo = summed(grad_wo, bit, 0, grad_in)
        for bit in z_bits[1:]:
            grad_wo = summed(grad_wo, bit, 0)
        grad_in = summed(grad_in, z_bits[0], 0)
        grads = pick(grads, my[head_bits[0]], 0).astype(F32) + other.astype(F32)
        grad_w2 = grads[4 * rw :]
        first = grads[: 4 * rw].astype(BF).reshape(2, 2, rw, n_out * ffl)
        first_other = swap(pick(first, 1 - my[x_bit], 0), x_bit)
        grad_w1 = placed_at(pick(first, my[x_bit], 0), first_other, my[x_bit], 0)
        grad_w1 = after(grad_w1, grad_in)
        came = swap(pick(grad_w1, 1 - my[c_bit], 1), c_bit)
        grad_w1 = placed_at(pick(grad_w1, my[c_bit], 1), came, my[c_bit], 1)
        grad_tokens = grad_one + grad_in
        grad_w1 = (
            jnp.transpose(grad_w1.reshape(4, rw, n_out, ffl), (1, 2, 0, 3))
            .reshape(rw, n_all * ffl)
            .astype(F32)
        )
        if packed:
            mats, vecs = owner_sums(got, width)
        else:
            got = got.astype(F32)
            mats = got[:, : n_cut - 9].reshape(H, repl, rw, 3, part)
            mats = jnp.transpose(mats, (3, 2, 0, 1, 4)).reshape(3, rw, width)
            vecs = jnp.sum(got[:, n_cut - 9 :], axis=0)
        lane = ((hi * n_blk + bi) & (share - 1)) * rw
        own_vecs = lax.dynamic_slice_in_dim(
            vecs[:8], lane, rw, 1, allow_negative_indices=False
        )
        grad_bq, grad_bv, grad_bo, grad_g1, grad_n1, grad_b2, grad_g2, grad_n2 = (
            own_vecs[i] for i in range(8)
        )
        grad_b1 = vecs[8, :ffl]
        return (
            out_rows,
            grad_tokens,
            mats[0],
            mats[1],
            mats[2],
            grad_bq,
            grad_bv,
            grad_wo,
            grad_bo,
            grad_g1,
            grad_n1,
            grad_w1,
            grad_b1,
            grad_w2,
            grad_b2,
            grad_g2,
            grad_n2,
        )

    return body


def solution(mesh):
    n_head, n_blk = mesh.shape["head"], mesh.shape["blk"]
    head_bits = tuple(f"h{i}" for i in range(n_head.bit_length() - 1))
    blk_bits = tuple(f"b{i}" for i in range(n_blk.bit_length() - 1))
    fine = Mesh(
        mesh.devices.reshape((2,) * len(head_bits + blk_bits)), head_bits + blk_bits
    )
    by_token = P(blk_bits + head_bits, None)
    by_row, by_entry = P(head_bits + blk_bits, None), P(head_bits + blk_bits)
    placed = (
        by_token,
        P(),
        by_token,
        by_row,
        by_row,
        by_row,
        by_entry,
        by_entry,
        by_row,
        by_entry,
        by_entry,
        by_entry,
        by_row,
        by_entry,
        by_row,
        by_entry,
        by_entry,
        by_entry,
    )
    given = (
        by_token,
        by_token,
        by_row,
        by_row,
        by_row,
        by_entry,
        by_entry,
        by_row,
        by_entry,
        by_entry,
        by_entry,
        by_row,
        by_entry,
        by_row,
        by_entry,
        by_entry,
        by_entry,
    )
    return jax.shard_map(
        make_body(head_bits, blk_bits),
        mesh=fine,
        in_specs=placed,
        out_specs=given,
        check_vma=False,
    )
```

```python
import functools

import jax
import jax.numpy as jnp
from jax import lax
from jax.experimental import pallas as pl
from jax.experimental.pallas import tpu as pltpu
from jax.sharding import Mesh, PartitionSpec as P

H = 16
HD = 64
DOCS = 24
EPS = 1e-05
NEG = -1e30
LANE = 128
TQ = 256
KB = 512
KB_LOG = KB.bit_length() - 1

BF = jnp.bfloat16
F32 = jnp.float32


def swap(value, axis):
    return lax.ppermute(value, axis, [(0, 1), (1, 0)])


def pick(value, index, axis):
    return lax.dynamic_index_in_dim(
        value, index, axis, keepdims=False, allow_negative_indices=False
    )


def placed_at(value, other, place, axis):
    value, other = jnp.expand_dims(value, axis), jnp.expand_dims(other, axis)
    twice = jnp.broadcast_to(
        value, value.shape[:axis] + (2,) + value.shape[axis + 1 :]
    )
    return lax.dynamic_update_slice_in_dim(
        twice, other, 1 - place, axis, allow_negative_indices=False
    )


def after(value, *others):
    return lax.optimization_barrier((value,) + others)[0]


def together(*values):
    return lax.optimization_barrier(values)


def with_other(value, axis, gate=None):
    sent = value if gate is None else after(value, gate)
    return jnp.concatenate([sent, swap(sent, axis)])


def left_product(former, latter):
    return lax.dot_general(
        former, latter, (((0,), (0,)), ((), ())), preferred_element_type=F32
    )


def right_product(former, latter):
    return lax.dot_general(
        former, latter, (((1,), (1,)), ((), ())), preferred_element_type=F32
    )


def product(former, latter):
    return jnp.dot(former, latter, preferred_element_type=F32)


def norm_parts(hidden):
    centre = hidden - jnp.mean(hidden, axis=-1, keepdims=True)
    rstd = lax.rsqrt(jnp.mean(centre * centre, axis=-1, keepdims=True) + EPS)
    return centre * rstd, rstd


def norm_back(unit, rstd, gain, grad):
    inner = grad * gain
    return rstd * (
        inner
        - jnp.mean(inner, axis=-1, keepdims=True)
        - unit * jnp.mean(inner * unit, axis=-1, keepdims=True)
    )


def same_doc(low_ref, high_ref, first, heads):
    row = lax.broadcasted_iota(jnp.int32, (KB, TQ), 0)
    place = first + row + (row >> 7) * (LANE * (heads - 1))
    return jnp.logical_and(place >= low_ref[...], place < high_ref[...])


def over_groups(tab, blocks, step, state):
    tile, tiles = pl.program_id(0), pl.num_programs(0)
    start, stop, inner, outer = (
        tab[2 * blocks + i * tiles + tile] for i in range(4)
    )
    state = lax.fori_loop(start, inner, functools.partial(step, True), state)
    state = lax.fori_loop(inner, outer, functools.partial(step, False), state)
    return lax.fori_loop(outer, stop, functools.partial(step, True), state)


def attend_kernel(blocks, heads, turns, first, last, tab, *refs):
    q0, q1, q2, q3, kv_a, kv_b, low, high = refs[:8]
    refs = refs[8:]
    if not first:
        (top_in, total_in, mixed_in), refs = refs[:3], refs[3:]
    kv, kvt = refs[:2]
    made, (acc, raw) = refs[2:5], refs[5:]
    tile, tiles = pl.program_id(0), pl.num_programs(0)
    head = tab[2 * blocks + 4 * tiles]
    start = tab[2 * blocks + tile]
    stop = tab[2 * blocks + tiles + tile]

    @pl.when(tile == 0)
    def _():
        for n in range(len(turns)):

            def place(i, carry):
                halves = []
                for j in range(4):
                    halves.append(kv_a[n * blocks + tab[4 * i + j]])
                    halves.append(kv_b[n * blocks + tab[blocks + 4 * i + j]])
                block = jnp.concatenate(halves, axis=0)
                at = (n * blocks + i * 4) * LANE
                at = pl.ds(pl.multiple_of(at, 4 * LANE), 4 * LANE)
                kv[at, :] = block
                kvt[:, at] = block.T
                return carry

            lax.fori_loop(0, blocks // 4, place, 0)

    query = jnp.concatenate([q0[...], q1[...], q2[...], q3[...]], axis=0)
    query_t = query.T
    if first:
        acc[...] = jnp.zeros_like(acc)
        state = (jnp.full((1, TQ), NEG, F32), jnp.zeros((1, TQ), F32))
    else:
        acc[...] = jnp.concatenate([jnp.zeros((HD, TQ), F32), mixed_in[...]], axis=0)
        state = (top_in[...], total_in[...])
    for n, turn in enumerate(turns):
        base = n * blocks * LANE
        parity = lax.bitwise_xor(head, turn) * LANE

        def ahead(j):
            at = pl.multiple_of(base + lax.min(j, stop - 1) * KB, KB)
            raw[lax.bitwise_and(j, 1)] = product(kv[pl.ds(at, KB), :], query_t)

        def step(masked, j, carry):
            top, total = carry
            scores = raw[lax.bitwise_and(j, 1)]
            ahead(j + 1)
            if masked:
                inside = same_doc(low, high, j * (KB * heads) + parity, heads)
                scores = jnp.where(inside, scores, NEG)
            new_top = jnp.maximum(top, jnp.max(scores, axis=0, keepdims=True))
            factor = jnp.exp(top - new_top)
            expo = jnp.exp(scores - new_top)
            total = total * factor + jnp.sum(expo, axis=0, keepdims=True)
            at = pl.ds(pl.multiple_of(base + j * KB, KB), KB)
            acc[...] = acc[...] * factor + product(kvt[:, at], expo.astype(BF))
            return new_top, total

        ahead(start)
        state = over_groups(tab, blocks, step, state)
    top, total = state
    if last:
        ctx, out, lse = made
        mixed = acc[HD:, :] / total
        lse[...] = top + jnp.log(total)
        for half in range(2):
            part = mixed[:, half * LANE : (half + 1) * LANE]
            out[half] = part
            ctx[half] = part.astype(BF)
    else:
        made[0][...], made[1][...], made[2][...] = top, total, acc[HD:, :]


def attend_back_kernel(blocks, heads, turns, first, tab, *refs):
    q0, q1, q2, q3, kv, kvt, low, high, lse, out, grad = refs[:11]
    refs = refs[11:]
    if not first:
        part_in, refs = refs[0], refs[1:]
    grad_q, grad_kv, acc, acc_kv = refs
    tile, tiles = pl.program_id(0), pl.num_programs(0)
    head = tab[2 * blocks + 4 * tiles]

    @pl.when(tile == 0)
    def _():
        def clear(j, carry):
            acc_kv[pl.ds(pl.multiple_of(j * KB, KB), KB), :] = jnp.zeros((KB, LANE), F32)
            return carry

        lax.fori_loop(0, len(turns) * blocks * LANE // KB, clear, 0)

    query = jnp.concatenate([q0[...], q1[...], q2[...], q3[...]], axis=0)
    query_t = query.T
    grad_t = jnp.concatenate([grad[0], grad[1]], axis=1).astype(F32)
    out_t = jnp.concatenate([out[0], out[1]], axis=1)
    delta = jnp.sum(grad_t * out_t, axis=0, keepdims=True)
    grad_pad = jnp.concatenate([jnp.zeros((HD, TQ), F32), grad_t], axis=0).astype(BF)
    grad_row = grad_pad.T
    log_sum = lse[...]
    acc[...] = jnp.zeros_like(acc)
    for n, turn in enumerate(turns):
        base = n * blocks * LANE
        parity = lax.bitwise_xor(head, turn) * LANE

        def step(masked, j, carry):
            at = pl.ds(pl.multiple_of(base + j * KB, KB), KB)
            keys = kv[at, :]
            scores = product(keys, query_t)
            if masked:
                inside = same_doc(low, high, j * (KB * heads) + parity, heads)
                scores = jnp.where(inside, scores, NEG)
            prob = jnp.exp(scores - log_sum)
            grad_prob = product(keys, grad_pad)
            grad_score = (prob * (grad_prob - delta)).astype(BF)
            acc_kv[at, :] += product(grad_score, query) + product(prob.astype(BF), grad_row)
            acc[...] += product(kvt[:, at], grad_score)
            return carry

        over_groups(tab, blocks, step, 0)
    if first:
        grad_q[...] = acc[:HD, :]
    else:
        result = ((acc[:HD, :] + part_in[...]) * (HD**-0.5)).astype(BF)
        grad_q[0] = result[:, :LANE]
        grad_q[1] = result[:, LANE:]

    @pl.when(tile == tiles - 1)
    def _():
        def write(b, carry):
            block = acc_kv[pl.ds(pl.multiple_of(b * LANE, LANE), LANE), :]
            grad_kv[b] = block.astype(grad_kv.dtype).T
            return carry

        lax.fori_loop(0, len(turns) * blocks, write, 0, unroll=4)


def whole_spec(shape):
    return pl.BlockSpec(shape, lambda t, tab: (0,) * len(shape))


def tile_specs(blocks):
    def half(at):
        return pl.BlockSpec((None, LANE // 2, LANE), lambda t, tab: (tab[at(t)], 0, 0))

    return (
        [
            half(lambda t: 2 * t),
            half(lambda t: blocks + 2 * t),
            half(lambda t: 2 * t + 1),
            half(lambda t: blocks + 2 * t + 1),
        ],
        pl.BlockSpec((None, 1, TQ), lambda t, tab: (t, 0, 0)),
        pl.BlockSpec((2, HD, LANE), lambda t, tab: (t, 0, 0)),
        pl.BlockSpec((None, HD, TQ), lambda t, tab: (t, 0, 0)),
    )


def attend(tab, heads, turns, query, kv_rel, low, high, state, last):
    blocks, nb = query[0].shape[0], kv_rel[0].shape[0]
    tiles, total = blocks // 2, nb * LANE
    halves, row, pair, tall = tile_specs(blocks)
    row_shape = jax.ShapeDtypeStruct((tiles, 1, TQ), F32)
    tall_shape = jax.ShapeDtypeStruct((tiles, HD, TQ), F32)
    if last:
        made = (
            jax.ShapeDtypeStruct((blocks, HD, LANE), BF),
            jax.ShapeDtypeStruct((blocks, HD, LANE), F32),
            row_shape,
        )
    return pl.pallas_call(
        functools.partial(attend_kernel, blocks, heads, turns, not state, last),
        out_shape=(
            jax.ShapeDtypeStruct((total, LANE), BF),
            jax.ShapeDtypeStruct((LANE, total), BF),
        )
        + (made if last else (row_shape, row_shape, tall_shape)),
        grid_spec=pltpu.PrefetchScalarGridSpec(
            num_scalar_prefetch=1,
            grid=(tiles,),
            in_specs=halves
            + [whole_spec((nb, LANE // 2, LANE))] * 2
            + [row, row]
            + ([row, row, tall] if state else []),
            out_specs=[whole_spec((total, LANE)), whole_spec((LANE, total))]
            + ([pair, pair, row] if last else [row, row, tall]),
            scratch_shapes=[
                pltpu.VMEM((LANE, TQ), F32),
                pltpu.VMEM((2, KB, TQ), F32),
            ],
        ),
        compiler_params=pltpu.CompilerParams(vmem_limit_bytes=56 << 20),
        cost_estimate=pl.CostEstimate(
            flops=20 * 10**9, bytes_accessed=6 * 10**6, transcendentals=4 * 10**6
        ),
    )(
        tab,
        query[0],
        query[1],
        query[0],
        query[1],
        kv_rel[0],
        kv_rel[1],
        low,
        high,
        *state,
    )


def attend_back(tab, heads, turns, query, kv, kvt, low, high, lse, out, grad, part):
    blocks, total = query[0].shape[0], kv.shape[0]
    halves, row, pair, tall = tile_specs(blocks)
    first = part is None
    if first:
        q_shape = jax.ShapeDtypeStruct((blocks // 2, HD, TQ), F32)
    else:
        q_shape = jax.ShapeDtypeStruct((blocks, HD, LANE), BF)
    return pl.pallas_call(
        functools.partial(attend_back_kernel, blocks, heads, turns, first),
        out_shape=(
            q_shape,
            jax.ShapeDtypeStruct((total // LANE, LANE, LANE), BF if first else F32),
        ),
        grid_spec=pltpu.PrefetchScalarGridSpec(
            num_scalar_prefetch=1,
            grid=(blocks // 2,),
            in_specs=halves
            + [
                whole_spec((total, LANE)),
                whole_spec((LANE, total)),
                row,
                row,
                row,
                pair,
                pair,
            ]
            + ([] if first else [tall]),
            out_specs=[
                tall if first else pair,
                whole_spec((total // LANE, LANE, LANE)),
            ],
            scratch_shapes=[
                pltpu.VMEM((LANE, TQ), F32),
                pltpu.VMEM((total, LANE), F32),
            ],
        ),
        compiler_params=pltpu.CompilerParams(vmem_limit_bytes=60 << 20),
        cost_estimate=pl.CostEstimate(
            flops=30 * 10**9, bytes_accessed=10 * 10**6, transcendentals=4 * 10**6
        ),
    )(
        tab,
        query[0],
        query[1],
        query[0],
        query[1],
        kv,
        kvt,
        low,
        high,
        lse,
        out,
        grad,
        *(() if first else (part,)),
    )


def cols_kernel(parts, tab, *refs):
    halves, (grad, cols, acc) = refs[:8], refs[8:]
    step = pl.program_id(0)
    rows = jnp.concatenate([half[...] for half in halves], axis=0)
    wide = jnp.concatenate([grad[i] for i in range(4)], axis=1)
    term = product(wide, rows)

    @pl.when(step == 0)
    def _():
        acc[...] = term

    @pl.when(step > 0)
    def _():
        acc[...] += term

    @pl.when(step == pl.num_programs(0) - 1)
    def _():
        for p in range(parts):
            block = acc[p * HD : (p + 1) * HD, :].T
            if len(cols.shape) == 2:
                cols[:, p * HD : (p + 1) * HD] = block.astype(BF)
            else:
                halves = block.reshape(cols.shape[0], 2, 16, HD)
                cols[:, p * 16 : (p + 1) * 16, :] = jnp.concatenate(
                    [halves[:, 0], halves[:, 1]], axis=-1
                ).astype(BF)


def head_columns(tab, stream, grad, shape):
    blocks, deep, _ = grad.shape
    width = stream[0].shape[-1]

    def half(at):
        return pl.BlockSpec(
            (None, LANE // 2, width), lambda t, tab: (tab[at + 4 * t], 0, 0)
        )

    return pl.pallas_call(
        functools.partial(cols_kernel, deep // HD),
        out_shape=jax.ShapeDtypeStruct(shape, BF),
        grid_spec=pltpu.PrefetchScalarGridSpec(
            num_scalar_prefetch=1,
            grid=(blocks // 4,),
            in_specs=[half(i + blocks * j) for i in range(4) for j in range(2)]
            + [pl.BlockSpec((4, deep, LANE), lambda t, tab: (t, 0, 0))],
            out_specs=whole_spec(shape),
            scratch_shapes=[pltpu.VMEM((deep, width), F32)],
        ),
        compiler_params=pltpu.CompilerParams(vmem_limit_bytes=24 << 20),
        cost_estimate=pl.CostEstimate(
            flops=4 * 10**9, bytes_accessed=2 * stream[0].size * 2, transcendentals=0
        ),
    )(tab, *(stream * 4), grad)


def owner_kernel(got, mats, vec):
    rows = got.shape[1]
    low = lax.broadcasted_iota(jnp.int32, (16, LANE), 1) < HD
    total = jnp.zeros(vec.shape, F32)
    for n in range(got.shape[0]):
        total = total + got[n, 48:rows, :].astype(F32)
    vec[...] = total
    for p in range(3):
        for pair in range(H // 2):
            even, odd = jnp.zeros((16, LANE), F32), jnp.zeros((16, LANE), F32)
            for base in range(0, got.shape[0], H):
                even = even + got[base + 2 * pair, p * 16 : (p + 1) * 16, :].astype(F32)
                odd = odd + got[base + 2 * pair + 1, p * 16 : (p + 1) * 16, :].astype(F32)
            at = slice(pair * LANE, (pair + 1) * LANE)
            mats[p, :16, at] = jnp.where(low, even, pltpu.roll(odd, HD, 1))
            mats[p, 16:, at] = jnp.where(low, pltpu.roll(even, HD, 1), odd)


def owner_sums(got, width):
    return pl.pallas_call(
        owner_kernel,
        out_shape=(
            jax.ShapeDtypeStruct((3, 32, width), F32),
            jax.ShapeDtypeStruct((got.shape[1] - 48, LANE), F32),
        ),
        compiler_params=pltpu.CompilerParams(vmem_limit_bytes=16 << 20),
        cost_estimate=pl.CostEstimate(
            flops=got.size, bytes_accessed=got.size * 2 + width * 400, transcendentals=0
        ),
    )(got)


def as_rows(vectors):
    return jnp.stack(
        [jnp.pad(v, ((0, 0), (0, LANE - v.shape[1]))) for v in vectors], axis=1
    )


def make_body(head_bits, blk_bits):
    n_head, n_blk = 1 << len(head_bits), 1 << len(blk_bits)
    n_all = n_head * n_blk
    every = head_bits + blk_bits
    z_bits, x_bit, c_bit = blk_bits[:-2], blk_bits[-2], blk_bits[-1]
    outer = head_bits + z_bits
    repl = n_blk // H
    part = HD // repl
    n_out, n_head_z = 1 << len(outer), len(outer)

    def body(
        tokens,
        segments,
        cotangent,
        w_query,
        w_key,
        w_value,
        b_query,
        b_value,
        w_output,
        b_output,
        gain_attn,
        shift_attn,
        w_inner,
        b_inner,
        w_outer,
        b_outer,
        gain_ffn,
        shift_ffn,
    ):
        rows, width = tokens.shape
        rw = w_query.shape[0]
        ffl = w_outer.shape[0]
        my = {bit: lax.axis_index(bit) for bit in every}
        hi, bi = lax.axis_index(head_bits), lax.axis_index(blk_bits)
        head = bi if repl == 1 else lax.div(bi, repl)
        sub = bi - head * repl

        def both(value, bit, axis, then=None):
            other = swap(value, bit)
            if then is not None:
                other = after(other, then)
            return placed_at(value, other, my[bit], axis)

        def summed(value, bit, axis, then=None):
            other = swap(pick(value, 1 - my[bit], axis).astype(BF), bit)
            if then is not None:
                other = after(other, then)
            return pick(value, my[bit], axis).astype(F32) + other.astype(F32)

        def traded(value, bits, thens=(None, None)):
            for axis, bit in enumerate(bits):
                other = swap(pick(value, 1 - my[bit], axis), bit)
                if thens[axis] is not None:
                    other = after(other, thens[axis])
                kept = pick(value, my[bit], axis)
                value = placed_at(kept, other, my[bit], axis)
            return value

        def over(value, bits, at, thens):
            for i, bit in enumerate(bits):
                value = both(value, bit, at + i, thens[i])
            return value

        def group_gather(part_rows):
            return with_other(with_other(part_rows, x_bit), c_bit)

        def group_scatter(partial):
            part_rows = partial.reshape(2, 2, rows, width)
            mine = part_rows[0] + swap(part_rows[1].astype(BF), c_bit).astype(F32)
            return mine[0] + swap(mine[1].astype(BF), x_bit).astype(F32)

        ways = (z_bits + (x_bit,), (x_bit,) + z_bits)
        flows = [tokens[: rows // 2], tokens[rows // 2 :]]
        hops = [[flow] for flow in flows]
        for i in range(len(ways[0])):
            for flow, way in zip(hops, ways, strict=True):
                flow.append(with_other(flow[-1], way[i]))

        small = as_rows(
            [
                v[None]
                for v in (
                    b_query,
                    b_value,
                    b_output,
                    gain_attn,
                    shift_attn,
                    b_outer,
                    gain_ffn,
                    shift_ffn,
                    b_inner,
                )
            ]
        )
        scale = HD**-0.5
        cut_q, cut_k, cut_v = (
            w.reshape(rw, H, HD) for w in (w_query * BF(scale), w_key, w_value)
        )
        cols = jnp.concatenate(
            [
                jnp.concatenate([cut_k, cut_v], axis=2),
                jnp.concatenate([cut_q, jnp.zeros_like(cut_q)], axis=2),
            ]
        )
        cols = jnp.transpose(cols, (1, 0, 2))[:, None]
        cols = jnp.broadcast_to(cols, (H, repl, 2 * rw, LANE))
        smalls = jnp.broadcast_to(small, (n_blk,) + small.shape[1:])
        cols_all = jnp.concatenate([cols.reshape(n_blk, 2 * rw, LANE), smalls], axis=1)
        got = lax.all_to_all(after(cols_all, hops[1][1]), blk_bits, 0, 0, tiled=True)
        for i, bit in enumerate(head_bits):
            got = both(got, bit, i, hops[1][-1])
        got = got.reshape((n_all,) + got.shape[len(head_bits) + 1 :])

        stream = [with_other(flow[-1], c_bit, got) for flow in hops]
        w_kv = got[:, :rw].reshape(width, LANE)
        w_q = got[:, rw : 2 * rw].reshape(width, LANE)
        vecs = got[:, 2 * rw :].astype(F32)
        named = [vecs[:, i, :rw].reshape(width) for i in range(8)]
        full_bq, full_bv, full_bo, full_g1, full_n1, full_b2, full_g2, full_n2 = named
        full_b1 = vecs[:, 8, :ffl].reshape(n_out, 4, ffl)
        b1_mine = pick(full_b1, my[x_bit] * 2 + my[c_bit], 1).reshape(n_out * ffl)

        n_z = len(z_bits)
        wo_row = over(w_output, z_bits, 0, hops[0][1 : 1 + n_z])
        wo_row = over(wo_row, head_bits, 0, [None] * (len(head_bits) - 1) + [hops[0][-1]])
        w1_cut = jnp.transpose(w_inner.reshape(rw, n_out, 2, 2, ffl), (2, 3, 0, 1, 4))
        w1_cut = traded(
            w1_cut.reshape(2, 2, rw, n_out * ffl), (x_bit, c_bit), hops[0][1:3]
        ).reshape(4 * rw, n_out * ffl)
        w_pair = after(jnp.concatenate([w1_cut, w_outer]), hops[1][2])
        w_pair = lax.all_gather(w_pair, outer)
        w1_mine = w_pair[:, : 4 * rw].reshape(width, n_out * ffl)
        w2_mine = w_pair[:, 4 * rw :].reshape(n_out * ffl, width)

        spot = jnp.arange(n_blk)

        def slots(way):
            apart = spot ^ bi
            total = 0
            for i, bit in enumerate(way + (c_bit,)):
                total = total + (((apart >> (len(blk_bits) - 1 - blk_bits.index(bit))) & 1) << i)
            return total

        slot = [slots(way) for way in ways]
        ids = jnp.arange(DOCS)[:, None]
        below = jnp.sum((segments[None] < ids).astype(jnp.int32), axis=1)
        upto = jnp.sum((segments[None] <= ids).astype(jnp.int32), axis=1)
        own_segs = pick(segments.reshape(n_blk, n_head, LANE), hi, 1).reshape(
            n_blk // 2, 1, TQ
        )
        member = own_segs[None] == ids[:, :, None, None]
        low = jnp.sum(jnp.where(member, below[:, None, None, None], 0), axis=0)
        high = jnp.sum(jnp.where(member, upto[:, None, None, None], 0), axis=0)
        far = KB_LOG + len(head_bits)
        start = low[:, 0, 0] >> far
        stop = (high[:, 0, -1] + ((1 << far) - 1)) >> far
        inner = (jnp.max(low, axis=(1, 2)) + ((1 << far) - 1)) >> far
        inner = jnp.clip(inner, start, stop)
        outer_end = jnp.clip(jnp.min(high, axis=(1, 2)) >> far, inner, stop)
        tab = jnp.concatenate(slot + [start, stop, inner, outer_end, hi[None]])
        tab = tab.astype(jnp.int32)

        bias = jnp.concatenate(
            [
                pick(full_bq.reshape(H, HD), head, 0) * scale,
                jnp.zeros((HD,), F32),
                jnp.zeros((HD,), F32),
                pick(full_bv.reshape(H, HD), head, 0),
            ]
        )
        kv_rel, query = [], []
        w_all = jnp.concatenate([w_q, w_kv], axis=1)
        for flow in stream:
            both_own = (product(flow, w_all) + bias).astype(BF)
            kv_rel.append(both_own[:, LANE:].reshape(n_blk, rows // 2, LANE))
            query.append(both_own[:, :LANE].reshape(n_blk, rows // 2, LANE))
        kv_pair = kv_near = jnp.concatenate(kv_rel, axis=1)
        wo_row = both(wo_row, x_bit, n_head_z, kv_near)
        w_line = jnp.concatenate([w_q[:, :HD] * BF(1.0 / scale), w_kv], axis=1).T
        if repl > 1:
            w_line = lax.dynamic_slice_in_dim(
                w_line.reshape(3, HD, width), sub * part, part, axis=1
            ).reshape(3 * part, width)
        group_other = swap(after(w_line, kv_near), x_bit)
        for bit in head_bits[::-1]:
            kv_pair = with_other(kv_pair, bit) if n_head > 2 else swap(kv_pair, bit)
        kv_far = kv_pair[n_blk:] if n_head > 2 else kv_pair
        kv_far = [kv_far[:, : rows // 2], kv_far[:, rows // 2 :]]
        near_turn, far_turns = (0,), tuple(range(1, n_head))
        kv, kvt, *state = attend(
            tab, n_head, near_turn, query, kv_rel, low, high, (), False
        )
        kv_two, kvt_two, ctx, out, lse = attend(
            tab, n_head, far_turns, query, kv_far, low, high, state, True
        )
        ctx = after(ctx, group_other)
        if repl > 1:
            ctx = lax.dynamic_slice_in_dim(ctx, sub * part, part, axis=1)
        ctx_t = lax.all_to_all(ctx, blk_bits, 0, 0, tiled=True).reshape(width, rows)

        full_wo = both(wo_row, c_bit, n_head_z + 1, ctx_t).reshape(width, width)

        w_line = placed_at(w_line, after(group_other, ctx), my[x_bit], 0)
        ctx_t = after(ctx_t, w_line)

        inputs = tokens.astype(F32)
        unit_one, rstd_one = norm_parts(inputs + left_product(ctx_t, full_wo) + full_bo)
        norm_one = unit_one * full_g1 + full_n1
        low_one = norm_one.astype(BF)

        near = with_other(low_one, x_bit)
        near, w1_mine, w2_mine = together(near, w1_mine, w2_mine)
        inner_in = with_other(near, c_bit)
        pre = product(inner_in, w1_mine) + b1_mine
        phi = 0.5 * (1.0 + lax.erf(pre * (0.5**0.5)))
        act = (pre * phi).astype(BF)
        slope = phi + pre * (jnp.exp(-0.5 * pre * pre) * ((2 * jnp.pi) ** -0.5))
        unit_two, rstd_two = norm_parts(
            norm_one + group_scatter(product(act, w2_mine)) + full_b2
        )
        out_rows = (unit_two * full_g2 + full_n2).astype(BF)

        up = cotangent.astype(F32)
        grad_n2 = jnp.sum(up, axis=0)
        grad_g2 = jnp.sum(up * unit_two, axis=0)
        grad_two = norm_back(unit_two, rstd_two, full_g2, up)
        dz = grad_two.astype(BF)
        grad_b2 = jnp.sum(dz.astype(F32), axis=0)
        dz_all = group_gather(dz)
        grad_pre = (slope * right_product(dz_all, w2_mine)).astype(BF)
        grad_b1 = jnp.sum(grad_pre.astype(F32), axis=0).reshape(n_out, 1, ffl)

        grad_w2 = left_product(act, dz_all).astype(BF).reshape(n_out, ffl, width)
        grad_w1 = left_product(inner_in, grad_pre).astype(BF).reshape(n_out, 4 * rw, width)
        grads = jnp.concatenate([grad_w1, grad_w2], axis=1)
        grads = grads.reshape(n_head, n_out // n_head, 4 * rw + ffl, width)
        grads = jnp.swapaxes(grads, 0, 1)
        grad_norm = right_product(grad_pre, w1_mine)
        grad_norm = grad_two + group_scatter(grad_norm)
        grads = lax.psum_scatter(grads, z_bits, scatter_dimension=0)
        grads = grads.reshape((2,) * len(head_bits) + (4 * rw + ffl, width))

        grad_n1 = jnp.sum(grad_norm, axis=0)
        grad_g1 = jnp.sum(grad_norm * unit_one, axis=0)
        grad_one = norm_back(unit_one, rstd_one, full_g1, grad_norm)
        da = grad_one.astype(BF)
        grad_bo = jnp.sum(da.astype(F32), axis=0)
        grad_ctx = right_product(full_wo, da).astype(BF).reshape(H, 1, HD, rows)
        grad_ctx = jnp.broadcast_to(grad_ctx, (H, repl, HD, rows)).reshape(n_blk, HD, rows)
        grad_heads = lax.all_to_all(grad_ctx, blk_bits, 0, 0, tiled=True)

        later = after(da, grad_ctx)

        by_core = ctx_t.reshape(n_all // 2, 2, rw, rows)

        def core_half(core):
            return product(pick(by_core, core, 1).reshape(width // 2, rows), later)

        wo_other = swap(core_half(1 - my[c_bit]).astype(BF), c_bit)
        grad_wo = core_half(my[c_bit]) + after(wo_other, grad_ctx).astype(F32)
        grad_wo = grad_wo.reshape((2,) * (len(every) - 1) + (rw, width))
        w_line = both(w_line, c_bit, 0, grad_ctx)
        grad_heads = after(grad_heads, grad_wo, w_line)
        w_line = w_line.reshape(4 * 3 * part, width)
        wo_at = len(every) - 2
        wo_other = swap(pick(grad_wo, 1 - my[x_bit], wo_at).astype(BF), x_bit)

        part_q, others = attend_back(
            tab,
            n_head,
            far_turns,
            query,
            kv_two,
            kvt_two,
            low,
            high,
            lse,
            out,
            grad_heads,
            None,
        )
        others = others.reshape(n_head - 1, n_blk, LANE, LANE)
        part_q, wo_other = together(part_q, wo_other)
        grad_q, grad_kv = attend_back(
            tab, n_head, near_turn, query, kv, kvt, low, high, lse, out, grad_heads, part_q
        )
        terms = [grad_kv] + [others[k] for k in range(n_head - 1)]
        for i, bit in list(enumerate(head_bits[::-1]))[::-1]:
            terms = [
                terms[k].astype(F32) + swap(terms[k + (1 << i)].astype(BF), bit).astype(F32)
                for k in range(1 << i)
            ]
        grad_kv = terms[0].astype(BF)
        grad_wo = pick(grad_wo, my[x_bit], wo_at) + wo_other.astype(F32)

        def own_part(grad, count):
            grad = grad.reshape(n_blk, count, HD, LANE)
            if repl > 1:
                grad = lax.dynamic_slice_in_dim(grad, sub * part, part, axis=2)
            return grad.reshape(n_blk, count * part, LANE)

        def line_rows(grad, count):
            sent = own_part(grad, count).reshape(n_blk // 4, 2, 2, count * part, rows)
            sent = jnp.transpose(sent, (2, 1, 0, 3, 4)).reshape(
                4, n_blk // 4, count * part, rows
            )
            return lax.all_to_all(sent, (c_bit, x_bit), 0, 0, tiled=True)

        def line_product(weights, came):
            came = jnp.transpose(came, (0, 2, 1, 3)).reshape(12 * part, n_blk // 4 * rows)
            return left_product(came, weights)

        grad_qkv = jnp.concatenate([grad_q, grad_kv], axis=1)
        line_kv = line_rows(grad_qkv, 3)
        for bit in head_bits:
            grad_wo = summed(grad_wo, bit, 0, grad_kv)
        wo_half = grad_wo

        grad_in = line_product(w_line, line_kv)

        packed = rw == 32 and repl == 1
        shape = (n_all, 48, LANE) if packed else (width, 3 * HD)
        halves = tuple(flow.reshape(n_blk, rows // 2, width) for flow in stream)
        cut = head_columns(tab, halves, grad_qkv, shape)
        if not packed:
            cut = cut.reshape(width, 3, HD)
            if repl > 1:
                cut = lax.dynamic_slice_in_dim(cut, sub * part, part, axis=2)
            cut = cut.reshape(n_all, rw * 3 * part // LANE, LANE)
        own = (jnp.arange(H) == head).astype(F32)[:, None]
        if repl > 1:
            own = own * (sub == 0).astype(F32)
        bias_rows = jnp.sum(grad_qkv.astype(F32), axis=(0, 2))
        grad_bq = (own * bias_rows[None, :HD]).reshape(width)
        grad_bv = (own * bias_rows[None, 2 * HD :]).reshape(width)
        mark = (jnp.arange(4) == my[x_bit] * 2 + my[c_bit]).astype(F32)[None, :, None]
        b1_abs = (grad_b1 * mark).reshape(n_all, ffl)
        smalls = jnp.stack(
            [
                grad_bq,
                grad_bv,
                *after((grad_bo, grad_g1, grad_n1, grad_b2, grad_g2, grad_n2), grad_q),
            ]
        ).reshape(8, width // LANE, 1, LANE)
        share = LANE // rw
        smalls = jnp.swapaxes(smalls, 0, 1).reshape(width // LANE, 1, 8, LANE)
        smalls = jnp.broadcast_to(smalls, (width // LANE, share, 8, LANE))
        smalls = jnp.concatenate(
            [smalls.reshape(n_all, 8, LANE), as_rows([b1_abs])], axis=1
        )
        cut = jnp.concatenate([cut, smalls.astype(BF)], axis=1)
        n_cut = cut.shape[1]
        cut = cut.reshape((2,) * len(head_bits) + (n_blk, n_cut, LANE))
        for bit in head_bits:
            cut = summed(cut, bit, 0, grad_in)
        sent = cut.astype(BF)
        got = lax.all_to_all(sent, blk_bits, 0, 0, tiled=True)
        grads = after(grads, grad_in)
        for bit in head_bits[1:]:
            grads = summed(grads, bit, 1)
        other = swap(pick(grads, 1 - my[head_bits[0]], 0).astype(BF), head_bits[0])
        grad_in = grad_in.reshape((2,) * n_z + (rows, width))
        for i in range(1, n_z)[::-1]:
            grad_in = summed(grad_in, z_bits[i], i)
        grad_wo = after(wo_half, line_kv)
        for bit in z_bits[:1]:
            grad_wo = summed(grad_wo, bit, 0, grad_in)
        for bit in z_bits[1:]:
            grad_wo = summed(grad_wo, bit, 0)
        grad_in = summed(grad_in, z_bits[0], 0)
        grads = pick(grads, my[head_bits[0]], 0).astype(F32) + other.astype(F32)
        grad_w2 = grads[4 * rw :]
        first = grads[: 4 * rw].astype(BF).reshape(2, 2, rw, n_out * ffl)
        first_other = swap(pick(first, 1 - my[x_bit], 0), x_bit)
        grad_w1 = placed_at(pick(first, my[x_bit], 0), first_other, my[x_bit], 0)
        grad_w1 = after(grad_w1, grad_in)
        came = swap(pick(grad_w1, 1 - my[c_bit], 1), c_bit)
        grad_w1 = placed_at(pick(grad_w1, my[c_bit], 1), came, my[c_bit], 1)
        grad_tokens = grad_one + grad_in
        grad_w1 = (
            jnp.transpose(grad_w1.reshape(4, rw, n_out, ffl), (1, 2, 0, 3))
            .reshape(rw, n_all * ffl)
            .astype(F32)
        )
        if packed:
            mats, vecs = owner_sums(got, width)
        else:
            got = got.astype(F32)
            mats = got[:, : n_cut - 9].reshape(H, repl, rw, 3, part)
            mats = jnp.transpose(mats, (3, 2, 0, 1, 4)).reshape(3, rw, width)
            vecs = jnp.sum(got[:, n_cut - 9 :], axis=0)
        lane = ((hi * n_blk + bi) & (share - 1)) * rw
        own_vecs = lax.dynamic_slice_in_dim(
            vecs[:8], lane, rw, 1, allow_negative_indices=False
        )
        grad_bq, grad_bv, grad_bo, grad_g1, grad_n1, grad_b2, grad_g2, grad_n2 = (
            own_vecs[i] for i in range(8)
        )
        grad_b1 = vecs[8, :ffl]
        return (
            out_rows,
            grad_tokens,
            mats[0],
            mats[1],
            mats[2],
            grad_bq,
            grad_bv,
            grad_wo,
            grad_bo,
            grad_g1,
            grad_n1,
            grad_w1,
            grad_b1,
            grad_w2,
            grad_b2,
            grad_g2,
            grad_n2,
        )

    return body


def solution(mesh):
    n_head, n_blk = mesh.shape["head"], mesh.shape["blk"]
    head_bits = tuple(f"h{i}" for i in range(n_head.bit_length() - 1))
    blk_bits = tuple(f"b{i}" for i in range(n_blk.bit_length() - 1))
    fine = Mesh(
        mesh.devices.reshape((2,) * len(head_bits + blk_bits)), head_bits + blk_bits
    )
    by_token = P(blk_bits + head_bits, None)
    by_row, by_entry = P(head_bits + blk_bits, None), P(head_bits + blk_bits)
    placed = (
        by_token,
        P(),
        by_token,
        by_row,
        by_row,
        by_row,
        by_entry,
        by_entry,
        by_row,
        by_entry,
        by_entry,
        by_entry,
        by_row,
        by_entry,
        by_row,
        by_entry,
        by_entry,
        by_entry,
    )
    given = (
        by_token,
        by_token,
        by_row,
        by_row,
        by_row,
        by_entry,
        by_entry,
        by_row,
        by_entry,
        by_entry,
        by_entry,
        by_row,
        by_entry,
        by_row,
        by_entry,
        by_entry,
        by_entry,
    )
    return jax.shard_map(
        make_body(head_bits, blk_bits),
        mesh=fine,
        in_specs=placed,
        out_specs=given,
        check_vma=False,
    )
```

```python
import functools

import jax
import jax.numpy as jnp
from jax import lax
from jax.experimental import pallas as pl
from jax.experimental.pallas import tpu as pltpu
from jax.sharding import Mesh, PartitionSpec as P

H = 16
HD = 64
DOCS = 24
EPS = 1e-05
NEG = -1e30
LANE = 128
TQ = 256
KB = 512
KB_LOG = KB.bit_length() - 1

BF = jnp.bfloat16
F32 = jnp.float32


def swap(value, axis):
    return lax.ppermute(value, axis, [(0, 1), (1, 0)])


def pick(value, index, axis):
    return lax.dynamic_index_in_dim(
        value, index, axis, keepdims=False, allow_negative_indices=False
    )


def placed_at(value, other, place, axis):
    value, other = jnp.expand_dims(value, axis), jnp.expand_dims(other, axis)
    twice = jnp.broadcast_to(
        value, value.shape[:axis] + (2,) + value.shape[axis + 1 :]
    )
    return lax.dynamic_update_slice_in_dim(
        twice, other, 1 - place, axis, allow_negative_indices=False
    )


def after(value, *others):
    return lax.optimization_barrier((value,) + others)[0]


def together(*values):
    return lax.optimization_barrier(values)


def with_other(value, axis, gate=None):
    sent = value if gate is None else after(value, gate)
    return jnp.concatenate([sent, swap(sent, axis)])


def left_product(former, latter):
    return lax.dot_general(
        former, latter, (((0,), (0,)), ((), ())), preferred_element_type=F32
    )


def right_product(former, latter):
    return lax.dot_general(
        former, latter, (((1,), (1,)), ((), ())), preferred_element_type=F32
    )


def product(former, latter):
    return jnp.dot(former, latter, preferred_element_type=F32)


def norm_parts(hidden):
    centre = hidden - jnp.mean(hidden, axis=-1, keepdims=True)
    rstd = lax.rsqrt(jnp.mean(centre * centre, axis=-1, keepdims=True) + EPS)
    return centre * rstd, rstd


def norm_back(unit, rstd, gain, grad):
    inner = grad * gain
    return rstd * (
        inner
        - jnp.mean(inner, axis=-1, keepdims=True)
        - unit * jnp.mean(inner * unit, axis=-1, keepdims=True)
    )


def same_doc(low_ref, high_ref, first, heads):
    row = lax.broadcasted_iota(jnp.int32, (KB, TQ), 0)
    place = first + row + (row >> 7) * (LANE * (heads - 1))
    return jnp.logical_and(place >= low_ref[...], place < high_ref[...])


def over_groups(tab, blocks, step, state):
    tile, tiles = pl.program_id(0), pl.num_programs(0)
    start, stop, inner, outer = (
        tab[2 * blocks + i * tiles + tile] for i in range(4)
    )
    state = lax.fori_loop(start, inner, functools.partial(step, True), state)
    state = lax.fori_loop(inner, outer, functools.partial(step, False), state)
    return lax.fori_loop(outer, stop, functools.partial(step, True), state)


def attend_kernel(blocks, heads, turns, first, last, tab, *refs):
    q0, q1, q2, q3, kv_a, kv_b, low, high = refs[:8]
    refs = refs[8:]
    if not first:
        (top_in, total_in, mixed_in), refs = refs[:3], refs[3:]
    kv, kvt = refs[:2]
    made, (acc, raw) = refs[2:5], refs[5:]
    tile, tiles = pl.program_id(0), pl.num_programs(0)
    head = tab[2 * blocks + 4 * tiles]
    start = tab[2 * blocks + tile]
    stop = tab[2 * blocks + tiles + tile]

    @pl.when(tile == 0)
    def _():
        for n in range(len(turns)):

            def place(i, carry):
                halves = []
                for j in range(4):
                    halves.append(kv_a[n * blocks + tab[4 * i + j]])
                    halves.append(kv_b[n * blocks + tab[blocks + 4 * i + j]])
                block = jnp.concatenate(halves, axis=0)
                at = (n * blocks + i * 4) * LANE
                at = pl.ds(pl.multiple_of(at, 4 * LANE), 4 * LANE)
                kv[at, :] = block
                kvt[:, at] = block.T
                return carry

            lax.fori_loop(0, blocks // 4, place, 0)

    query = jnp.concatenate([q0[...], q1[...], q2[...], q3[...]], axis=0)
    query_t = query.T
    if first:
        acc[...] = jnp.zeros_like(acc)
        state = (jnp.full((1, TQ), NEG, F32), jnp.zeros((1, TQ), F32))
    else:
        acc[...] = jnp.concatenate([jnp.zeros((HD, TQ), F32), mixed_in[...]], axis=0)
        state = (top_in[...], total_in[...])
    for n, turn in enumerate(turns):
        base = n * blocks * LANE
        parity = lax.bitwise_xor(head, turn) * LANE

        def ahead(j):
            at = pl.multiple_of(base + lax.min(j, stop - 1) * KB, KB)
            raw[lax.bitwise_and(j, 1)] = product(kv[pl.ds(at, KB), :], query_t)

        def step(masked, j, carry):
            top, total = carry
            scores = raw[lax.bitwise_and(j, 1)]
            ahead(j + 1)
            if masked:
                inside = same_doc(low, high, j * (KB * heads) + parity, heads)
                scores = jnp.where(inside, scores, NEG)
            new_top = jnp.maximum(top, jnp.max(scores, axis=0, keepdims=True))
            factor = jnp.exp(top - new_top)
            expo = jnp.exp(scores - new_top)
            total = total * factor + jnp.sum(expo, axis=0, keepdims=True)
            at = pl.ds(pl.multiple_of(base + j * KB, KB), KB)
            acc[...] = acc[...] * factor + product(kvt[:, at], expo.astype(BF))
            return new_top, total

        ahead(start)
        state = over_groups(tab, blocks, step, state)
    top, total = state
    if last:
        ctx, out, lse = made
        mixed = acc[HD:, :] / total
        lse[...] = top + jnp.log(total)
        for half in range(2):
            part = mixed[:, half * LANE : (half + 1) * LANE]
            out[half] = part
            ctx[half] = part.astype(BF)
    else:
        made[0][...], made[1][...], made[2][...] = top, total, acc[HD:, :]


def attend_back_kernel(blocks, heads, turns, first, tab, *refs):
    q0, q1, q2, q3, kv, kvt, low, high, lse, out, grad = refs[:11]
    refs = refs[11:]
    if not first:
        part_in, refs = refs[0], refs[1:]
    grad_q, grad_kv, acc, acc_kv = refs
    tile, tiles = pl.program_id(0), pl.num_programs(0)
    head = tab[2 * blocks + 4 * tiles]

    @pl.when(tile == 0)
    def _():
        def clear(j, carry):
            acc_kv[pl.ds(pl.multiple_of(j * KB, KB), KB), :] = jnp.zeros((KB, LANE), F32)
            return carry

        lax.fori_loop(0, len(turns) * blocks * LANE // KB, clear, 0)

    query = jnp.concatenate([q0[...], q1[...], q2[...], q3[...]], axis=0)
    query_t = query.T
    grad_t = jnp.concatenate([grad[0], grad[1]], axis=1).astype(F32)
    out_t = jnp.concatenate([out[0], out[1]], axis=1)
    delta = jnp.sum(grad_t * out_t, axis=0, keepdims=True)
    grad_pad = jnp.concatenate([jnp.zeros((HD, TQ), F32), grad_t], axis=0).astype(BF)
    grad_row = grad_pad.T
    log_sum = lse[...]
    acc[...] = jnp.zeros_like(acc)
    for n, turn in enumerate(turns):
        base = n * blocks * LANE
        parity = lax.bitwise_xor(head, turn) * LANE

        def step(masked, j, carry):
            at = pl.ds(pl.multiple_of(base + j * KB, KB), KB)
            keys = kv[at, :]
            scores = product(keys, query_t)
            if masked:
                inside = same_doc(low, high, j * (KB * heads) + parity, heads)
                scores = jnp.where(inside, scores, NEG)
            prob = jnp.exp(scores - log_sum)
            grad_prob = product(keys, grad_pad)
            grad_score = (prob * (grad_prob - delta)).astype(BF)
            acc_kv[at, :] += product(grad_score, query) + product(prob.astype(BF), grad_row)
            acc[...] += product(kvt[:, at], grad_score)
            return carry

        over_groups(tab, blocks, step, 0)
    if first:
        grad_q[...] = acc[:HD, :]
    else:
        result = ((acc[:HD, :] + part_in[...]) * (HD**-0.5)).astype(BF)
        grad_q[0] = result[:, :LANE]
        grad_q[1] = result[:, LANE:]

    @pl.when(tile == tiles - 1)
    def _():
        def write(b, carry):
            block = acc_kv[pl.ds(pl.multiple_of(b * LANE, LANE), LANE), :]
            grad_kv[b] = block.astype(grad_kv.dtype).T
            return carry

        lax.fori_loop(0, len(turns) * blocks, write, 0, unroll=4)


def whole_spec(shape):
    return pl.BlockSpec(shape, lambda t, tab: (0,) * len(shape))


def tile_specs(blocks):
    def half(at):
        return pl.BlockSpec((None, LANE // 2, LANE), lambda t, tab: (tab[at(t)], 0, 0))

    return (
        [
            half(lambda t: 2 * t),
            half(lambda t: blocks + 2 * t),
            half(lambda t: 2 * t + 1),
            half(lambda t: blocks + 2 * t + 1),
        ],
        pl.BlockSpec((None, 1, TQ), lambda t, tab: (t, 0, 0)),
        pl.BlockSpec((2, HD, LANE), lambda t, tab: (t, 0, 0)),
        pl.BlockSpec((None, HD, TQ), lambda t, tab: (t, 0, 0)),
    )


def attend(tab, heads, turns, query, kv_rel, low, high, state, last):
    blocks, nb = query[0].shape[0], kv_rel[0].shape[0]
    tiles, total = blocks // 2, nb * LANE
    halves, row, pair, tall = tile_specs(blocks)
    row_shape = jax.ShapeDtypeStruct((tiles, 1, TQ), F32)
    tall_shape = jax.ShapeDtypeStruct((tiles, HD, TQ), F32)
    if last:
        made = (
            jax.ShapeDtypeStruct((blocks, HD, LANE), BF),
            jax.ShapeDtypeStruct((blocks, HD, LANE), F32),
            row_shape,
        )
    return pl.pallas_call(
        functools.partial(attend_kernel, blocks, heads, turns, not state, last),
        out_shape=(
            jax.ShapeDtypeStruct((total, LANE), BF),
            jax.ShapeDtypeStruct((LANE, total), BF),
        )
        + (made if last else (row_shape, row_shape, tall_shape)),
        grid_spec=pltpu.PrefetchScalarGridSpec(
            num_scalar_prefetch=1,
            grid=(tiles,),
            in_specs=halves
            + [whole_spec((nb, LANE // 2, LANE))] * 2
            + [row, row]
            + ([row, row, tall] if state else []),
            out_specs=[whole_spec((total, LANE)), whole_spec((LANE, total))]
            + ([pair, pair, row] if last else [row, row, tall]),
            scratch_shapes=[
                pltpu.VMEM((LANE, TQ), F32),
                pltpu.VMEM((2, KB, TQ), F32),
            ],
        ),
        compiler_params=pltpu.CompilerParams(vmem_limit_bytes=56 << 20),
        cost_estimate=pl.CostEstimate(
            flops=20 * 10**9, bytes_accessed=6 * 10**6, transcendentals=4 * 10**6
        ),
    )(
        tab,
        query[0],
        query[1],
        query[0],
        query[1],
        kv_rel[0],
        kv_rel[1],
        low,
        high,
        *state,
    )


def attend_back(tab, heads, turns, query, kv, kvt, low, high, lse, out, grad, part):
    blocks, total = query[0].shape[0], kv.shape[0]
    halves, row, pair, tall = tile_specs(blocks)
    first = part is None
    if first:
        q_shape = jax.ShapeDtypeStruct((blocks // 2, HD, TQ), F32)
    else:
        q_shape = jax.ShapeDtypeStruct((blocks, HD, LANE), BF)
    return pl.pallas_call(
        functools.partial(attend_back_kernel, blocks, heads, turns, first),
        out_shape=(
            q_shape,
            jax.ShapeDtypeStruct((total // LANE, LANE, LANE), BF if first else F32),
        ),
        grid_spec=pltpu.PrefetchScalarGridSpec(
            num_scalar_prefetch=1,
            grid=(blocks // 2,),
            in_specs=halves
            + [
                whole_spec((total, LANE)),
                whole_spec((LANE, total)),
                row,
                row,
                row,
                pair,
                pair,
            ]
            + ([] if first else [tall]),
            out_specs=[
                tall if first else pair,
                whole_spec((total // LANE, LANE, LANE)),
            ],
            scratch_shapes=[
                pltpu.VMEM((LANE, TQ), F32),
                pltpu.VMEM((total, LANE), F32),
            ],
        ),
        compiler_params=pltpu.CompilerParams(vmem_limit_bytes=60 << 20),
        cost_estimate=pl.CostEstimate(
            flops=30 * 10**9, bytes_accessed=10 * 10**6, transcendentals=4 * 10**6
        ),
    )(
        tab,
        query[0],
        query[1],
        query[0],
        query[1],
        kv,
        kvt,
        low,
        high,
        lse,
        out,
        grad,
        *(() if first else (part,)),
    )


def cols_kernel(parts, tab, *refs):
    halves, (grad, cols, acc) = refs[:8], refs[8:]
    step = pl.program_id(0)
    rows = jnp.concatenate([half[...] for half in halves], axis=0)
    wide = jnp.concatenate([grad[i] for i in range(4)], axis=1)
    term = product(wide, rows)

    @pl.when(step == 0)
    def _():
        acc[...] = term

    @pl.when(step > 0)
    def _():
        acc[...] += term

    @pl.when(step == pl.num_programs(0) - 1)
    def _():
        for p in range(parts):
            block = acc[p * HD : (p + 1) * HD, :].T
            if len(cols.shape) == 2:
                cols[:, p * HD : (p + 1) * HD] = block.astype(BF)
            else:
                halves = block.reshape(cols.shape[0], 2, 16, HD)
                cols[:, p * 16 : (p + 1) * 16, :] = jnp.concatenate(
                    [halves[:, 0], halves[:, 1]], axis=-1
                ).astype(BF)


def head_columns(tab, stream, grad, shape):
    blocks, deep, _ = grad.shape
    width = stream[0].shape[-1]

    def half(at):
        return pl.BlockSpec(
            (None, LANE // 2, width), lambda t, tab: (tab[at + 4 * t], 0, 0)
        )

    return pl.pallas_call(
        functools.partial(cols_kernel, deep // HD),
        out_shape=jax.ShapeDtypeStruct(shape, BF),
        grid_spec=pltpu.PrefetchScalarGridSpec(
            num_scalar_prefetch=1,
            grid=(blocks // 4,),
            in_specs=[half(i + blocks * j) for i in range(4) for j in range(2)]
            + [pl.BlockSpec((4, deep, LANE), lambda t, tab: (t, 0, 0))],
            out_specs=whole_spec(shape),
            scratch_shapes=[pltpu.VMEM((deep, width), F32)],
        ),
        compiler_params=pltpu.CompilerParams(vmem_limit_bytes=24 << 20),
        cost_estimate=pl.CostEstimate(
            flops=4 * 10**9, bytes_accessed=2 * stream[0].size * 2, transcendentals=0
        ),
    )(tab, *(stream * 4), grad)


def owner_kernel(got, mats, vec):
    rows = got.shape[1]
    low = lax.broadcasted_iota(jnp.int32, (16, LANE), 1) < HD
    total = jnp.zeros(vec.shape, F32)
    for n in range(got.shape[0]):
        total = total + got[n, 48:rows, :].astype(F32)
    vec[...] = total
    for p in range(3):
        for pair in range(H // 2):
            even, odd = jnp.zeros((16, LANE), F32), jnp.zeros((16, LANE), F32)
            for base in range(0, got.shape[0], H):
                even = even + got[base + 2 * pair, p * 16 : (p + 1) * 16, :].astype(F32)
                odd = odd + got[base + 2 * pair + 1, p * 16 : (p + 1) * 16, :].astype(F32)
            at = slice(pair * LANE, (pair + 1) * LANE)
            mats[p, :16, at] = jnp.where(low, even, pltpu.roll(odd, HD, 1))
            mats[p, 16:, at] = jnp.where(low, pltpu.roll(even, HD, 1), odd)


def owner_sums(got, width):
    return pl.pallas_call(
        owner_kernel,
        out_shape=(
            jax.ShapeDtypeStruct((3, 32, width), F32),
            jax.ShapeDtypeStruct((got.shape[1] - 48, LANE), F32),
        ),
        compiler_params=pltpu.CompilerParams(vmem_limit_bytes=16 << 20),
        cost_estimate=pl.CostEstimate(
            flops=got.size, bytes_accessed=got.size * 2 + width * 400, transcendentals=0
        ),
    )(got)


def as_rows(vectors):
    return jnp.stack(
        [jnp.pad(v, ((0, 0), (0, LANE - v.shape[1]))) for v in vectors], axis=1
    )


def make_body(head_bits, blk_bits):
    n_head, n_blk = 1 << len(head_bits), 1 << len(blk_bits)
    n_all = n_head * n_blk
    every = head_bits + blk_bits
    z_bits, x_bit, c_bit = blk_bits[:-2], blk_bits[-2], blk_bits[-1]
    outer = head_bits + z_bits
    repl = n_blk // H
    part = HD // repl
    n_out, n_head_z = 1 << len(outer), len(outer)

    def body(
        tokens,
        segments,
        cotangent,
        w_query,
        w_key,
        w_value,
        b_query,
        b_value,
        w_output,
        b_output,
        gain_attn,
        shift_attn,
        w_inner,
        b_inner,
        w_outer,
        b_outer,
        gain_ffn,
        shift_ffn,
    ):
        rows, width = tokens.shape
        rw = w_query.shape[0]
        ffl = w_outer.shape[0]
        my = {bit: lax.axis_index(bit) for bit in every}
        hi, bi = lax.axis_index(head_bits), lax.axis_index(blk_bits)
        head = bi if repl == 1 else lax.div(bi, repl)
        sub = bi - head * repl

        def both(value, bit, axis, then=None):
            other = swap(value, bit)
            if then is not None:
                other = after(other, then)
            return placed_at(value, other, my[bit], axis)

        def summed(value, bit, axis, then=None):
            other = swap(pick(value, 1 - my[bit], axis).astype(BF), bit)
            if then is not None:
                other = after(other, then)
            return pick(value, my[bit], axis).astype(F32) + other.astype(F32)

        def traded(value, bits, thens=(None, None)):
            for axis, bit in enumerate(bits):
                other = swap(pick(value, 1 - my[bit], axis), bit)
                if thens[axis] is not None:
                    other = after(other, thens[axis])
                kept = pick(value, my[bit], axis)
                value = placed_at(kept, other, my[bit], axis)
            return value

        def over(value, bits, at, thens):
            for i, bit in enumerate(bits):
                value = both(value, bit, at + i, thens[i])
            return value

        def group_gather(part_rows):
            return with_other(with_other(part_rows, x_bit), c_bit)

        def group_scatter(partial):
            part_rows = partial.reshape(2, 2, rows, width)
            mine = part_rows[0] + swap(part_rows[1].astype(BF), c_bit).astype(F32)
            return mine[0] + swap(mine[1].astype(BF), x_bit).astype(F32)

        ways = (z_bits + (x_bit,), (x_bit,) + z_bits)
        flows = [tokens[: rows // 2], tokens[rows // 2 :]]
        hops = [[flow] for flow in flows]
        for i in range(len(ways[0])):
            for flow, way in zip(hops, ways, strict=True):
                flow.append(with_other(flow[-1], way[i]))

        small = as_rows(
            [
                v[None]
                for v in (
                    b_query,
                    b_value,
                    b_output,
                    gain_attn,
                    shift_attn,
                    b_outer,
                    gain_ffn,
                    shift_ffn,
                    b_inner,
                )
            ]
        )
        scale = HD**-0.5
        cut_q, cut_k, cut_v = (
            w.reshape(rw, H, HD) for w in (w_query * BF(scale), w_key, w_value)
        )
        cols = jnp.concatenate(
            [
                jnp.concatenate([cut_k, cut_v], axis=2),
                jnp.concatenate([cut_q, jnp.zeros_like(cut_q)], axis=2),
            ]
        )
        cols = jnp.transpose(cols, (1, 0, 2))[:, None]
        cols = jnp.broadcast_to(cols, (H, repl, 2 * rw, LANE))
        smalls = jnp.broadcast_to(small, (n_blk,) + small.shape[1:])
        cols_all = jnp.concatenate([cols.reshape(n_blk, 2 * rw, LANE), smalls], axis=1)
        got = lax.all_to_all(after(cols_all, hops[1][1]), blk_bits, 0, 0, tiled=True)
        for i, bit in enumerate(head_bits):
            got = both(got, bit, i, hops[1][-1])
        got = got.reshape((n_all,) + got.shape[len(head_bits) + 1 :])

        stream = [with_other(flow[-1], c_bit, got) for flow in hops]
        w_kv = got[:, :rw].reshape(width, LANE)
        w_q = got[:, rw : 2 * rw].reshape(width, LANE)
        vecs = got[:, 2 * rw :].astype(F32)
        named = [vecs[:, i, :rw].reshape(width) for i in range(8)]
        full_bq, full_bv, full_bo, full_g1, full_n1, full_b2, full_g2, full_n2 = named
        full_b1 = vecs[:, 8, :ffl].reshape(n_out, 4, ffl)
        b1_mine = pick(full_b1, my[x_bit] * 2 + my[c_bit], 1).reshape(n_out * ffl)

        n_z = len(z_bits)
        wo_row = over(w_output, z_bits, 0, hops[0][1 : 1 + n_z])
        wo_row = over(wo_row, head_bits, 0, [None] * (len(head_bits) - 1) + [hops[0][-1]])
        w1_cut = jnp.transpose(w_inner.reshape(rw, n_out, 2, 2, ffl), (2, 3, 0, 1, 4))
        w1_cut = traded(
            w1_cut.reshape(2, 2, rw, n_out * ffl), (x_bit, c_bit), hops[0][1:3]
        ).reshape(4 * rw, n_out * ffl)
        w_pair = after(jnp.concatenate([w1_cut, w_outer]), hops[1][2])
        w_pair = lax.all_gather(w_pair, outer)
        w1_mine = w_pair[:, : 4 * rw].reshape(width, n_out * ffl)
        w2_mine = w_pair[:, 4 * rw :].reshape(n_out * ffl, width)

        spot = jnp.arange(n_blk)

        def slots(way):
            apart = spot ^ bi
            total = 0
            for i, bit in enumerate(way + (c_bit,)):
                total = total + (((apart >> (len(blk_bits) - 1 - blk_bits.index(bit))) & 1) << i)
            return total

        slot = [slots(way) for way in ways]
        ids = jnp.arange(DOCS)[:, None]
        below = jnp.sum((segments[None] < ids).astype(jnp.int32), axis=1)
        upto = jnp.sum((segments[None] <= ids).astype(jnp.int32), axis=1)
        own_segs = pick(segments.reshape(n_blk, n_head, LANE), hi, 1).reshape(
            n_blk // 2, 1, TQ
        )
        member = own_segs[None] == ids[:, :, None, None]
        low = jnp.sum(jnp.where(member, below[:, None, None, None], 0), axis=0)
        high = jnp.sum(jnp.where(member, upto[:, None, None, None], 0), axis=0)
        far = KB_LOG + len(head_bits)
        start = low[:, 0, 0] >> far
        stop = (high[:, 0, -1] + ((1 << far) - 1)) >> far
        inner = (jnp.max(low, axis=(1, 2)) + ((1 << far) - 1)) >> far
        inner = jnp.clip(inner, start, stop)
        outer_end = jnp.clip(jnp.min(high, axis=(1, 2)) >> far, inner, stop)
        tab = jnp.concatenate(slot + [start, stop, inner, outer_end, hi[None]])
        tab = tab.astype(jnp.int32)

        bias = jnp.concatenate(
            [
                pick(full_bq.reshape(H, HD), head, 0) * scale,
                jnp.zeros((HD,), F32),
                jnp.zeros((HD,), F32),
                pick(full_bv.reshape(H, HD), head, 0),
            ]
        )
        kv_rel, query = [], []
        w_all = jnp.concatenate([w_q, w_kv], axis=1)
        for flow in stream:
            both_own = (product(flow, w_all) + bias).astype(BF)
            kv_rel.append(both_own[:, LANE:].reshape(n_blk, rows // 2, LANE))
            query.append(both_own[:, :LANE].reshape(n_blk, rows // 2, LANE))
        kv_pair = kv_near = jnp.concatenate(kv_rel, axis=1)
        wo_row = both(wo_row, x_bit, n_head_z, kv_near)
        w_line = jnp.concatenate([w_q[:, :HD] * BF(1.0 / scale), w_kv], axis=1).T
        if repl > 1:
            w_line = lax.dynamic_slice_in_dim(
                w_line.reshape(3, HD, width), sub * part, part, axis=1
            ).reshape(3 * part, width)
        group_other = swap(after(w_line, kv_near), x_bit)
        for bit in head_bits[::-1]:
            kv_pair = with_other(kv_pair, bit) if n_head > 2 else swap(kv_pair, bit)
        kv_far = kv_pair[n_blk:] if n_head > 2 else kv_pair
        kv_far = [kv_far[:, : rows // 2], kv_far[:, rows // 2 :]]
        near_turn, far_turns = (0,), tuple(range(1, n_head))
        kv, kvt, *state = attend(
            tab, n_head, near_turn, query, kv_rel, low, high, (), False
        )
        kv_two, kvt_two, ctx, out, lse = attend(
            tab, n_head, far_turns, query, kv_far, low, high, state, True
        )
        ctx = after(ctx, group_other)
        if repl > 1:
            ctx = lax.dynamic_slice_in_dim(ctx, sub * part, part, axis=1)
        ctx_t = lax.all_to_all(ctx, blk_bits, 0, 0, tiled=True).reshape(width, rows)

        full_wo = both(wo_row, c_bit, n_head_z + 1, ctx_t).reshape(width, width)

        w_line = placed_at(w_line, after(group_other, ctx), my[x_bit], 0)
        ctx_t = after(ctx_t, w_line)

        inputs = tokens.astype(F32)
        unit_one, rstd_one = norm_parts(inputs + left_product(ctx_t, full_wo) + full_bo)
        norm_one = unit_one * full_g1 + full_n1
        low_one = norm_one.astype(BF)

        near = with_other(low_one, x_bit)
        near, w1_mine, w2_mine = together(near, w1_mine, w2_mine)
        inner_in = with_other(near, c_bit)
        pre = product(inner_in, w1_mine) + b1_mine
        phi = 0.5 * (1.0 + lax.erf(pre * (0.5**0.5)))
        act = (pre * phi).astype(BF)
        slope = phi + pre * (jnp.exp(-0.5 * pre * pre) * ((2 * jnp.pi) ** -0.5))
        unit_two, rstd_two = norm_parts(
            norm_one + group_scatter(product(act, w2_mine)) + full_b2
        )
        out_rows = (unit_two * full_g2 + full_n2).astype(BF)

        up = cotangent.astype(F32)
        grad_n2 = jnp.sum(up, axis=0)
        grad_g2 = jnp.sum(up * unit_two, axis=0)
        grad_two = norm_back(unit_two, rstd_two, full_g2, up)
        dz = grad_two.astype(BF)
        grad_b2 = jnp.sum(dz.astype(F32), axis=0)
        dz_all = group_gather(dz)
        grad_pre = (slope * right_product(dz_all, w2_mine)).astype(BF)
        grad_b1 = jnp.sum(grad_pre.astype(F32), axis=0).reshape(n_out, 1, ffl)

        grad_w2 = left_product(act, dz_all).astype(BF).reshape(n_out, ffl, width)
        grad_w1 = left_product(inner_in, grad_pre).astype(BF).reshape(n_out, 4 * rw, width)
        grads = jnp.concatenate([grad_w1, grad_w2], axis=1)
        grads = grads.reshape(n_head, n_out // n_head, 4 * rw + ffl, width)
        grads = jnp.swapaxes(grads, 0, 1)
        grad_norm = right_product(grad_pre, w1_mine)
        grad_norm = grad_two + group_scatter(grad_norm)
        grads = lax.psum_scatter(grads, z_bits, scatter_dimension=0)
        grads = grads.reshape((2,) * len(head_bits) + (4 * rw + ffl, width))

        grad_n1 = jnp.sum(grad_norm, axis=0)
        grad_g1 = jnp.sum(grad_norm * unit_one, axis=0)
        grad_one = norm_back(unit_one, rstd_one, full_g1, grad_norm)
        da = grad_one.astype(BF)
        grad_bo = jnp.sum(da.astype(F32), axis=0)
        grad_ctx = right_product(full_wo, da).astype(BF).reshape(H, 1, HD, rows)
        grad_ctx = jnp.broadcast_to(grad_ctx, (H, repl, HD, rows)).reshape(n_blk, HD, rows)
        grad_heads = lax.all_to_all(grad_ctx, blk_bits, 0, 0, tiled=True)

        later = after(da, grad_ctx)

        by_core = ctx_t.reshape(n_all // 2, 2, rw, rows)

        def core_half(core):
            return product(pick(by_core, core, 1).reshape(width // 2, rows), later)

        wo_other = swap(core_half(1 - my[c_bit]).astype(BF), c_bit)
        grad_wo = core_half(my[c_bit]) + after(wo_other, grad_ctx).astype(F32)
        grad_wo = grad_wo.reshape((2,) * (len(every) - 1) + (rw, width))
        w_line = both(w_line, c_bit, 0, grad_ctx)
        grad_heads = after(grad_heads, grad_wo, w_line)
        w_line = w_line.reshape(4 * 3 * part, width)
        wo_at = len(every) - 2
        wo_other = swap(pick(grad_wo, 1 - my[x_bit], wo_at).astype(BF), x_bit)

        part_q, others = attend_back(
            tab,
            n_head,
            far_turns,
            query,
            kv_two,
            kvt_two,
            low,
            high,
            lse,
            out,
            grad_heads,
            None,
        )
        others = others.reshape(n_head - 1, n_blk, LANE, LANE)
        part_q, wo_other = together(part_q, wo_other)
        grad_q, grad_kv = attend_back(
            tab, n_head, near_turn, query, kv, kvt, low, high, lse, out, grad_heads, part_q
        )
        terms = [grad_kv] + [others[k] for k in range(n_head - 1)]
        for i, bit in list(enumerate(head_bits[::-1]))[::-1]:
            terms = [
                terms[k].astype(F32) + swap(terms[k + (1 << i)].astype(BF), bit).astype(F32)
                for k in range(1 << i)
            ]
        grad_kv = terms[0].astype(BF)
        grad_wo = pick(grad_wo, my[x_bit], wo_at) + wo_other.astype(F32)

        def own_part(grad, count):
            grad = grad.reshape(n_blk, count, HD, LANE)
            if repl > 1:
                grad = lax.dynamic_slice_in_dim(grad, sub * part, part, axis=2)
            return grad.reshape(n_blk, count * part, LANE)

        def line_rows(grad, count):
            sent = own_part(grad, count).reshape(n_blk // 4, 2, 2, count * part, rows)
            sent = jnp.transpose(sent, (2, 1, 0, 3, 4)).reshape(
                4, n_blk // 4, count * part, rows
            )
            return lax.all_to_all(sent, (c_bit, x_bit), 0, 0, tiled=True)

        def line_product(weights, came):
            came = jnp.transpose(came, (0, 2, 1, 3)).reshape(12 * part, n_blk // 4 * rows)
            return left_product(came, weights)

        grad_qkv = jnp.concatenate([grad_q, grad_kv], axis=1)
        line_kv = line_rows(grad_qkv, 3)
        for bit in head_bits:
            grad_wo = summed(grad_wo, bit, 0, grad_kv)
        wo_half = grad_wo

        grad_in = line_product(w_line, line_kv)

        packed = rw == 32 and repl == 1
        shape = (n_all, 48, LANE) if packed else (width, 3 * HD)
        halves = tuple(flow.reshape(n_blk, rows // 2, width) for flow in stream)
        cut = head_columns(tab, halves, grad_qkv, shape)
        if not packed:
            cut = cut.reshape(width, 3, HD)
            if repl > 1:
                cut = lax.dynamic_slice_in_dim(cut, sub * part, part, axis=2)
            cut = cut.reshape(n_all, rw * 3 * part // LANE, LANE)
        own = (jnp.arange(H) == head).astype(F32)[:, None]
        if repl > 1:
            own = own * (sub == 0).astype(F32)
        bias_rows = jnp.sum(grad_qkv.astype(F32), axis=(0, 2))
        grad_bq = (own * bias_rows[None, :HD]).reshape(width)
        grad_bv = (own * bias_rows[None, 2 * HD :]).reshape(width)
        mark = (jnp.arange(4) == my[x_bit] * 2 + my[c_bit]).astype(F32)[None, :, None]
        b1_abs = (grad_b1 * mark).reshape(n_all, ffl)
        smalls = jnp.stack(
            [
                grad_bq,
                grad_bv,
                *after((grad_bo, grad_g1, grad_n1, grad_b2, grad_g2, grad_n2), grad_q),
            ]
        ).reshape(8, width // LANE, 1, LANE)
        share = LANE // rw
        smalls = jnp.swapaxes(smalls, 0, 1).reshape(width // LANE, 1, 8, LANE)
        smalls = jnp.broadcast_to(smalls, (width // LANE, share, 8, LANE))
        smalls = jnp.concatenate(
            [smalls.reshape(n_all, 8, LANE), as_rows([b1_abs])], axis=1
        )
        cut = jnp.concatenate([cut, smalls.astype(BF)], axis=1)
        n_cut = cut.shape[1]
        cut = cut.reshape((2,) * len(head_bits) + (n_blk, n_cut, LANE))
        for bit in head_bits:
            cut = summed(cut, bit, 0, grad_in)
        sent = cut.astype(BF)
        got = lax.all_to_all(sent, blk_bits, 0, 0, tiled=True)
        grads = after(grads, line_kv)
        for bit in head_bits[1:]:
            grads = summed(grads, bit, 1)
        other = swap(pick(grads, 1 - my[head_bits[0]], 0).astype(BF), head_bits[0])
        grad_in = grad_in.reshape((2,) * n_z + (rows, width))
        for i in range(1, n_z)[::-1]:
            grad_in = summed(grad_in, z_bits[i], i)
        grad_wo = after(wo_half, line_kv)
        for bit in z_bits[:1]:
            grad_wo = summed(grad_wo, bit, 0, grad_in)
        for bit in z_bits[1:]:
            grad_wo = summed(grad_wo, bit, 0)
        grad_in = summed(grad_in, z_bits[0], 0)
        grads = pick(grads, my[head_bits[0]], 0).astype(F32) + other.astype(F32)
        grad_w2 = grads[4 * rw :]
        first = grads[: 4 * rw].astype(BF).reshape(2, 2, rw, n_out * ffl)
        first_other = swap(pick(first, 1 - my[x_bit], 0), x_bit)
        grad_w1 = placed_at(pick(first, my[x_bit], 0), first_other, my[x_bit], 0)
        grad_w1 = after(grad_w1, grad_in)
        came = swap(pick(grad_w1, 1 - my[c_bit], 1), c_bit)
        grad_w1 = placed_at(pick(grad_w1, my[c_bit], 1), came, my[c_bit], 1)
        grad_tokens = grad_one + grad_in
        grad_w1 = (
            jnp.transpose(grad_w1.reshape(4, rw, n_out, ffl), (1, 2, 0, 3))
            .reshape(rw, n_all * ffl)
            .astype(F32)
        )
        if packed:
            mats, vecs = owner_sums(got, width)
        else:
            got = got.astype(F32)
            mats = got[:, : n_cut - 9].reshape(H, repl, rw, 3, part)
            mats = jnp.transpose(mats, (3, 2, 0, 1, 4)).reshape(3, rw, width)
            vecs = jnp.sum(got[:, n_cut - 9 :], axis=0)
        lane = ((hi * n_blk + bi) & (share - 1)) * rw
        own_vecs = lax.dynamic_slice_in_dim(
            vecs[:8], lane, rw, 1, allow_negative_indices=False
        )
        grad_bq, grad_bv, grad_bo, grad_g1, grad_n1, grad_b2, grad_g2, grad_n2 = (
            own_vecs[i] for i in range(8)
        )
        grad_b1 = vecs[8, :ffl]
        return (
            out_rows,
            grad_tokens,
            mats[0],
            mats[1],
            mats[2],
            grad_bq,
            grad_bv,
            grad_wo,
            grad_bo,
            grad_g1,
            grad_n1,
            grad_w1,
            grad_b1,
            grad_w2,
            grad_b2,
            grad_g2,
            grad_n2,
        )

    return body


def solution(mesh):
    n_head, n_blk = mesh.shape["head"], mesh.shape["blk"]
    head_bits = tuple(f"h{i}" for i in range(n_head.bit_length() - 1))
    blk_bits = tuple(f"b{i}" for i in range(n_blk.bit_length() - 1))
    fine = Mesh(
        mesh.devices.reshape((2,) * len(head_bits + blk_bits)), head_bits + blk_bits
    )
    by_token = P(blk_bits + head_bits, None)
    by_row, by_entry = P(head_bits + blk_bits, None), P(head_bits + blk_bits)
    placed = (
        by_token,
        P(),
        by_token,
        by_row,
        by_row,
        by_row,
        by_entry,
        by_entry,
        by_row,
        by_entry,
        by_entry,
        by_entry,
        by_row,
        by_entry,
        by_row,
        by_entry,
        by_entry,
        by_entry,
    )
    given = (
        by_token,
        by_token,
        by_row,
        by_row,
        by_row,
        by_entry,
        by_entry,
        by_row,
        by_entry,
        by_entry,
        by_entry,
        by_row,
        by_entry,
        by_row,
        by_entry,
        by_entry,
        by_entry,
    )
    return jax.shard_map(
        make_body(head_bits, blk_bits),
        mesh=fine,
        in_specs=placed,
        out_specs=given,
        check_vma=False,
    )
```
